128 devices in a mesh: group: 2 (over core), dom: 64 (over y, z, x).
Axes of the slice: x: 4, y: 4, z: 4, core: 2. Of those that a mesh axis runs over, the one named last changes fastest.
Arguments:
- nodes: bfloat16 [2, 65536, 512], P('group', 'dom'), may hold values from -6 to 6
- edges: bfloat16 [2, 131072, 512], P('group', 'dom'), may hold values from -6 to 6
- node_cotangent: bfloat16 [2, 65536, 512], P('group', 'dom'), may hold values from -6 to 6
- edge_cotangent: bfloat16 [2, 131072, 512], P('group', 'dom'), may hold values from -6 to 6
- senders: int32 [2, 131072], P('group', 'dom'), may hold values from 0 to 1535, as said below
- receivers: int32 [2, 131072], P('group', 'dom'), may hold values from 0 to 1023
- send_rows: int32 [2, 4096, 8], P('group', 'dom'), may hold values from 0 to 1023
- edge_in: bfloat16 [1536, 512], replicated, may hold values from -0.15625 to 0.15625
- edge_out: bfloat16 [512, 512], replicated, may hold values from -0.25 to 0.25
- edge_gain: float32 [512], replicated, may hold values from 0.1 to 1.9
- node_in: bfloat16 [1024, 512], replicated, may hold values from -0.1875 to 0.1875
- node_out: bfloat16 [512, 512], replicated, may hold values from -0.25 to 0.25
- node_gain: float32 [512], replicated, may hold values from 0.1 to 1.9
Outputs:
- grad_edges: bfloat16 [2, 131072, 512], P('group', 'dom')
- grad_nodes: bfloat16 [2, 65536, 512], P('group', 'dom')
- grad_edge_in: float32 [1536, 512], P('dom')
- grad_edge_out: float32 [512, 512], P('dom')
- grad_node_in: float32 [1024, 512], P('dom')
- grad_node_out: float32 [512, 512], P('dom')
- grad_edge_gain: float32 [512], P('dom')
- grad_node_gain: float32 [512], P('dom')
The draws below stay inside these ranges and needn't reach their ends.
Inputs may be any that keep to these rules, and one draw needn't show every extreme that they name: `senders`: an id below 1024 is a row of the edge's own partition; an id 1024 + p * 8 + s is slot s of the list partition p of the same graph sends to the edge's partition. The slots read from one peer lie below a count of that edge's partition and peer, and on every partition some peer's slot 7 is read.
All inputs are finite; a program needn't handle non-finite values.
Results may differ from the reference program's by a relative error of at most 0.019.
Values may be sent and summed in bfloat16 or wider, within the bound.
No kernel may reach another device: no remote copies, remote signals or barrier semaphores. Data moves between devices by JAX's collectives and lax.ppermute only.
A program may use at most 128 MiB of HBM per device.

```python
import jax
import jax.numpy as jnp
from jax import lax

W = 512
NODE_DEV = 1024
EDGE_DEV = 2048
CAP = 8
DOMAINS = 64
GRAPHS = 2
NODES = 65536
EDGES = 131072


def draw_senders(key, part):
    keys = jax.random.split(jax.random.fold_in(key, 7), 6)
    used = jax.random.randint(keys[0], (GRAPHS, DOMAINS, DOMAINS), 1, CAP + 1)
    full_peer = jax.random.randint(keys[1], (GRAPHS, DOMAINS), 0, DOMAINS)
    peer_iota = jnp.arange(DOMAINS, dtype=jnp.int32)[None, None, :]
    used = jnp.where(peer_iota == full_peer[:, :, None], CAP, used)
    peer = jax.random.randint(keys[2], (GRAPHS, DOMAINS, EDGE_DEV), 0, DOMAINS)
    noise = jax.random.randint(keys[3], (GRAPHS, DOMAINS, EDGE_DEV), 0, 1 << 20)
    limit = jnp.take_along_axis(used, peer, axis=2)
    slot = noise % limit
    halo_ids = NODE_DEV + peer * CAP + slot
    local_ids = jax.random.randint(keys[4], (GRAPHS, DOMAINS, EDGE_DEV), 0, NODE_DEV)
    picker = jax.random.randint(keys[5], (GRAPHS, DOMAINS, EDGE_DEV), 0, 2)
    result = jnp.where(picker == 0, local_ids, halo_ids)
    result = result.at[:, :, 0].set(NODE_DEV + full_peer * CAP + CAP - 1)
    return result.reshape(GRAPHS, DOMAINS * EDGE_DEV).astype(jnp.int32)


def place_ends(values, rng, smallest, largest):
    index_at = [jax.random.randint(jax.random.fold_in(rng, axis), (), 0, length) for axis, length in enumerate(values.shape)]
    main_axis = values.shape.index(max(values.shape))
    neighbour = index_at[:main_axis] + [(index_at[main_axis] + 1) % values.shape[main_axis]] + index_at[main_axis + 1:]
    return values.at[tuple(index_at)].set(smallest).at[tuple(neighbour)].set(largest)


def shard_levels(key, shape, pieces, low, high):
    def one(position, blocks):
        steps = jax.random.uniform(jax.random.fold_in(jax.random.fold_in(key, 6), position), (blocks,), jnp.float32, low / len(pieces), high / len(pieces))
        return jnp.repeat(jnp.exp(steps), shape[position] // blocks).reshape((-1,) + (1,) * (len(shape) - position - 1))

    level = one(*pieces[0])
    for cut in pieces[1:]:
        level = level * one(*cut)
    return level


def gaussian(stream_key, extent, spread, reach, cuts=(), kind=jnp.bfloat16):
    array = jax.random.normal(stream_key, extent, jnp.float32) * spread
    if len(cuts) > 0:
        array = shard_levels(stream_key, extent, cuts, -0.22, 0.18) * array
    return jnp.clip(array, min=-reach, max=reach).astype(kind)


def setup_inputs(seed: int = 0) -> dict:
    streams_of = jax.random.split(jax.random.key(seed), 14)
    return {
        "nodes": gaussian(streams_of[0], (GRAPHS, NODES, W), 1.0, 6.0, ((0, 2), (1, 64))),
        "edges": gaussian(streams_of[1], (GRAPHS, EDGES, W), 1.0, 6.0, ((0, 2), (1, 64))),
        "node_cotangent": gaussian(streams_of[2], (GRAPHS, NODES, W), 1.0, 6.0, ((0, 2), (1, 64))),
        "edge_cotangent": gaussian(streams_of[3], (GRAPHS, EDGES, W), 1.0, 6.0, ((0, 2), (1, 64))),
        "senders": draw_senders(jax.random.fold_in(streams_of[13], 71), 0),
        "receivers": place_ends(jax.random.randint(streams_of[5], (GRAPHS, EDGES), 0, NODE_DEV), jax.random.fold_in(streams_of[5], 1), 0, NODE_DEV - 1).astype(jnp.int32),
        "send_rows": place_ends(jax.random.randint(streams_of[6], (GRAPHS, DOMAINS * DOMAINS, CAP), 0, NODE_DEV), jax.random.fold_in(streams_of[6], 1), 0, NODE_DEV - 1).astype(jnp.int32),
        "edge_in": gaussian(streams_of[7], (3 * W, W), (3 * W) ** -0.5, 0.15625),
        "edge_out": gaussian(streams_of[8], (W, W), W ** -0.5, 0.25),
        "edge_gain": jnp.clip(1.0 + 0.18 * jax.random.normal(streams_of[9], (W,), jnp.float32), 0.1, 1.9),
        "node_in": gaussian(streams_of[10], (2 * W, W), (2 * W) ** -0.5, 0.1875),
        "node_out": gaussian(streams_of[11], (W, W), W ** -0.5, 0.25),
        "node_gain": jnp.clip(1.0 + 0.18 * jax.random.normal(streams_of[12], (W,), jnp.float32), 0.1, 1.9),
    }


def swish(value):
    return value * jax.nn.sigmoid(value)

def swish_slope(value):
    logistic = jax.nn.sigmoid(value)
    return logistic * (1.0 + value * (1.0 - logistic))

def normalize(hidden):
    centre = hidden - lax.optimization_barrier(jnp.mean(hidden, axis=-1, keepdims=True))
    inverse = lax.rsqrt(lax.optimization_barrier(jnp.mean(centre * centre, axis=-1, keepdims=True)) + 1e-05)
    return (centre * inverse, inverse)

def norm_back(upstream, gain, normed, inverse):
    scaled = upstream * gain
    return inverse * (scaled - lax.optimization_barrier(jnp.mean(scaled, axis=-1, keepdims=True)) - normed * lax.optimization_barrier(jnp.mean(scaled * normed, axis=-1, keepdims=True)))

def one_graph(node_rows, edge_rows, node_cot, edge_cot, send_ids, recv_ids, lists, edge_in, edge_out, edge_gain, node_in, node_out, node_gain):
    edge_index = jnp.arange(EDGES, dtype=jnp.int32)
    owner = edge_index // EDGE_DEV
    recv_node = owner * NODE_DEV + recv_ids
    lists = lists.reshape(DOMAINS, DOMAINS, CAP)
    halo_pos = jnp.maximum(send_ids - NODE_DEV, 0)
    peer = halo_pos // CAP
    slot = halo_pos % CAP
    remote_row = lists[peer, owner, slot]
    send_node = jnp.where(send_ids < NODE_DEV, owner * NODE_DEV + send_ids, peer * NODE_DEV + remote_row)
    edge_input = jnp.concatenate([edge_rows, node_rows[send_node], node_rows[recv_node]], axis=1)
    edge_pre = jnp.dot(edge_input, edge_in, preferred_element_type=jnp.float32)
    edge_act = swish(edge_pre).astype(jnp.bfloat16)
    edge_post = jnp.dot(edge_act, edge_out, preferred_element_type=jnp.float32)
    edge_hat, edge_inv = normalize(edge_post)
    update = (edge_hat * edge_gain).astype(jnp.bfloat16)
    gathered = jax.ops.segment_sum(update.astype(jnp.float32), recv_node, NODES).astype(jnp.bfloat16)
    node_input = jnp.concatenate([node_rows, gathered], axis=1)
    node_pre = jnp.dot(node_input, node_in, preferred_element_type=jnp.float32)
    node_act = swish(node_pre).astype(jnp.bfloat16)
    node_post = jnp.dot(node_act, node_out, preferred_element_type=jnp.float32)
    node_hat, node_inv = normalize(node_post)
    node_upstream = node_cot.astype(jnp.float32)
    node_gain_grad = lax.optimization_barrier(jnp.sum(node_upstream * node_hat, axis=0))
    node_post_grad = norm_back(node_upstream, node_gain, node_hat, node_inv).astype(jnp.bfloat16)
    node_out_grad = jnp.dot(node_act.T, node_post_grad, preferred_element_type=jnp.float32)
    node_act_grad = jnp.dot(node_post_grad, node_out.T, preferred_element_type=jnp.float32)
    node_pre_grad = (node_act_grad * swish_slope(node_pre)).astype(jnp.bfloat16)
    node_in_grad = jnp.dot(node_input.T, node_pre_grad, preferred_element_type=jnp.float32)
    node_input_grad = jnp.dot(node_pre_grad, node_in.T, preferred_element_type=jnp.float32)
    gathered_grad = node_input_grad[:, W:].astype(jnp.bfloat16)
    update_grad = edge_cot.astype(jnp.float32) + gathered_grad[recv_node].astype(jnp.float32)
    edge_gain_grad = lax.optimization_barrier(jnp.sum(update_grad * edge_hat, axis=0))
    edge_post_grad = norm_back(update_grad, edge_gain, edge_hat, edge_inv).astype(jnp.bfloat16)
    edge_out_grad = jnp.dot(edge_act.T, edge_post_grad, preferred_element_type=jnp.float32)
    edge_act_grad = jnp.dot(edge_post_grad, edge_out.T, preferred_element_type=jnp.float32)
    edge_pre_grad = (edge_act_grad * swish_slope(edge_pre)).astype(jnp.bfloat16)
    edge_in_grad = jnp.dot(edge_input.T, edge_pre_grad, preferred_element_type=jnp.float32)
    edge_input_grad = jnp.dot(edge_pre_grad, edge_in.T, preferred_element_type=jnp.float32)
    grad_edges = (edge_cot.astype(jnp.float32) + edge_input_grad[:, :W]).astype(jnp.bfloat16)
    node_total = node_upstream + node_input_grad[:, :W]
    node_total = node_total + jax.ops.segment_sum(edge_input_grad[:, W:2 * W], send_node, NODES)
    node_total = node_total + jax.ops.segment_sum(edge_input_grad[:, 2 * W:], recv_node, NODES)
    grad_nodes = node_total.astype(jnp.bfloat16)
    return (grad_edges, grad_nodes, (edge_in_grad, edge_out_grad, node_in_grad, node_out_grad, edge_gain_grad, node_gain_grad))

def reference(nodes, edges, node_cotangent, edge_cotangent, senders, receivers, send_rows, edge_in, edge_out, edge_gain, node_in, node_out, node_gain):
    edge_list = []
    node_list = []
    totals = None
    for graph in range(GRAPHS):
        grad_e, grad_n, parts = one_graph(nodes[graph], edges[graph], node_cotangent[graph], edge_cotangent[graph], senders[graph], receivers[graph], send_rows[graph], edge_in, edge_out, edge_gain, node_in, node_out, node_gain)
        edge_list.append(grad_e)
        node_list.append(grad_n)
        if totals is None:
            totals = parts
        else:
            totals = tuple((first + second for first, second in zip(totals, parts)))
    return (jnp.stack(edge_list), jnp.stack(node_list), totals[0], totals[1], totals[2], totals[3], totals[4], totals[5])
```

```python
import functools

import jax
import jax.numpy as jnp
from jax import lax
from jax.experimental import pallas as pl
from jax.experimental.pallas import tpu as pltpu
from jax.sharding import PartitionSpec as P

BF = jnp.bfloat16
F32 = jnp.float32
LANES = 128
VMEM_LIMIT = 58 * 1024 * 1024


def dot(a, b):
    return jnp.dot(a, b, preferred_element_type=F32)


def dot_nt(a, b):
    return lax.dot_general(a, b, (((1,), (1,)), ((), ())), preferred_element_type=F32)


def dot_tn(a, b):
    return lax.dot_general(a, b, (((0,), (0,)), ((), ())), preferred_element_type=F32)


def spread(ids):
    return jnp.broadcast_to(ids, (LANES, ids.shape[1])).T


def pick(spread_ids, count):
    lane = lax.broadcasted_iota(jnp.int32, spread_ids.shape, 1)
    tiles = [
        jnp.where(spread_ids == lane + LANES * k, 1.0, 0.0).astype(BF)
        for k in range(count // LANES)
    ]
    return jnp.concatenate(tiles, axis=1)


def pick_t(ids, first, count):
    row = lax.broadcasted_iota(jnp.int32, (count, ids.shape[1]), 0) + first
    return jnp.where(row == ids, 1.0, 0.0).astype(BF)


def swish_both(pre):
    gate = jax.nn.sigmoid(pre)
    return pre * gate, gate * (1.0 + pre * (1.0 - gate))


def normalize(hidden):
    centre = hidden - jnp.mean(hidden, axis=-1, keepdims=True)
    inverse = lax.rsqrt(jnp.mean(centre * centre, axis=-1, keepdims=True) + 1e-05)
    return centre * inverse, inverse


def norm_back(upstream, gain, normed, inverse):
    scaled = upstream * gain
    return inverse * (
        scaled
        - jnp.mean(scaled, axis=-1, keepdims=True)
        - normed * jnp.mean(scaled * normed, axis=-1, keepdims=True)
    )


def fold(value):
    return jnp.sum(value.reshape(value.shape[0] // 8, 8, value.shape[1]), axis=0)


def outgoing_kernel(list_ref, nodes_ref, out_ref):
    sel = pick(spread(list_ref[...]), nodes_ref.shape[0])
    out_ref[...] = dot(sel, nodes_ref[...]).astype(BF)


def gain_rows(edge_gain, node_gain, domains, width):
    per = edge_gain.shape[1] // domains
    shape = (domains, edge_gain.shape[1])
    own = lax.broadcasted_iota(jnp.int32, shape, 1) // per == lax.broadcasted_iota(
        jnp.int32, shape, 0
    )
    col = lax.broadcasted_iota(jnp.int32, (edge_gain.shape[1], width), 0) % per
    lane = lax.broadcasted_iota(jnp.int32, (edge_gain.shape[1], width), 1)
    total = 0.0
    for k, gain in enumerate((edge_gain, node_gain)):
        mine = jnp.where(own, jnp.broadcast_to(gain, shape), 0.0).astype(BF)
        place = jnp.where(lane == col + per * k, 1.0, 0.0).astype(BF)
        total = total + dot(mine, place)
    return total


def main_kernel(
    g_ref,
    send_ref,
    recv_ref,
    nodes_ref,
    edges_ref,
    arrived_ref,
    ncot_ref,
    ecot_ref,
    ein_ref,
    eout_ref,
    egain_ref,
    nin_ref,
    nout_ref,
    ngain_ref,
    ret_ref,
    keep_ref,
    give_ref,
    act_ref,
    epostg_ref,
    epg_ref,
    sums_ref,
    ntotal_ref,
    cs,
    cr,
    sel_r,
    sel_rt,
    table,
    slope,
    hat,
    inv,
    gath,
    nact,
    npostg,
    nprg,
    gg,
    eacc,
    nacc,
    share,
):
    w = nodes_ref.shape[1]
    n = nodes_ref.shape[0]
    e = edges_ref.shape[0]
    h = arrived_ref.shape[0]
    half = w // 2
    domains = share.shape[0]
    eb = 512
    nb = 512
    cs[...] = spread(send_ref[...])
    cr[...] = spread(recv_ref[...])
    table[0:w, :] = ein_ref[0:w, :]
    for k in range(n // nb):
        rows = slice(k * nb, (k + 1) * nb)
        x = nodes_ref[rows, :]
        table[w + k * nb : w + (k + 1) * nb, :] = dot(x, ein_ref[w : 2 * w, :]).astype(BF)
        table[w + n + h + k * nb : w + n + h + (k + 1) * nb, :] = dot(
            x, ein_ref[2 * w : 3 * w, :]
        ).astype(BF)
    table[w + n : w + n + h, :] = dot(arrived_ref[...], ein_ref[w : 2 * w, :]).astype(BF)
    egain = egain_ref[...]
    ngain = ngain_ref[...]

    def edge_forward(b, carry):
        rows = pl.ds(pl.multiple_of(b * eb, eb), eb)
        r = pick(cr[rows, :], n)
        sel_r[rows, :] = r
        s = pick(cs[rows, :], n + h)
        left = jnp.concatenate([edges_ref[rows, :], s, r], axis=1)
        pre = dot(left, table[...])
        act, slp = swish_both(pre)
        act = act.astype(BF)
        act_ref[rows, :] = act
        slope[rows, :] = slp
        normed, inverse = normalize(dot(act, eout_ref[...]))
        hat[rows, :] = normed
        inv[rows, :] = jnp.broadcast_to(inverse, (eb, LANES))
        epostg_ref[rows, :] = (normed * egain).astype(BF)
        return carry

    lax.fori_loop(0, e // eb, edge_forward, 0)
    nacc[...] = jnp.zeros_like(nacc)
    eacc[...] = jnp.zeros_like(eacc)

    def node_block(b, carry):
        first = pl.multiple_of(b * nb, nb)
        rows = pl.ds(first, nb)
        rt = pick_t(recv_ref[...], first, nb)
        sel_rt[rows, :] = rt
        gathered = dot(rt, epostg_ref[...]).astype(BF)
        gath[rows, :] = gathered
        pre = dot(jnp.concatenate([nodes_ref[rows, :], gathered], axis=1), nin_ref[...])
        act, slp = swish_both(pre)
        act = act.astype(BF)
        nact[rows, :] = act
        normed, inverse = normalize(dot(act, nout_ref[...]))
        upstream = ncot_ref[rows, :].astype(F32)
        nacc[...] += fold(upstream * normed)
        postg = norm_back(upstream, ngain, normed, inverse).astype(BF)
        npostg[rows, :] = postg
        preg = (dot_nt(postg, nout_ref[...]) * slp).astype(BF)
        nprg[rows, :] = preg
        back = dot_nt(preg, nin_ref[...])
        ntotal_ref[rows, :] = upstream + back[:, :w]
        gg[rows, :] = back[:, w:].astype(BF)
        return carry

    lax.fori_loop(0, n // nb, node_block, 0)

    def edge_backward(b, carry):
        rows = pl.ds(pl.multiple_of(b * eb, eb), eb)
        upstream = ecot_ref[rows, :].astype(F32) + dot(sel_r[rows, :], gg[...])
        normed = hat[rows, :]
        eacc[...] += fold(upstream * normed)
        postg = norm_back(upstream, egain, normed, inv[rows, 0:1]).astype(BF)
        epostg_ref[rows, :] = postg
        epg_ref[rows, :] = (dot_nt(postg, eout_ref[...]) * slope[rows, :]).astype(BF)
        return carry

    lax.fori_loop(0, e // eb, edge_backward, 0)

    def node_sums(b, carry):
        first = pl.multiple_of(b * nb, nb)
        rows = pl.ds(first, nb)
        st = pick_t(send_ref[...], first, nb)
        sums_ref[rows, :] = dot(st, epg_ref[...]).astype(BF)
        sums_ref[pl.ds(pl.multiple_of(n + h + b * nb, nb), nb), :] = dot(
            sel_rt[rows, :], epg_ref[...]
        ).astype(BF)
        return carry

    lax.fori_loop(0, n // nb, node_sums, 0)
    halo = dot(pick_t(send_ref[...], n, h), epg_ref[...]).astype(BF)
    sums_ref[n : n + h, :] = halo
    ret = dot_nt(halo, ein_ref[w : 2 * w, :])
    per = h // domains
    ret_ref[:, 0:per, :] = ret[:, :half].reshape(domains, per, half).astype(BF)
    ret_ref[:, per : 2 * per, :] = ret[:, half:].reshape(domains, per, half).astype(BF)

    mine = g_ref[0]
    for out_ref, which in ((keep_ref, mine), (give_ref, 1 - mine)):
        cols = pl.ds(pl.multiple_of(which * half, half), half)
        pg = nprg[:, cols]
        for k, source in enumerate((nodes_ref, gath)):
            grad = dot_tn(source[...], pg)
            share[k * (domains // 2) : (k + 1) * (domains // 2), 0:16, :] = grad.reshape(
                domains // 2, 16, half
            )
        share[:, 16:24, :] = dot_tn(nact[...], npostg[:, cols]).reshape(domains, 8, half)
        gains = gain_rows(
            jnp.sum(eacc[...], axis=0, keepdims=True),
            jnp.sum(nacc[...], axis=0, keepdims=True),
            domains,
            half,
        )
        share[:, 24:32, :] = jnp.broadcast_to(gains[:, None, :], (domains, 8, half))
        out_ref[...] = share[...].astype(BF)


def grad_edges_kernel(epg_ref, ecot_ref, ein_ref, out_ref):
    eb = 512
    w = ecot_ref.shape[1]

    def block(b, carry):
        rows = pl.ds(pl.multiple_of(b * eb, eb), eb)
        out_ref[rows, :] = (
            ecot_ref[rows, :].astype(F32) + dot_nt(epg_ref[rows, :], ein_ref[0:w, :])
        ).astype(BF)
        return carry

    lax.fori_loop(0, ecot_ref.shape[0] // eb, block, 0)


def edge_weights_kernel(
    g_ref, edges_ref, nodes_ref, arrived_ref, act_ref, epostg_ref, epg_ref, sums_ref,
    keep_ref, give_ref, share,
):
    w = nodes_ref.shape[1]
    n = nodes_ref.shape[0]
    h = arrived_ref.shape[0]
    half = w // 2
    domains = share.shape[0]
    mine = g_ref[0]
    per = 3 * w // domains // 8
    for out_ref, which in ((keep_ref, mine), (give_ref, 1 - mine)):
        cols = pl.ds(pl.multiple_of(which * half, half), half)
        both = dot_tn(
            nodes_ref[...],
            jnp.concatenate([sums_ref[0:n, cols], sums_ref[n + h :, cols]], axis=1),
        )
        parts = (
            dot_tn(edges_ref[...], epg_ref[:, cols]),
            both[:, :half] + dot_tn(arrived_ref[...], sums_ref[n : n + h, cols]),
            both[:, half:],
        )
        for k, part in enumerate(parts):
            for j in range(w // 8):
                t = k * (w // 8) + j
                share[t // per, (t % per) * 8 : (t % per) * 8 + 8, :] = part[j * 8 : j * 8 + 8, :]
        share[:, 24:32, :] = dot_tn(act_ref[...], epostg_ref[:, cols]).reshape(domains, 8, half)
        out_ref[...] = share[...].astype(BF)


def local_sums_kernel(sums_ref, ntotal_ref, ein_ref, out_ref):
    w = ein_ref.shape[1]
    n = ntotal_ref.shape[0]
    h = sums_ref.shape[0] - 2 * n
    nb = 512

    def block(b, carry):
        first = pl.multiple_of(b * nb, nb)
        rows = pl.ds(first, nb)
        out_ref[rows, :] = (
            ntotal_ref[rows, :]
            + dot_nt(sums_ref[rows, :], ein_ref[w : 2 * w, :])
            + dot_nt(
                sums_ref[pl.ds(pl.multiple_of(n + h + b * nb, nb), nb), :],
                ein_ref[2 * w : 3 * w, :],
            )
        )
        return carry

    lax.fori_loop(0, n // nb, block, 0)


def grad_nodes_kernel(list_ref, first_ref, total_ref, out_ref, node_ref):
    n, w = total_ref.shape
    domains = first_ref.shape[0]
    half = first_ref.shape[2]
    left = first_ref[:, 0:8, :].astype(F32).reshape(domains * 8, half)
    right = first_ref[:, 8:16, :].astype(F32).reshape(domains * 8, half)
    back = jnp.concatenate([left, right], axis=1).astype(BF)
    out_ref[...] = (total_ref[...] + dot(pick_t(list_ref[...], 0, n), back)).astype(BF)
    node_ref[...] = jnp.sum(first_ref[:, 16:48, :].astype(F32), axis=0)


def sum_kernel(second_ref, node_ref, out_ref):
    out_ref[0:32, :] = jnp.sum(second_ref[...].astype(F32), axis=0).astype(BF)
    out_ref[32:64, :] = node_ref[...].astype(BF)


def outputs_kernel(both_ref, ein_ref, eout_ref, nin_ref, nout_ref, gains_ref):
    half = both_ref.shape[2]
    for k in range(2):
        cols = slice(k * half, (k + 1) * half)
        ein_ref[:, cols] = both_ref[k, 0:24, :].astype(F32)
        eout_ref[:, cols] = both_ref[k, 24:32, :].astype(F32)
        nin_ref[:, cols] = both_ref[k, 32:48, :].astype(F32)
        nout_ref[:, cols] = both_ref[k, 48:56, :].astype(F32)
    gains_ref[...] = both_ref[0, 56:64, 0:LANES].astype(F32)


def join_kernel(ret_ref, keep_ref, got_ref, out_ref):
    out_ref[:, 0:16, :] = ret_ref[...]
    out_ref[:, 16:48, :] = (keep_ref[...].astype(F32) + got_ref[...].astype(F32)).astype(BF)


def add_kernel(keep_ref, got_ref, out_ref):
    out_ref[...] = (keep_ref[...].astype(F32) + got_ref[...].astype(F32)).astype(BF)


VM = pl.BlockSpec(memory_space=pltpu.VMEM)
SM = pl.BlockSpec(memory_space=pltpu.SMEM)


def call(kernel, outs, in_specs, scratch=(), name=None):
    return pl.pallas_call(
        kernel,
        out_shape=[jax.ShapeDtypeStruct(s, d) for s, d in outs],
        in_specs=in_specs,
        out_specs=[VM] * len(outs),
        scratch_shapes=list(scratch),
        compiler_params=pltpu.CompilerParams(vmem_limit_bytes=VMEM_LIMIT),
        name=name,
    )


def swapped(value):
    return lax.ppermute(value, "group", [(0, 1), (1, 0)])


def exchanged(value):
    return lax.all_to_all(value, "dom", split_axis=0, concat_axis=0, tiled=True)


def local(
    nodes,
    edges,
    node_cotangent,
    edge_cotangent,
    senders,
    receivers,
    send_rows,
    edge_in,
    edge_out,
    edge_gain,
    node_in,
    node_out,
    node_gain,
):
    x = nodes[0]
    ed = edges[0]
    n, w = x.shape
    e = ed.shape[0]
    domains, slots = send_rows.shape[1:]
    h = domains * slots
    half = w // 2
    flat_list = send_rows.reshape(1, h)
    me = lax.axis_index("group").astype(jnp.int32).reshape(1)
    egain = edge_gain.reshape(1, w)
    ngain = node_gain.reshape(1, w)
    vm = pltpu.VMEM

    (outgoing,) = call(outgoing_kernel, [((h, w), BF)], [VM, VM], name="outgoing")(flat_list, x)
    arrived = exchanged(outgoing.reshape(domains, slots, w)).reshape(h, w)

    ret, keep, give, act, epostg, epg, sums, ntotal = call(
        main_kernel,
        [
            ((domains, 16, half), BF),
            ((domains, 32, half), BF),
            ((domains, 32, half), BF),
            ((e, w), BF),
            ((e, w), BF),
            ((e, w), BF),
            ((2 * n + h, w), BF),
            ((n, w), F32),
        ],
        [SM] + [VM] * 13,
        [
            vm((e, LANES), jnp.int32),
            vm((e, LANES), jnp.int32),
            vm((e, n), BF),
            vm((n, e), BF),
            vm((w + 2 * n + h, w), BF),
            vm((e, w), F32),
            vm((e, w), F32),
            vm((e, LANES), F32),
            vm((n, w), BF),
            vm((n, w), BF),
            vm((n, w), BF),
            vm((n, w), BF),
            vm((n, w), BF),
            vm((8, w), F32),
            vm((8, w), F32),
            vm((domains, 32, half), F32),
        ],
        name="main",
    )(
        me, senders, receivers, x, ed, arrived, node_cotangent[0], edge_cotangent[0],
        edge_in, edge_out, egain, node_in, node_out, ngain,
    )
    got = swapped(give)
    (grad_edges,) = call(grad_edges_kernel, [((e, w), BF)], [VM] * 3, name="grad_edges")(
        epg, edge_cotangent[0], edge_in
    )
    (joined,) = call(join_kernel, [((domains, 48, half), BF)], [VM] * 3, name="join")(
        ret, keep, got
    )
    first = exchanged(joined)
    keep2, give2 = call(
        edge_weights_kernel,
        [((domains, 32, half), BF)] * 2,
        [SM] + [VM] * 7,
        [vm((domains, 32, half), F32)],
        name="edge_weights",
    )(me, ed, x, arrived, act, epostg, epg, sums)
    got2 = swapped(give2)
    (total,) = call(local_sums_kernel, [((n, w), F32)], [VM] * 3, name="local_sums")(
        sums, ntotal, edge_in
    )
    (joined2,) = call(add_kernel, [((domains, 32, half), BF)], [VM] * 2, name="add")(keep2, got2)
    second = exchanged(joined2)
    grad_nodes, node_sums = call(
        grad_nodes_kernel, [((n, w), BF), ((32, half), F32)], [VM] * 3, name="grad_nodes"
    )(flat_list, first, total)
    (mine,) = call(sum_kernel, [((64, half), BF)], [VM] * 2, name="sum")(second, node_sums)
    both = lax.all_gather(mine, "group", axis=0, tiled=False)
    g_ein, g_eout, g_nin, g_nout, gains = call(
        outputs_kernel,
        [((24, w), F32), ((8, w), F32), ((16, w), F32), ((8, w), F32), ((8, LANES), F32)],
        [VM],
        name="outputs",
    )(both)
    return (
        grad_edges[None],
        grad_nodes[None],
        g_ein,
        g_eout,
        g_nin,
        g_nout,
        gains[0, 0:8],
        gains[0, 8:16],
    )


def solution(mesh):
    split = P("group", "dom", None)
    placed = (split,) * 4 + (P("group", "dom"),) * 2 + (split,) + (P(),) * 6
    return jax.shard_map(
        local,
        mesh=mesh,
        in_specs=placed,
        out_specs=(split,) * 2 + (P("dom", None),) * 4 + (P("dom"),) * 2,
        check_vma=False,
    )
```

```python
import functools

import jax
import jax.numpy as jnp
from jax import lax
from jax.experimental import pallas as pl
from jax.experimental.pallas import tpu as pltpu
from jax.sharding import PartitionSpec as P

BF = jnp.bfloat16
F32 = jnp.float32
LANES = 128
MIB = 1024 * 1024


def dot(a, b):
    return jnp.dot(a, b, preferred_element_type=F32)


def dot_nt(a, b):
    return lax.dot_general(a, b, (((1,), (1,)), ((), ())), preferred_element_type=F32)


def dot_tn(a, b):
    return lax.dot_general(a, b, (((0,), (0,)), ((), ())), preferred_element_type=F32)


def spread(ids):
    return jnp.broadcast_to(ids, (LANES, ids.shape[1])).T


def pick(spread_ids, count):
    lane = lax.broadcasted_iota(jnp.int32, spread_ids.shape, 1)
    tiles = [
        jnp.where(spread_ids == lane + LANES * k, 1.0, 0.0).astype(BF)
        for k in range(count // LANES)
    ]
    return jnp.concatenate(tiles, axis=1)


def pick_t(ids, first, count):
    row = lax.broadcasted_iota(jnp.int32, (count, ids.shape[1]), 0) + first
    return jnp.where(row == ids, 1.0, 0.0).astype(BF)


def swish_both(pre):
    gate = jax.nn.sigmoid(pre)
    return pre * gate, gate * (1.0 + pre * (1.0 - gate))


def normalize(hidden):
    centre = hidden - jnp.mean(hidden, axis=-1, keepdims=True)
    inverse = lax.rsqrt(jnp.mean(centre * centre, axis=-1, keepdims=True) + 1e-05)
    return centre * inverse, inverse


def norm_back(upstream, gain, normed, inverse):
    scaled = upstream * gain
    return inverse * (
        scaled
        - jnp.mean(scaled, axis=-1, keepdims=True)
        - normed * jnp.mean(scaled * normed, axis=-1, keepdims=True)
    )


def fold(value):
    return jnp.sum(value.reshape(value.shape[0] // 8, 8, value.shape[1]), axis=0)


def outgoing_kernel(list_ref, nodes_ref, out_ref, rows_ref):
    slots, domains = list_ref.shape
    for s in range(slots):
        sel = pick(spread(list_ref[s : s + 1, :]), nodes_ref.shape[0])
        rows = dot(sel, nodes_ref[...])
        for k in range(rows_ref.shape[0]):
            rows_ref[k, pl.ds(s, domains, stride=slots), :] = rows[:, k * LANES : (k + 1) * LANES]
    for k in range(rows_ref.shape[0]):
        out_ref[:, k * LANES : (k + 1) * LANES] = rows_ref[k].astype(BF)


def early_kernel(send_ref, recv_ref, edges_ref, nodes_ref, ein_ref, out_ref, table):
    n, w = nodes_ref.shape

    @pl.when(pl.program_id(0) == 0)
    def _():
        table[0:w, :] = ein_ref[0:w, :]
        table[w : w + n, :] = dot(nodes_ref[...], ein_ref[w : 2 * w, :]).astype(BF)
        table[w + n : w + 2 * n, :] = dot(nodes_ref[...], ein_ref[2 * w : 3 * w, :]).astype(BF)

    left = jnp.concatenate(
        [edges_ref[...], pick(spread(send_ref[...]), n), pick(spread(recv_ref[...]), n)], axis=1
    )
    out_ref[...] = dot(left, table[...])


def gain_rows(edge_gain, node_gain, domains, width):
    per = edge_gain.shape[1] // domains
    shape = (domains, edge_gain.shape[1])
    own = lax.broadcasted_iota(jnp.int32, shape, 1) // per == lax.broadcasted_iota(
        jnp.int32, shape, 0
    )
    col = lax.broadcasted_iota(jnp.int32, (edge_gain.shape[1], width), 0) % per
    lane = lax.broadcasted_iota(jnp.int32, (edge_gain.shape[1], width), 1)
    total = 0.0
    for k, gain in enumerate((edge_gain, node_gain)):
        mine = jnp.where(own, jnp.broadcast_to(gain, shape), 0.0).astype(BF)
        place = jnp.where(lane == col + per * k, 1.0, 0.0).astype(BF)
        total = total + dot(mine, place)
    return total


def main_kernel(
    g_ref, send_ref, recv_ref, egain_ref, ngain_ref,
    arrived_hbm, ein_hbm, pre_hbm, eout_hbm, nodes_hbm, nin_hbm, nout_hbm, ncot_hbm, ecot_hbm,
    ret_ref, keep_ref, give_ref, halo_ref,
    act_hbm, epostg_hbm, epg_hbm, ntotal_hbm,
    arrived, weight, hat, eout, nodes, nin, nout, ncot, ecot,
    act_ref, epostg_ref, epg_ref, ntotal_ref,
    cs, cr, slope, inv, gath, nact, npostg, nprg, gg, eacc, nacc, share,
    in_sem, pre_sem, out_sem,
):
    n, w = nodes.shape
    e = hat.shape[0]
    h = arrived.shape[0]
    half = w // 2
    domains = share.shape[0]
    eb = 512
    nb = 512
    blocks = e // eb

    loads = [
        pltpu.make_async_copy(source, target, in_sem.at[k])
        for k, (source, target) in enumerate(
            (
                (arrived_hbm, arrived),
                (ein_hbm.at[pl.ds(w, w), :], weight),
                (eout_hbm, eout),
                (nodes_hbm, nodes),
                (nin_hbm, nin),
                (nout_hbm, nout),
                (ncot_hbm, ncot),
                (ecot_hbm, ecot),
            )
        )
    ]

    def pre_load(b):
        rows = pl.ds(pl.multiple_of(b * eb, eb), eb)
        return pltpu.make_async_copy(pre_hbm.at[rows, :], hat.at[rows, :], pre_sem.at[b])

    def store(source, target, k, b):
        rows = pl.ds(pl.multiple_of(b * eb, eb), eb)
        return pltpu.make_async_copy(source.at[rows, :], target.at[rows, :], out_sem.at[k, b])

    for k in range(3):
        loads[k].start()
    for b in range(blocks):
        pre_load(b).start()
    for k in range(3, 8):
        loads[k].start()
    cs[...] = spread(send_ref[...])
    cr[...] = spread(recv_ref[...])
    egain = egain_ref[...]
    ngain = ngain_ref[...]
    for k in range(3):
        loads[k].wait()
    far = dot(arrived[...], weight[...]).astype(BF)
    arrived[...] = far

    def edge_forward(b, carry):
        rows = pl.ds(pl.multiple_of(b * eb, eb), eb)
        sel = pick(cs[rows, :] - n, h)
        pre_load(b).wait()
        pre = hat[rows, :] + dot(sel, arrived[...])
        act, slp = swish_both(pre)
        act = act.astype(BF)
        act_ref[rows, :] = act
        store(act_ref, act_hbm, 0, b).start()
        slope[rows, :] = slp
        normed, inverse = normalize(dot(act, eout[...]))
        hat[rows, :] = normed
        inv[rows, :] = jnp.broadcast_to(inverse, (eb, LANES))
        epostg_ref[rows, :] = (normed * egain).astype(BF)
        return carry

    lax.fori_loop(0, blocks, edge_forward, 0)
    nacc[...] = jnp.zeros_like(nacc)
    eacc[...] = jnp.zeros_like(eacc)
    for k in range(3, 7):
        loads[k].wait()

    def node_block(b, carry):
        first = pl.multiple_of(b * nb, nb)
        rows = pl.ds(first, nb)
        gathered = dot(pick_t(recv_ref[...], first, nb), epostg_ref[...]).astype(BF)
        gath[rows, :] = gathered
        pre = dot(jnp.concatenate([nodes[rows, :], gathered], axis=1), nin[...])
        act, slp = swish_both(pre)
        act = act.astype(BF)
        nact[rows, :] = act
        normed, inverse = normalize(dot(act, nout[...]))
        upstream = ncot[rows, :].astype(F32)
        nacc[...] += fold(upstream * normed)
        postg = norm_back(upstream, ngain, normed, inverse).astype(BF)
        npostg[rows, :] = postg
        preg = (dot_nt(postg, nout[...]) * slp).astype(BF)
        nprg[rows, :] = preg
        back = dot_nt(preg, nin[...])
        ntotal_ref[rows, :] = upstream + back[:, :w]
        store(ntotal_ref, ntotal_hbm, 3, b).start()
        gg[rows, :] = back[:, w:].astype(BF)
        return carry

    lax.fori_loop(0, n // nb, node_block, 0)
    loads[7].wait()

    def edge_backward(b, carry):
        rows = pl.ds(pl.multiple_of(b * eb, eb), eb)
        upstream = ecot[rows, :].astype(F32) + dot(pick(cr[rows, :], n), gg[...])
        normed = hat[rows, :]
        eacc[...] += fold(upstream * normed)
        postg = norm_back(upstream, egain, normed, inv[rows, 0:1]).astype(BF)
        epostg_ref[rows, :] = postg
        store(epostg_ref, epostg_hbm, 1, b).start()
        epg_ref[rows, :] = (dot_nt(postg, eout[...]) * slope[rows, :]).astype(BF)
        store(epg_ref, epg_hbm, 2, b).start()
        return carry

    lax.fori_loop(0, blocks, edge_backward, 0)
    halo = dot(pick_t(send_ref[...], n, h), epg_ref[...]).astype(BF)
    halo_ref[...] = halo
    ret = dot_nt(halo, weight[...])
    per = h // domains
    ret_ref[:, 0:per, :] = ret[:, :half].reshape(domains, per, half).astype(BF)
    ret_ref[:, per : 2 * per, :] = ret[:, half:].reshape(domains, per, half).astype(BF)

    mine = g_ref[0]
    gains = gain_rows(
        jnp.sum(eacc[...], axis=0, keepdims=True),
        jnp.sum(nacc[...], axis=0, keepdims=True),
        domains,
        half,
    )
    share[:, 24:32, :] = jnp.broadcast_to(gains[:, None, :], (domains, 8, half))
    for out_ref, which in ((keep_ref, mine), (give_ref, 1 - mine)):
        cols = pl.ds(pl.multiple_of(which * half, half), half)
        pg = nprg[:, cols]
        for k, source in enumerate((nodes, gath)):
            grad = dot_tn(source[...], pg)
            share[k * (domains // 2) : (k + 1) * (domains // 2), 0:16, :] = grad.reshape(
                domains // 2, 16, half
            )
        share[:, 16:24, :] = dot_tn(nact[...], npostg[:, cols]).reshape(domains, 8, half)
        out_ref[...] = share[...].astype(BF)
    for b in range(blocks):
        store(act_ref, act_hbm, 0, b).wait()
        store(epostg_ref, epostg_hbm, 1, b).wait()
        store(epg_ref, epg_hbm, 2, b).wait()
    for b in range(n // nb):
        store(ntotal_ref, ntotal_hbm, 3, b).wait()


def grad_edges_kernel(epg_ref, ecot_ref, ein_ref, out_ref):
    out_ref[...] = (ecot_ref[...].astype(F32) + dot_nt(epg_ref[...], ein_ref[...])).astype(BF)


def edge_weights_kernel(
    g_ref, send_ref, recv_ref,
    epg_hbm, edges_hbm, nodes_hbm, arrived_hbm, halo_hbm, act_hbm, epostg_hbm,
    keep_ref, give_ref, sums_hbm,
    epg, edges, nodes, arrived, halo, act, epostg, sums, share, in_sem, out_sem,
):
    n, w = nodes.shape
    half = w // 2
    domains = share.shape[0]
    nb = 512
    loads = [
        pltpu.make_async_copy(source, target, in_sem.at[k])
        for k, (source, target) in enumerate(
            (
                (epg_hbm, epg),
                (edges_hbm, edges),
                (nodes_hbm, nodes),
                (arrived_hbm, arrived),
                (halo_hbm, halo),
                (act_hbm, act),
                (epostg_hbm, epostg),
            )
        )
    ]
    for load in loads:
        load.start()
    loads[0].wait()

    def node_sums(b, carry):
        first = pl.multiple_of(b * nb, nb)
        later = pl.multiple_of(n + b * nb, nb)
        sums[pl.ds(first, nb), :] = dot(pick_t(send_ref[...], first, nb), epg[...]).astype(BF)
        sums[pl.ds(later, nb), :] = dot(pick_t(recv_ref[...], first, nb), epg[...]).astype(BF)
        return carry

    lax.fori_loop(0, n // nb, node_sums, 0)
    out = pltpu.make_async_copy(sums, sums_hbm, out_sem)
    out.start()
    for load in loads[1:]:
        load.wait()
    mine = g_ref[0]
    per = 3 * w // domains // 8
    for out_ref, which in ((keep_ref, mine), (give_ref, 1 - mine)):
        cols = pl.ds(pl.multiple_of(which * half, half), half)
        both = dot_tn(nodes[...], jnp.concatenate([sums[0:n, cols], sums[n:, cols]], axis=1))
        parts = (
            dot_tn(edges[...], epg[:, cols]),
            both[:, :half] + dot_tn(arrived[...], halo[:, cols]),
            both[:, half:],
        )
        for k, part in enumerate(parts):
            for j in range(w // 8):
                t = k * (w // 8) + j
                share[t // per, (t % per) * 8 : (t % per) * 8 + 8, :] = part[j * 8 : j * 8 + 8, :]
        share[:, 24:32, :] = dot_tn(act[...], epostg[:, cols]).reshape(domains, 8, half)
        out_ref[...] = share[...].astype(BF)
    out.wait()


def local_sums_kernel(send_ref, recv_ref, ntotal_ref, ws_ref, wr_ref, out_ref):
    out_ref[...] = (
        ntotal_ref[...] + dot_nt(send_ref[...], ws_ref[...]) + dot_nt(recv_ref[...], wr_ref[...])
    )


def grad_nodes_kernel(list_ref, first_ref, total_ref, out_ref, back):
    domains, rows, half = first_ref.shape
    slots = rows // 2
    block = total_ref.shape[0]

    @pl.when(pl.program_id(0) == 0)
    def _():
        for k in range(2):
            part = first_ref[:, k * slots : (k + 1) * slots, :].astype(F32)
            back[:, k * half : (k + 1) * half] = part.reshape(domains * slots, half).astype(BF)

    sel = pick_t(list_ref[...], pl.program_id(0) * block, block)
    out_ref[...] = (total_ref[...] + dot(sel, back[...])).astype(BF)


def sum_kernel(all_ref, out_ref):
    out_ref[...] = jnp.sum(all_ref[...].astype(F32), axis=0).astype(BF)


def edge_outputs_kernel(g_ref, mine_ref, got_ref, ein_ref, eout_ref):
    half = mine_ref.shape[1]
    low = g_ref[0] == 0
    mine = mine_ref[...].astype(F32)
    got = got_ref[...].astype(F32)
    for k, value in enumerate((jnp.where(low, mine, got), jnp.where(low, got, mine))):
        cols = slice(k * half, (k + 1) * half)
        ein_ref[:, cols] = value[0:24, :]
        eout_ref[:, cols] = value[24:32, :]


def node_outputs_kernel(g_ref, mine_ref, got_ref, nin_ref, nout_ref, gains_ref):
    half = mine_ref.shape[1]
    low = g_ref[0] == 0
    mine = mine_ref[...].astype(F32)
    got = got_ref[...].astype(F32)
    for k, value in enumerate((jnp.where(low, mine, got), jnp.where(low, got, mine))):
        cols = slice(k * half, (k + 1) * half)
        nin_ref[:, cols] = value[0:16, :]
        nout_ref[:, cols] = value[16:24, :]
    gains_ref[...] = mine[24:32, 0:LANES]


def join_kernel(ret_ref, keep_ref, got_ref, out_ref):
    out_ref[:, 0:16, :] = ret_ref[...]
    out_ref[:, 16:48, :] = (keep_ref[...].astype(F32) + got_ref[...].astype(F32)).astype(BF)


def add_kernel(keep_ref, got_ref, out_ref):
    out_ref[...] = (keep_ref[...].astype(F32) + got_ref[...].astype(F32)).astype(BF)


VM = pl.BlockSpec(memory_space=pltpu.VMEM)
SM = pl.BlockSpec(memory_space=pltpu.SMEM)
ANY = pl.BlockSpec(memory_space=pltpu.HBM)


def whole(shape):
    return pl.BlockSpec(shape, lambda i: (0,) * len(shape))


def along(shape, dim, first=0):
    return pl.BlockSpec(
        shape, lambda i: tuple(first + i if d == dim else 0 for d in range(len(shape)))
    )


def call(kernel, outs, in_specs, out_specs, scratch=(), name=None, mib=16, grid=(), far=True):
    return pl.pallas_call(
        kernel,
        out_shape=[pltpu.HBM(s, d) if far else jax.ShapeDtypeStruct(s, d) for s, d in outs],
        grid=grid,
        in_specs=in_specs,
        out_specs=out_specs,
        scratch_shapes=list(scratch),
        compiler_params=pltpu.CompilerParams(vmem_limit_bytes=mib * MIB),
        name=name,
    )


def far(*values):
    return tuple(pltpu.with_memory_space_constraint(v, pltpu.HBM) for v in values)


def swapped(value):
    return lax.ppermute(value, "group", [(0, 1), (1, 0)])


def exchanged(value):
    return lax.all_to_all(value, "dom", split_axis=0, concat_axis=0, tiled=True)


def local(
    nodes,
    edges,
    node_cotangent,
    edge_cotangent,
    senders,
    receivers,
    send_rows,
    edge_in,
    edge_out,
    edge_gain,
    node_in,
    node_out,
    node_gain,
):
    x = nodes[0]
    ed = edges[0]
    ncot = node_cotangent[0]
    ecot = edge_cotangent[0]
    n, w = x.shape
    e = ed.shape[0]
    domains, slots = send_rows.shape[1:]
    h = domains * slots
    half = w // 2
    me = lax.axis_index("group").astype(jnp.int32).reshape(1)
    egain = edge_gain.reshape(1, w)
    ngain = node_gain.reshape(1, w)
    vm = pltpu.VMEM
    dma = pltpu.SemaphoreType.DMA

    (outgoing,) = call(
        outgoing_kernel, [((h, w), BF)], [VM, VM], [VM], [vm((w // LANES, h, LANES), F32)], name="outgoing"
    )(send_rows[0].T, *far(x))
    arrived = exchanged(outgoing.reshape(domains, slots, w)).reshape(h, w)
    eb = 512
    (pre,) = call(
        early_kernel,
        [((e, w), F32)],
        [
            along((1, eb), 1),
            along((1, eb), 1),
            along((eb, w), 0),
            whole((n, w)),
            whole((3 * w, w)),
        ],
        [along((eb, w), 0)],
        [vm((w + 2 * n, w), BF)],
        name="early",
        mib=32,
        grid=(e // eb,),
    )(senders, receivers, *far(ed, x, edge_in))

    ret, keep, give, halo, act, epostg, epg, ntotal = call(
        main_kernel,
        [
            ((domains, 2 * slots, half), BF),
            ((domains, 32, half), BF),
            ((domains, 32, half), BF),
            ((h, w), BF),
            ((e, w), BF),
            ((e, w), BF),
            ((e, w), BF),
            ((n, w), F32),
        ],
        [SM] + [VM] * 4 + [ANY] * 9,
        [VM] * 4 + [ANY] * 4,
        [
            vm((h, w), BF),
            vm((w, w), BF),
            vm((e, w), F32),
            vm((w, w), BF),
            vm((n, w), BF),
            vm((2 * w, w), BF),
            vm((w, w), BF),
            vm((n, w), BF),
            vm((e, w), BF),
            vm((e, w), BF),
            vm((e, w), BF),
            vm((e, w), BF),
            vm((n, w), F32),
            vm((e, LANES), jnp.int32),
            vm((e, LANES), jnp.int32),
            vm((e, w), F32),
            vm((e, LANES), F32),
            vm((n, w), BF),
            vm((n, w), BF),
            vm((n, w), BF),
            vm((n, w), BF),
            vm((n, w), BF),
            vm((8, w), F32),
            vm((8, w), F32),
            vm((domains, 32, half), F32),
            dma((8,)),
            dma((e // eb,)),
            dma((4, e // eb)),
        ],
        name="main",
        mib=54,
    )(
        me, senders, receivers, egain, ngain,
        arrived, edge_in, pre, edge_out, x, node_in, node_out, ncot, ecot,
    )
    share = ((domains, 32, half), BF)
    part = along((domains // 4, 32, half), 0)
    (joined,) = call(
        join_kernel,
        [((domains, 48, half), BF)],
        [along((domains // 4, 16, half), 0), part, part],
        [along((domains // 4, 48, half), 0)],
        name="join",
        grid=(4,),
    )(ret, keep, swapped(give))
    joined, epg = lax.optimization_barrier((joined, epg))
    first = exchanged(joined)
    keep2, give2, sums = call(
        edge_weights_kernel,
        [share, share, ((2 * n, w), BF)],
        [SM] + [VM] * 2 + [ANY] * 7,
        [VM, VM, ANY],
        [
            vm((e, w), BF),
            vm((e, w), BF),
            vm((n, w), BF),
            vm((h, w), BF),
            vm((h, w), BF),
            vm((e, w), BF),
            vm((e, w), BF),
            vm((2 * n, w), BF),
            vm((domains, 32, half), F32),
            dma((7,)),
            dma,
        ],
        name="edge_weights",
        mib=44,
    )(me, senders, receivers, *far(epg, ed, x, arrived, halo, act, epostg))
    (joined2,) = call(add_kernel, [share], [part, part], [part], name="add", grid=(4,))(
        keep2, swapped(give2)
    )
    joined2, first = lax.optimization_barrier((joined2, first))
    second = exchanged(joined2)
    (grad_edges,) = call(
        grad_edges_kernel,
        [((e, w), BF)],
        [along((eb, w), 0), along((eb, w), 0), whole((w, w))],
        [along((eb, w), 0)],
        name="grad_edges",
        grid=(e // eb,),
    )(*far(epg, ecot, edge_in))
    nb = 256
    (total,) = call(
        local_sums_kernel,
        [((n, w), F32)],
        [
            along((nb, w), 0),
            along((nb, w), 0, n // nb),
            along((nb, w), 0),
            pl.BlockSpec((w, w), lambda i: (1, 0)),
            pl.BlockSpec((w, w), lambda i: (2, 0)),
        ],
        [along((nb, w), 0)],
        name="local_sums",
        grid=(n // nb,),
    )(*far(sums, sums, ntotal, edge_in, edge_in))
    (grad_nodes,) = call(
        grad_nodes_kernel,
        [((n, w), BF)],
        [whole((1, h)), whole((domains, 2 * slots, half)), along((nb, w), 0)],
        [along((nb, w), 0)],
        [vm((h, w), BF)],
        name="grad_nodes",
        grid=(n // nb,),
    )(send_rows.reshape(1, h), first, *far(total))
    (node_sum,) = call(
        sum_kernel,
        [((32, half), BF)],
        [along((domains, 16, half), 1, 1)],
        [along((16, half), 0)],
        name="node_sum",
        grid=(2,),
    )(first)
    g_nin, g_nout, gains = call(
        node_outputs_kernel,
        [((16, w), F32), ((8, w), F32), ((8, LANES), F32)],
        [SM, VM, VM],
        [VM] * 3,
        name="node_outputs",
    )(me, node_sum, swapped(node_sum))
    (edge_sum,) = call(
        sum_kernel,
        [((32, half), BF)],
        [along((domains, 16, half), 1)],
        [along((16, half), 0)],
        name="edge_sum",
        grid=(2,),
    )(second)
    g_ein, g_eout = call(
        edge_outputs_kernel,
        [((24, w), F32), ((8, w), F32)],
        [SM, VM, VM],
        [VM] * 2,
        name="edge_outputs",
    )(me, edge_sum, swapped(edge_sum))
    return (
        grad_edges[None],
        grad_nodes[None],
        g_ein,
        g_eout,
        g_nin,
        g_nout,
        gains[0, 0:8],
        gains[0, 8:16],
    )


def solution(mesh):
    split = P("group", "dom", None)
    placed = (split,) * 4 + (P("group", "dom"),) * 2 + (split,) + (P(),) * 6
    return jax.shard_map(
        local,
        mesh=mesh,
        in_specs=placed,
        out_specs=(split,) * 2 + (P("dom", None),) * 4 + (P("dom"),) * 2,
        check_vma=False,
    )
```

```python
import functools

import jax
import jax.numpy as jnp
from jax import lax
from jax.experimental import pallas as pl
from jax.experimental.pallas import tpu as pltpu
from jax.sharding import PartitionSpec as P

BF = jnp.bfloat16
F32 = jnp.float32
LANES = 128
MIB = 1024 * 1024


def dot(a, b):
    return jnp.dot(a, b, preferred_element_type=F32)


def dot_nt(a, b):
    return lax.dot_general(a, b, (((1,), (1,)), ((), ())), preferred_element_type=F32)


def dot_tn(a, b):
    return lax.dot_general(a, b, (((0,), (0,)), ((), ())), preferred_element_type=F32)


def spread(ids):
    return jnp.broadcast_to(ids, (LANES, ids.shape[1])).T


def pick(spread_ids, count):
    lane = lax.broadcasted_iota(jnp.int32, spread_ids.shape, 1)
    from_lane = (spread_ids - lane).astype(jnp.int16)
    one = jnp.ones(spread_ids.shape, BF)
    tiles = [
        jnp.where(from_lane == jnp.int16(LANES * k), one, jnp.zeros_like(one))
        for k in range(count // LANES)
    ]
    return jnp.concatenate(tiles, axis=1)


def pick_t(ids, first, count):
    row = lax.broadcasted_iota(jnp.int32, (count, ids.shape[1]), 0) + first
    return jnp.where(row == ids, 1.0, 0.0).astype(BF)


def swish_both(pre):
    gate = jax.nn.sigmoid(pre)
    return pre * gate, gate * (1.0 + pre * (1.0 - gate))


def normalize(hidden):
    centre = hidden - jnp.mean(hidden, axis=-1, keepdims=True)
    inverse = lax.rsqrt(jnp.mean(centre * centre, axis=-1, keepdims=True) + 1e-05)
    return centre * inverse, inverse


def norm_back(upstream, gain, normed, inverse):
    scaled = upstream * gain
    return inverse * (
        scaled
        - jnp.mean(scaled, axis=-1, keepdims=True)
        - normed * jnp.mean(scaled * normed, axis=-1, keepdims=True)
    )


def fold(value):
    return jnp.sum(value.reshape(value.shape[0] // 8, 8, value.shape[1]), axis=0)


def outgoing_kernel(list_ref, nodes_ref, out_ref, rows_ref):
    slots, domains = list_ref.shape
    ids = jnp.concatenate([spread(list_ref[s : s + 1, :]) for s in range(slots)], axis=0)
    rows = dot(pick(ids, nodes_ref.shape[0]), nodes_ref[...])
    for s in range(slots):
        for k in range(rows_ref.shape[0]):
            rows_ref[k, pl.ds(s, domains, stride=slots), :] = rows[
                s * domains : (s + 1) * domains, k * LANES : (k + 1) * LANES
            ]
    for k in range(rows_ref.shape[0]):
        out_ref[:, k * LANES : (k + 1) * LANES] = rows_ref[k].astype(BF)


def early_kernel(send_ref, recv_ref, edges_ref, nodes_ref, ein_ref, out_ref, table):
    n, w = nodes_ref.shape

    @pl.when(pl.program_id(0) == 0)
    def _():
        table[0:w, :] = ein_ref[0:w, :]
        table[w : w + n, :] = dot(nodes_ref[...], ein_ref[w : 2 * w, :]).astype(BF)
        table[w + n : w + 2 * n, :] = dot(nodes_ref[...], ein_ref[2 * w : 3 * w, :]).astype(BF)

    left = jnp.concatenate(
        [edges_ref[...], pick(spread(send_ref[...]), n), pick(spread(recv_ref[...]), n)], axis=1
    )
    out_ref[...] = dot(left, table[...])


def gain_rows(edge_gain, node_gain, domains, width):
    per = edge_gain.shape[1] // domains
    shape = (domains, edge_gain.shape[1])
    own = lax.broadcasted_iota(jnp.int32, shape, 1) // per == lax.broadcasted_iota(
        jnp.int32, shape, 0
    )
    col = lax.broadcasted_iota(jnp.int32, (edge_gain.shape[1], width), 0) % per
    lane = lax.broadcasted_iota(jnp.int32, (edge_gain.shape[1], width), 1)
    total = 0.0
    for k, gain in enumerate((edge_gain, node_gain)):
        mine = jnp.where(own, jnp.broadcast_to(gain, shape), 0.0).astype(BF)
        place = jnp.where(lane == col + per * k, 1.0, 0.0).astype(BF)
        total = total + dot(mine, place)
    return total


def main_kernel(
    g_ref, send_ref, recv_ref, egain_ref, ngain_ref,
    arrived_hbm, ein_hbm, pre_hbm, eout_hbm, nodes_hbm, nin_hbm, nout_hbm, ncot_hbm, ecot_hbm,
    ret_ref, keep_ref, give_ref, halo_ref,
    act_hbm, epostg_hbm, epg_hbm, ntotal_hbm,
    arrived, weight, hat, own, turned, nodes, ncot, ecot,
    act_ref, epostg_ref, epg_ref, ntotal_ref,
    cs, cr, slope, inv, gath, nact, npostg, nprg, gg, eacc, nacc, share,
    in_sem, pre_sem, out_sem,
):
    n, w = nodes.shape
    e = hat.shape[0]
    h = arrived.shape[0]
    half = w // 2
    domains = share.shape[0]
    eb = 512
    nb = 512
    blocks = e // eb

    loads = [
        pltpu.make_async_copy(source, target, in_sem.at[k])
        for k, (source, target) in enumerate(
            (
                (arrived_hbm, arrived),
                (ein_hbm.at[pl.ds(w, w), :], weight),
                (eout_hbm, own.at[pl.ds(0, w), :]),
                (nin_hbm, own.at[pl.ds(w, 2 * w), :]),
                (nout_hbm, own.at[pl.ds(3 * w, w), :]),
                (nodes_hbm, nodes),
                (ncot_hbm, ncot),
                (ecot_hbm, ecot),
            )
        )
    ]

    def pre_load(b):
        rows = pl.ds(pl.multiple_of(b * eb, eb), eb)
        return pltpu.make_async_copy(pre_hbm.at[rows, :], hat.at[rows, :], pre_sem.at[b])

    def store(source, target, k, b):
        rows = pl.ds(pl.multiple_of(b * eb, eb), eb)
        return pltpu.make_async_copy(source.at[rows, :], target.at[rows, :], out_sem.at[k, b])

    for k in range(3):
        loads[k].start()
    pre_load(0).start()
    for k in range(3, 5):
        loads[k].start()
    for b in range(1, blocks):
        pre_load(b).start()
    for k in range(5, 8):
        loads[k].start()
    cs[...] = spread(send_ref[...])
    cr[...] = spread(recv_ref[...])
    egain = egain_ref[...]
    ngain = ngain_ref[...]
    for k in range(5):
        loads[k].wait()
    far = dot(arrived[...], weight[...]).astype(BF)
    arrived[...] = far

    def edge_forward(b, carry):
        rows = pl.ds(pl.multiple_of(b * eb, eb), eb)
        sel = pick(cs[rows, :] - n, h)
        pre_load(b).wait()
        pre = hat[rows, :] + dot(sel, arrived[...])
        act, slp = swish_both(pre)
        act = act.astype(BF)
        act_ref[rows, :] = act
        store(act_ref, act_hbm, 0, b).start()
        slope[rows, :] = slp
        turned[rows, :] = own[rows, :].T
        normed, inverse = normalize(dot(act, own[0:w, :]))
        hat[rows, :] = normed
        inv[rows, :] = jnp.broadcast_to(inverse, (eb, LANES))
        epostg_ref[rows, :] = (normed * egain).astype(BF)
        return carry

    lax.fori_loop(0, blocks, edge_forward, 0)
    nacc[...] = jnp.zeros_like(nacc)
    eacc[...] = jnp.zeros_like(eacc)
    for k in range(5, 7):
        loads[k].wait()

    def node_block(b, carry):
        first = pl.multiple_of(b * nb, nb)
        rows = pl.ds(first, nb)
        gathered = dot(pick_t(recv_ref[...], first, nb), epostg_ref[...]).astype(BF)
        gath[rows, :] = gathered
        pre = dot(jnp.concatenate([nodes[rows, :], gathered], axis=1), own[w : 3 * w, :])
        act, slp = swish_both(pre)
        act = act.astype(BF)
        nact[rows, :] = act
        normed, inverse = normalize(dot(act, own[3 * w :, :]))
        upstream = ncot[rows, :].astype(F32)
        nacc[...] += fold(upstream * normed)
        postg = norm_back(upstream, ngain, normed, inverse).astype(BF)
        npostg[rows, :] = postg
        preg = (dot(postg, turned[3 * w :, :]) * slp).astype(BF)
        nprg[rows, :] = preg
        ntotal_ref[rows, :] = upstream + dot(preg, turned[w : 2 * w, :])
        store(ntotal_ref, ntotal_hbm, 3, b).start()
        gg[rows, :] = dot(preg, turned[2 * w : 3 * w, :]).astype(BF)
        return carry

    lax.fori_loop(0, n // nb, node_block, 0)
    loads[7].wait()

    def edge_backward(b, carry):
        rows = pl.ds(pl.multiple_of(b * eb, eb), eb)
        upstream = ecot[rows, :].astype(F32) + dot(pick(cr[rows, :], n), gg[...])
        normed = hat[rows, :]
        eacc[...] += fold(upstream * normed)
        postg = norm_back(upstream, egain, normed, inv[rows, 0:1]).astype(BF)
        epostg_ref[rows, :] = postg
        store(epostg_ref, epostg_hbm, 1, b).start()
        epg_ref[rows, :] = (dot(postg, turned[0:w, :]) * slope[rows, :]).astype(BF)
        store(epg_ref, epg_hbm, 2, b).start()
        return carry

    lax.fori_loop(0, blocks, edge_backward, 0)
    halo = dot(pick_t(send_ref[...], n, h), epg_ref[...]).astype(BF)
    halo_ref[...] = halo
    ret = dot_nt(halo, weight[...])
    per = h // domains
    ret_ref[:, 0:per, :] = ret[:, :half].reshape(domains, per, half).astype(BF)
    ret_ref[:, per : 2 * per, :] = ret[:, half:].reshape(domains, per, half).astype(BF)

    gains = gain_rows(
        jnp.sum(eacc[...], axis=0, keepdims=True),
        jnp.sum(nacc[...], axis=0, keepdims=True),
        domains,
        half,
    )
    gains = jnp.concatenate([gains, gains], axis=1)
    share[:, 24:32, :] = jnp.broadcast_to(gains[:, None, :], (domains, 8, w))
    for k, source in enumerate((nodes, gath)):
        share[k * (domains // 2) : (k + 1) * (domains // 2), 0:16, :] = dot_tn(
            source[...], nprg[...]
        ).reshape(domains // 2, 16, w)
    share[:, 16:24, :] = dot_tn(nact[...], npostg[...]).reshape(domains, 8, w)
    mine = g_ref[0]
    keep_ref[...] = share[:, :, pl.ds(pl.multiple_of(mine * half, half), half)].astype(BF)
    give_ref[...] = share[:, :, pl.ds(pl.multiple_of((1 - mine) * half, half), half)].astype(BF)
    for b in range(blocks):
        store(act_ref, act_hbm, 0, b).wait()
        store(epostg_ref, epostg_hbm, 1, b).wait()
        store(epg_ref, epg_hbm, 2, b).wait()
    for b in range(n // nb):
        store(ntotal_ref, ntotal_hbm, 3, b).wait()


def grad_edges_kernel(epg_ref, ecot_ref, ein_ref, out_ref, turned):
    @pl.when(pl.program_id(0) == 0)
    def _():
        turned[...] = ein_ref[...].T

    out_ref[...] = (ecot_ref[...].astype(F32) + dot(epg_ref[...], turned[...])).astype(BF)


def edge_weights_kernel(
    g_ref, send_ref, recv_ref,
    epg_hbm, edges_hbm, nodes_hbm, arrived_hbm, halo_hbm, act_hbm, epostg_hbm,
    keep_ref, give_ref, sums_hbm,
    epg, edges, nodes, arrived, halo, act, epostg, sums, share, in_sem, out_sem,
):
    n, w = nodes.shape
    half = w // 2
    domains = share.shape[0]
    nb = 512
    loads = [
        pltpu.make_async_copy(source, target, in_sem.at[k])
        for k, (source, target) in enumerate(
            (
                (epg_hbm, epg),
                (edges_hbm, edges),
                (nodes_hbm, nodes),
                (arrived_hbm, arrived),
                (halo_hbm, halo),
                (act_hbm, act),
                (epostg_hbm, epostg),
            )
        )
    ]
    for load in loads:
        load.start()
    loads[0].wait()

    def node_sums(b, carry):
        first = pl.multiple_of(b * nb, nb)
        later = pl.multiple_of(n + b * nb, nb)
        sums[pl.ds(first, nb), :] = dot(pick_t(send_ref[...], first, nb), epg[...]).astype(BF)
        sums[pl.ds(later, nb), :] = dot(pick_t(recv_ref[...], first, nb), epg[...]).astype(BF)
        return carry

    lax.fori_loop(0, n // nb, node_sums, 0)
    out = pltpu.make_async_copy(sums, sums_hbm, out_sem)
    out.start()
    for load in loads[1:]:
        load.wait()
    per = 3 * w // domains // 8

    def put(k, part):
        for j in range(w // 8):
            t = k * (w // 8) + j
            share[t // per, (t % per) * 8 : (t % per) * 8 + 8, :] = part[j * 8 : j * 8 + 8, :]

    put(0, dot_tn(edges[...], epg[...]))
    both = dot_tn(nodes[...], jnp.concatenate([sums[0:n, :], sums[n:, :]], axis=1))
    put(1, both[:, :w] + dot_tn(arrived[...], halo[...]))
    put(2, both[:, w:])
    share[:, 24:32, :] = dot_tn(act[...], epostg[...]).reshape(domains, 8, w)
    mine = g_ref[0]
    keep_ref[...] = share[:, :, pl.ds(pl.multiple_of(mine * half, half), half)].astype(BF)
    give_ref[...] = share[:, :, pl.ds(pl.multiple_of((1 - mine) * half, half), half)].astype(BF)
    out.wait()


def local_sums_kernel(send_ref, recv_ref, ntotal_ref, ws_ref, wr_ref, out_ref, turned):
    w = ws_ref.shape[0]

    @pl.when(pl.program_id(0) == 0)
    def _():
        turned[0:w, :] = ws_ref[...].T
        turned[w:, :] = wr_ref[...].T

    both = jnp.concatenate([send_ref[...], recv_ref[...]], axis=1)
    out_ref[...] = ntotal_ref[...] + dot(both, turned[...])


def grad_nodes_kernel(list_ref, first_ref, total_ref, out_ref, back):
    domains, rows, half = first_ref.shape
    slots = rows // 2
    block = total_ref.shape[0]

    @pl.when(pl.program_id(0) == 0)
    def _():
        for k in range(2):
            part = first_ref[:, k * slots : (k + 1) * slots, :].astype(F32)
            back[:, k * half : (k + 1) * half] = part.reshape(domains * slots, half).astype(BF)

    sel = pick_t(list_ref[...], pl.program_id(0) * block, block)
    out_ref[...] = (total_ref[...] + dot(sel, back[...])).astype(BF)


def sum_kernel(all_ref, out_ref):
    out_ref[...] = jnp.sum(all_ref[...].astype(F32), axis=0).astype(BF)


def edge_outputs_kernel(g_ref, mine_ref, got_ref, ein_ref, eout_ref):
    half = mine_ref.shape[1]
    low = g_ref[0] == 0
    mine = mine_ref[...].astype(F32)
    got = got_ref[...].astype(F32)
    for k, value in enumerate((jnp.where(low, mine, got), jnp.where(low, got, mine))):
        cols = slice(k * half, (k + 1) * half)
        ein_ref[:, cols] = value[0:24, :]
        eout_ref[:, cols] = value[24:32, :]


def node_outputs_kernel(g_ref, mine_ref, got_ref, nin_ref, nout_ref, gains_ref):
    half = mine_ref.shape[1]
    low = g_ref[0] == 0
    mine = mine_ref[...].astype(F32)
    got = got_ref[...].astype(F32)
    for k, value in enumerate((jnp.where(low, mine, got), jnp.where(low, got, mine))):
        cols = slice(k * half, (k + 1) * half)
        nin_ref[:, cols] = value[0:16, :]
        nout_ref[:, cols] = value[16:24, :]
    gains_ref[...] = mine[24:32, 0:LANES]


def join_kernel(ret_ref, keep_ref, got_ref, out_ref):
    out_ref[:, 0:16, :] = ret_ref[...]
    out_ref[:, 16:48, :] = (keep_ref[...].astype(F32) + got_ref[...].astype(F32)).astype(BF)


def add_kernel(keep_ref, got_ref, out_ref):
    out_ref[...] = (keep_ref[...].astype(F32) + got_ref[...].astype(F32)).astype(BF)


VM = pl.BlockSpec(memory_space=pltpu.VMEM)
SM = pl.BlockSpec(memory_space=pltpu.SMEM)
ANY = pl.BlockSpec(memory_space=pltpu.HBM)


def whole(shape):
    return pl.BlockSpec(shape, lambda i: (0,) * len(shape))


def along(shape, dim, first=0):
    return pl.BlockSpec(
        shape, lambda i: tuple(first + i if d == dim else 0 for d in range(len(shape)))
    )


def call(kernel, outs, in_specs, out_specs, scratch=(), name=None, mib=16, grid=(), far=True):
    return pl.pallas_call(
        kernel,
        out_shape=[pltpu.HBM(s, d) if far else jax.ShapeDtypeStruct(s, d) for s, d in outs],
        grid=grid,
        in_specs=in_specs,
        out_specs=out_specs,
        scratch_shapes=list(scratch),
        compiler_params=pltpu.CompilerParams(vmem_limit_bytes=mib * MIB),
        name=name,
    )


def far(*values):
    return tuple(pltpu.with_memory_space_constraint(v, pltpu.HBM) for v in values)


def swapped(value):
    return lax.ppermute(value, "group", [(0, 1), (1, 0)])


def exchanged(value):
    return lax.all_to_all(value, "dom", split_axis=0, concat_axis=0, tiled=True)


def local(
    nodes,
    edges,
    node_cotangent,
    edge_cotangent,
    senders,
    receivers,
    send_rows,
    edge_in,
    edge_out,
    edge_gain,
    node_in,
    node_out,
    node_gain,
):
    x = nodes[0]
    ed = edges[0]
    ncot = node_cotangent[0]
    ecot = edge_cotangent[0]
    n, w = x.shape
    e = ed.shape[0]
    domains, slots = send_rows.shape[1:]
    h = domains * slots
    half = w // 2
    me = lax.axis_index("group").astype(jnp.int32).reshape(1)
    egain = edge_gain.reshape(1, w)
    ngain = node_gain.reshape(1, w)
    vm = pltpu.VMEM
    dma = pltpu.SemaphoreType.DMA

    (outgoing,) = call(
        outgoing_kernel, [((h, w), BF)], [VM, VM], [VM], [vm((w // LANES, h, LANES), F32)], name="outgoing"
    )(send_rows[0].T, *far(x))
    arrived = exchanged(outgoing.reshape(domains, slots, w)).reshape(h, w)
    eb = 512
    (pre,) = call(
        early_kernel,
        [((e, w), F32)],
        [
            along((1, eb), 1),
            along((1, eb), 1),
            along((eb, w), 0),
            whole((n, w)),
            whole((3 * w, w)),
        ],
        [along((eb, w), 0)],
        [vm((w + 2 * n, w), BF)],
        name="early",
        mib=32,
        grid=(e // eb,),
    )(senders, receivers, *far(ed, x, edge_in))

    ret, keep, give, halo, act, epostg, epg, ntotal = call(
        main_kernel,
        [
            ((domains, 2 * slots, half), BF),
            ((domains, 32, half), BF),
            ((domains, 32, half), BF),
            ((h, w), BF),
            ((e, w), BF),
            ((e, w), BF),
            ((e, w), BF),
            ((n, w), F32),
        ],
        [SM] + [VM] * 4 + [ANY] * 9,
        [VM] * 4 + [ANY] * 4,
        [
            vm((h, w), BF),
            vm((w, w), BF),
            vm((e, w), F32),
            vm((4 * w, w), BF),
            vm((4 * w, w), BF),
            vm((n, w), BF),
            vm((n, w), BF),
            vm((e, w), BF),
            vm((e, w), BF),
            vm((e, w), BF),
            vm((e, w), BF),
            vm((n, w), F32),
            vm((e, LANES), jnp.int32),
            vm((e, LANES), jnp.int32),
            vm((e, w), F32),
            vm((e, LANES), F32),
            vm((n, w), BF),
            vm((n, w), BF),
            vm((n, w), BF),
            vm((n, w), BF),
            vm((n, w), BF),
            vm((8, w), F32),
            vm((8, w), F32),
            vm((domains, 32, w), F32),
            dma((8,)),
            dma((e // eb,)),
            dma((4, e // eb)),
        ],
        name="main",
        mib=54,
    )(
        me, senders, receivers, egain, ngain,
        arrived, edge_in, pre, edge_out, x, node_in, node_out, ncot, ecot,
    )
    share = ((domains, 32, half), BF)
    part = along((domains // 4, 32, half), 0)
    (grad_edges,) = call(
        grad_edges_kernel,
        [((e, w), BF)],
        [along((eb, w), 0), along((eb, w), 0), whole((w, w))],
        [along((eb, w), 0)],
        [vm((w, w), BF)],
        name="grad_edges",
        grid=(e // eb,),
    )(*far(epg, ecot, edge_in))
    got, grad_edges = lax.optimization_barrier((swapped(give), grad_edges))
    (joined,) = call(
        join_kernel,
        [((domains, 48, half), BF)],
        [along((domains // 4, 16, half), 0), part, part],
        [along((domains // 4, 48, half), 0)],
        name="join",
        grid=(4,),
    )(*far(ret, keep), got)
    joined, epg = lax.optimization_barrier((joined, epg))
    first = exchanged(joined)
    keep2, give2, sums = call(
        edge_weights_kernel,
        [share, share, ((2 * n, w), BF)],
        [SM] + [VM] * 2 + [ANY] * 7,
        [VM, VM, ANY],
        [
            vm((e, w), BF),
            vm((e, w), BF),
            vm((n, w), BF),
            vm((h, w), BF),
            vm((h, w), BF),
            vm((e, w), BF),
            vm((e, w), BF),
            vm((2 * n, w), BF),
            vm((domains, 32, w), F32),
            dma((7,)),
            dma,
        ],
        name="edge_weights",
        mib=44,
    )(me, senders, receivers, *far(epg, ed, x, arrived, halo, act, epostg))
    nb = 256
    (total,) = call(
        local_sums_kernel,
        [((n, w), F32)],
        [
            along((nb, w), 0),
            along((nb, w), 0, n // nb),
            along((nb, w), 0),
            pl.BlockSpec((w, w), lambda i: (1, 0)),
            pl.BlockSpec((w, w), lambda i: (2, 0)),
        ],
        [along((nb, w), 0)],
        [vm((2 * w, w), BF)],
        name="local_sums",
        grid=(n // nb,),
    )(*far(sums, sums, ntotal, edge_in, edge_in))
    got2, total = lax.optimization_barrier((swapped(give2), total))
    (joined2,) = call(add_kernel, [share], [part, part], [part], name="add", grid=(4,))(
        *far(keep2), got2
    )
    joined2, first = lax.optimization_barrier((joined2, first))
    second = exchanged(joined2)
    (grad_nodes,) = call(
        grad_nodes_kernel,
        [((n, w), BF)],
        [whole((1, h)), whole((domains, 2 * slots, half)), along((nb, w), 0)],
        [along((nb, w), 0)],
        [vm((h, w), BF)],
        name="grad_nodes",
        grid=(n // nb,),
    )(send_rows.reshape(1, h), first, *far(total))
    (node_sum,) = call(
        sum_kernel,
        [((32, half), BF)],
        [along((domains, 16, half), 1, 1)],
        [along((16, half), 0)],
        name="node_sum",
        grid=(2,),
    )(first)
    g_nin, g_nout, gains = call(
        node_outputs_kernel,
        [((16, w), F32), ((8, w), F32), ((8, LANES), F32)],
        [SM, VM, VM],
        [VM] * 3,
        name="node_outputs",
    )(me, *far(node_sum), swapped(node_sum))
    (edge_sum,) = call(
        sum_kernel,
        [((32, half), BF)],
        [along((domains, 16, half), 1)],
        [along((16, half), 0)],
        name="edge_sum",
        grid=(2,),
    )(second)
    g_ein, g_eout = call(
        edge_outputs_kernel,
        [((24, w), F32), ((8, w), F32)],
        [SM, VM, VM],
        [VM] * 2,
        name="edge_outputs",
    )(me, *far(edge_sum), swapped(edge_sum))
    return (
        grad_edges[None],
        grad_nodes[None],
        g_ein,
        g_eout,
        g_nin,
        g_nout,
        gains[0, 0:8],
        gains[0, 8:16],
    )


def solution(mesh):
    split = P("group", "dom", None)
    placed = (split,) * 4 + (P("group", "dom"),) * 2 + (split,) + (P(),) * 6
    return jax.shard_map(
        local,
        mesh=mesh,
        in_specs=placed,
        out_specs=(split,) * 2 + (P("dom", None),) * 4 + (P("dom"),) * 2,
        check_vma=False,
    )
```

```python
import functools

import jax
import jax.numpy as jnp
from jax import lax
from jax.experimental import pallas as pl
from jax.experimental.pallas import tpu as pltpu
from jax.sharding import PartitionSpec as P

BF = jnp.bfloat16
F32 = jnp.float32
LANES = 128
MIB = 1024 * 1024
NEAR = True


def dot(a, b):
    return jnp.dot(a, b, preferred_element_type=F32)


def dot_nt(a, b):
    return lax.dot_general(a, b, (((1,), (1,)), ((), ())), preferred_element_type=F32)


def dot_tn(a, b):
    return lax.dot_general(a, b, (((0,), (0,)), ((), ())), preferred_element_type=F32)


def spread(ids):
    return jnp.broadcast_to(ids, (LANES, ids.shape[1])).T


def pick(spread_ids, count):
    lane = lax.broadcasted_iota(jnp.int32, spread_ids.shape, 1)
    from_lane = (spread_ids - lane).astype(jnp.int16)
    one = jnp.ones(spread_ids.shape, BF)
    tiles = [
        jnp.where(from_lane == jnp.int16(LANES * k), one, jnp.zeros_like(one))
        for k in range(count // LANES)
    ]
    return jnp.concatenate(tiles, axis=1)


def pick_t(ids, first, count):
    row = lax.broadcasted_iota(jnp.int32, (count, ids.shape[1]), 0) + first
    return jnp.where(row == ids, 1.0, 0.0).astype(BF)


def swish_both(pre):
    gate = jax.nn.sigmoid(pre)
    return pre * gate, gate * (1.0 + pre * (1.0 - gate))


def normalize(hidden):
    centre = hidden - jnp.mean(hidden, axis=-1, keepdims=True)
    inverse = lax.rsqrt(jnp.mean(centre * centre, axis=-1, keepdims=True) + 1e-05)
    return centre * inverse, inverse


def norm_back(upstream, gain, normed, inverse):
    scaled = upstream * gain
    return inverse * (
        scaled
        - jnp.mean(scaled, axis=-1, keepdims=True)
        - normed * jnp.mean(scaled * normed, axis=-1, keepdims=True)
    )


def fold(value):
    return jnp.sum(value.reshape(value.shape[0] // 8, 8, value.shape[1]), axis=0)


def outgoing_kernel(list_ref, nodes_ref, out_ref, rows_ref):
    slots, domains = list_ref.shape
    ids = jnp.concatenate([spread(list_ref[s : s + 1, :]) for s in range(slots)], axis=0)
    rows = dot(pick(ids, nodes_ref.shape[0]), nodes_ref[...])
    for s in range(slots):
        for k in range(rows_ref.shape[0]):
            rows_ref[k, pl.ds(s, domains, stride=slots), :] = rows[
                s * domains : (s + 1) * domains, k * LANES : (k + 1) * LANES
            ]
    for k in range(rows_ref.shape[0]):
        out_ref[:, k * LANES : (k + 1) * LANES] = rows_ref[k].astype(BF)


def early_kernel(send_ref, recv_ref, edges_ref, nodes_ref, ein_ref, out_ref, table):
    n, w = nodes_ref.shape

    @pl.when(pl.program_id(0) == 0)
    def _():
        table[0:w, :] = ein_ref[0:w, :]
        table[w : w + n, :] = dot(nodes_ref[...], ein_ref[w : 2 * w, :]).astype(BF)
        table[w + n : w + 2 * n, :] = dot(nodes_ref[...], ein_ref[2 * w : 3 * w, :]).astype(BF)

    left = jnp.concatenate(
        [edges_ref[...], pick(spread(send_ref[...]), n), pick(spread(recv_ref[...]), n)], axis=1
    )
    out_ref[...] = dot(left, table[...])


def gain_rows(edge_gain, node_gain, domains, width):
    per = edge_gain.shape[1] // domains
    shape = (domains, edge_gain.shape[1])
    own = lax.broadcasted_iota(jnp.int32, shape, 1) // per == lax.broadcasted_iota(
        jnp.int32, shape, 0
    )
    col = lax.broadcasted_iota(jnp.int32, (edge_gain.shape[1], width), 0) % per
    lane = lax.broadcasted_iota(jnp.int32, (edge_gain.shape[1], width), 1)
    total = 0.0
    for k, gain in enumerate((edge_gain, node_gain)):
        mine = jnp.where(own, jnp.broadcast_to(gain, shape), 0.0).astype(BF)
        place = jnp.where(lane == col + per * k, 1.0, 0.0).astype(BF)
        total = total + dot(mine, place)
    return total


def main_kernel(
    g_ref, send_ref, recv_ref, egain_ref, ngain_ref, arrived_ref,
    ein_hbm, pre_hbm, eout_hbm, nodes_hbm, nin_hbm, nout_hbm, ncot_hbm, ecot_hbm,
    ret_ref, keep_ref, give_ref, halo_ref,
    act_hbm, epostg_hbm, epg_hbm, ntotal_hbm,
    weight, hat, eout, nodes, nin, nout, ncot, ecot,
    act_ref, epostg_ref, epg_ref, ntotal_ref,
    slope, inv, gath, nact, npostg, nprg, gg, eacc, nacc,
    in_sem, pre_sem, out_sem,
):
    n, w = nodes.shape
    e = hat.shape[0]
    h = arrived_ref.shape[0]
    half = w // 2
    domains = ret_ref.shape[0]
    eb = 512
    blocks = e // eb
    loads = [
        pltpu.make_async_copy(source, target, in_sem.at[k])
        for k, (source, target) in enumerate(
            (
                (ein_hbm.at[pl.ds(w, w), :], weight),
                (eout_hbm, eout),
                (nodes_hbm, nodes),
                (nin_hbm, nin),
                (nout_hbm, nout),
                (ncot_hbm, ncot),
                (ecot_hbm, ecot),
            )
        )
    ]

    def rows(b):
        return slice(b * eb, (b + 1) * eb)

    pre_loads = [
        pltpu.make_async_copy(pre_hbm.at[rows(b), :], hat.at[rows(b), :], pre_sem.at[b])
        for b in range(blocks)
    ]
    stores = []

    def store(source, target, k, b):
        copy = pltpu.make_async_copy(
            source.at[rows(b), :], target.at[rows(b), :], out_sem.at[k, b]
        )
        copy.start()
        stores.append(copy)

    loads[0].start()
    pre_loads[0].start()
    loads[1].start()
    for load in pre_loads[1:] + loads[2:]:
        load.start()
    egain = egain_ref[...]
    ngain = ngain_ref[...]
    nacc[...] = jnp.zeros_like(nacc)
    eacc[...] = jnp.zeros_like(eacc)
    loads[0].wait()
    far_table = dot(arrived_ref[...], weight[...]).astype(BF)
    gg[0:h, :] = far_table
    loads[1].wait()

    def far_part(b):
        return dot(pick(spread(send_ref[:, rows(b)]) - n, h), gg[0:h, :])

    def edge_act(b, far_pre):
        pre_loads[b].wait()
        act, slp = swish_both(hat[rows(b), :] + far_pre)
        act = act.astype(BF)
        act_ref[rows(b), :] = act
        store(act_ref, act_hbm, 0, b)
        slope[rows(b), :] = slp
        return act

    def edge_norm(b, post):
        normed, inverse = normalize(post)
        hat[rows(b), :] = normed
        inv[rows(b), :] = jnp.broadcast_to(inverse, (eb, LANES))
        epostg_ref[rows(b), :] = (normed * egain).astype(BF)

    pre, act, post = {}, {}, {}
    for t in range(blocks + 3):
        if t < blocks:
            pre[t] = far_part(t)
        if 0 <= t - 2 < blocks:
            post[t - 2] = dot(act.pop(t - 2), eout[...])
        if 0 <= t - 1 < blocks:
            act[t - 1] = edge_act(t - 1, pre.pop(t - 1))
        if 0 <= t - 3 < blocks:
            edge_norm(t - 3, post.pop(t - 3))
    for load in loads[2:6]:
        load.wait()

    def node_gather(b):
        gathered = dot(pick_t(recv_ref[...], b * eb, eb), epostg_ref[...]).astype(BF)
        gath[rows(b), :] = gathered
        return dot(jnp.concatenate([nodes[rows(b), :], gathered], axis=1), nin[...])

    def node_act(b, value):
        act, slp = swish_both(value)
        act = act.astype(BF)
        nact[rows(b), :] = act
        return act, slp

    def node_back(b, value):
        normed, inverse = normalize(value)
        upstream = ncot[rows(b), :].astype(F32)
        nacc[...] += fold(upstream * normed)
        postg = norm_back(upstream, ngain, normed, inverse).astype(BF)
        npostg[rows(b), :] = postg
        return postg

    def node_turn(b, value, slp):
        preg = (value * slp).astype(BF)
        nprg[rows(b), :] = preg
        return preg

    def node_end(b, preg):
        back = dot_nt(preg, nin[...])
        ntotal_ref[rows(b), :] = ncot[rows(b), :].astype(F32) + back[:, :w]
        store(ntotal_ref, ntotal_hbm, 3, b)
        gg[rows(b), :] = back[:, w:].astype(BF)

    pre0 = node_gather(0)
    pre1 = node_gather(1)
    act0, slope0 = node_act(0, pre0)
    post0 = dot(act0, nout[...])
    act1, slope1 = node_act(1, pre1)
    post1 = dot(act1, nout[...])
    postg0 = node_back(0, post0)
    turn0 = dot_nt(postg0, nout[...])
    postg1 = node_back(1, post1)
    turn1 = dot_nt(postg1, nout[...])
    preg0 = node_turn(0, turn0, slope0)
    preg1 = node_turn(1, turn1, slope1)
    node_end(0, preg0)
    node_end(1, preg1)
    loads[6].wait()

    def edge_gather(b):
        return dot(pick(spread(recv_ref[:, rows(b)]), n), gg[...])

    def edge_back(b, value):
        upstream = ecot[rows(b), :].astype(F32) + value
        normed = hat[rows(b), :]
        eacc[...] += fold(upstream * normed)
        postg = norm_back(upstream, egain, normed, inv[rows(b), 0:1]).astype(BF)
        epostg_ref[rows(b), :] = postg
        store(epostg_ref, epostg_hbm, 1, b)
        return postg

    def edge_end(b, value):
        epg_ref[rows(b), :] = (value * slope[rows(b), :]).astype(BF)
        store(epg_ref, epg_hbm, 2, b)

    pre, act, post = {}, {}, {}
    for t in range(blocks + 3):
        if t < blocks:
            pre[t] = edge_gather(t)
        if 0 <= t - 2 < blocks:
            post[t - 2] = dot_nt(act.pop(t - 2), eout[...])
        if 0 <= t - 1 < blocks:
            act[t - 1] = edge_back(t - 1, pre.pop(t - 1))
        if 0 <= t - 3 < blocks:
            edge_end(t - 3, post.pop(t - 3))
    halo = dot(pick_t(send_ref[...], n, h), epg_ref[...]).astype(BF)
    halo_ref[...] = halo
    ret = dot_nt(halo, weight[...])
    per = h // domains
    ret_ref[:, 0:per, :] = ret[:, :half].reshape(domains, per, half).astype(BF)
    ret_ref[:, per : 2 * per, :] = ret[:, half:].reshape(domains, per, half).astype(BF)

    gains = gain_rows(
        jnp.sum(eacc[...], axis=0, keepdims=True),
        jnp.sum(nacc[...], axis=0, keepdims=True),
        domains,
        half,
    )
    gains = jnp.broadcast_to(gains[:, None, :], (domains, 8, half))
    mine = g_ref[0]
    for out_ref, which in ((keep_ref, mine), (give_ref, 1 - mine)):
        cols = pl.ds(pl.multiple_of(which * half, half), half)
        pg = nprg[:, cols]
        for k, source in enumerate((nodes, gath)):
            grad = dot_tn(source[...], pg).reshape(domains // 2, 16, half)
            out_ref[k * (domains // 2) : (k + 1) * (domains // 2), 0:16, :] = grad.astype(BF)
        last = dot_tn(nact[...], npostg[:, cols]).reshape(domains, 8, half)
        out_ref[:, 16:32, :] = jnp.concatenate([last, gains], axis=1).astype(BF)
    for copy in stores:
        copy.wait()


def grad_edges_kernel(epg_ref, ecot_ref, ein_ref, *refs):
    out_ref = refs[-1]
    out_ref[...] = (ecot_ref[...].astype(F32) + dot_nt(epg_ref[...], ein_ref[...])).astype(BF)


def edge_weights_kernel(
    g_ref, send_ref, recv_ref,
    epg_hbm, edges_hbm, nodes_hbm, arrived_hbm, halo_hbm, act_hbm, epostg_hbm,
    keep_ref, give_ref, sums_hbm,
    epg, edges, nodes, arrived, halo, act, epostg, sums, share, in_sem, out_sem,
):
    n, w = nodes.shape
    half = w // 2
    domains = share.shape[0]
    nb = 512
    loads = [
        pltpu.make_async_copy(source, target, in_sem.at[k])
        for k, (source, target) in enumerate(
            (
                (epg_hbm, epg),
                (edges_hbm, edges),
                (nodes_hbm, nodes),
                (arrived_hbm, arrived),
                (halo_hbm, halo),
                (act_hbm, act),
                (epostg_hbm, epostg),
            )
        )
    ]
    for load in loads:
        load.start()
    loads[0].wait()

    def node_sums(b, carry):
        first = pl.multiple_of(b * nb, nb)
        later = pl.multiple_of(n + b * nb, nb)
        sums[pl.ds(first, nb), :] = dot(pick_t(send_ref[...], first, nb), epg[...]).astype(BF)
        sums[pl.ds(later, nb), :] = dot(pick_t(recv_ref[...], first, nb), epg[...]).astype(BF)
        return carry

    lax.fori_loop(0, n // nb, node_sums, 0)
    out = pltpu.make_async_copy(sums, sums_hbm, out_sem)
    out.start()
    for load in loads[1:]:
        load.wait()
    per = 3 * w // domains // 8

    def put(k, part):
        for j in range(w // 8):
            t = k * (w // 8) + j
            share[t // per, (t % per) * 8 : (t % per) * 8 + 8, :] = part[j * 8 : j * 8 + 8, :]

    put(0, dot_tn(edges[...], epg[...]))
    both = dot_tn(nodes[...], jnp.concatenate([sums[0:n, :], sums[n:, :]], axis=1))
    put(1, both[:, :w] + dot_tn(arrived[...], halo[...]))
    put(2, both[:, w:])
    share[:, 24:32, :] = dot_tn(act[...], epostg[...]).reshape(domains, 8, w)
    mine = g_ref[0]
    keep_ref[...] = share[:, :, pl.ds(pl.multiple_of(mine * half, half), half)].astype(BF)
    give_ref[...] = share[:, :, pl.ds(pl.multiple_of((1 - mine) * half, half), half)].astype(BF)
    out.wait()


def local_sums_kernel(send_ref, recv_ref, ntotal_ref, ws_ref, wr_ref, out_ref):
    out_ref[...] = (
        ntotal_ref[...] + dot_nt(send_ref[...], ws_ref[...]) + dot_nt(recv_ref[...], wr_ref[...])
    )


def grad_nodes_kernel(list_ref, first_ref, total_ref, out_ref, back):
    domains, rows, half = first_ref.shape
    slots = rows // 2
    block = total_ref.shape[0]

    @pl.when(pl.program_id(0) == 0)
    def _():
        for k in range(2):
            part = first_ref[:, k * slots : (k + 1) * slots, :].astype(F32)
            back[:, k * half : (k + 1) * half] = part.reshape(domains * slots, half).astype(BF)

    sel = pick_t(list_ref[...], pl.program_id(0) * block, block)
    out_ref[...] = (total_ref[...] + dot(sel, back[...])).astype(BF)


def sum_kernel(all_ref, out_ref):
    out_ref[...] = jnp.sum(all_ref[...].astype(F32), axis=0).astype(BF)


def edge_outputs_kernel(g_ref, mine_ref, got_ref, ein_ref, eout_ref):
    half = mine_ref.shape[1]
    low = g_ref[0] == 0
    mine = mine_ref[...].astype(F32)
    got = got_ref[...].astype(F32)
    for k, value in enumerate((jnp.where(low, mine, got), jnp.where(low, got, mine))):
        cols = slice(k * half, (k + 1) * half)
        ein_ref[:, cols] = value[0:24, :]
        eout_ref[:, cols] = value[24:32, :]


def node_outputs_kernel(g_ref, mine_ref, got_ref, nin_ref, nout_ref, gains_ref):
    half = mine_ref.shape[1]
    low = g_ref[0] == 0
    mine = mine_ref[...].astype(F32)
    got = got_ref[...].astype(F32)
    for k, value in enumerate((jnp.where(low, mine, got), jnp.where(low, got, mine))):
        cols = slice(k * half, (k + 1) * half)
        nin_ref[:, cols] = value[0:16, :]
        nout_ref[:, cols] = value[16:24, :]
    gains_ref[...] = mine[24:32, 0:LANES]


def join_kernel(ret_ref, keep_ref, got_ref, out_ref):
    out_ref[:, 0:16, :] = ret_ref[...]
    out_ref[:, 16:48, :] = (keep_ref[...].astype(F32) + got_ref[...].astype(F32)).astype(BF)


def add_kernel(keep_ref, got_ref, out_ref):
    out_ref[...] = (keep_ref[...].astype(F32) + got_ref[...].astype(F32)).astype(BF)


VM = pl.BlockSpec(memory_space=pltpu.VMEM)
SM = pl.BlockSpec(memory_space=pltpu.SMEM)
ANY = pl.BlockSpec(memory_space=pltpu.HBM)


def whole(shape):
    return pl.BlockSpec(shape, lambda i: (0,) * len(shape))


def along(shape, dim, first=0):
    return pl.BlockSpec(
        shape, lambda i: tuple(first + i if d == dim else 0 for d in range(len(shape)))
    )


def call(kernel, outs, in_specs, out_specs, scratch=(), name=None, mib=16, grid=(), alias=None):
    return pl.pallas_call(
        kernel,
        out_shape=[
            jax.ShapeDtypeStruct(*o[:2]) if o[2:] == (NEAR,) else pltpu.HBM(*o) for o in outs
        ],
        grid=grid,
        in_specs=in_specs,
        out_specs=out_specs,
        scratch_shapes=list(scratch),
        compiler_params=pltpu.CompilerParams(vmem_limit_bytes=mib * MIB),
        input_output_aliases=alias or {},
        name=name,
    )


def far(*values):
    return tuple(pltpu.with_memory_space_constraint(v, pltpu.HBM) for v in values)


def swapped(value):
    return lax.ppermute(value, "group", [(0, 1), (1, 0)])


def exchanged(value):
    return lax.all_to_all(value, "dom", split_axis=0, concat_axis=0, tiled=True)


def local(
    nodes,
    edges,
    node_cotangent,
    edge_cotangent,
    senders,
    receivers,
    send_rows,
    edge_in,
    edge_out,
    edge_gain,
    node_in,
    node_out,
    node_gain,
):
    x = nodes[0]
    ed = edges[0]
    ncot = node_cotangent[0]
    ecot = edge_cotangent[0]
    n, w = x.shape
    e = ed.shape[0]
    domains, slots = send_rows.shape[1:]
    h = domains * slots
    half = w // 2
    me = lax.axis_index("group").astype(jnp.int32).reshape(1)
    egain = edge_gain.reshape(1, w)
    ngain = node_gain.reshape(1, w)
    vm = pltpu.VMEM
    dma = pltpu.SemaphoreType.DMA

    (outgoing,) = call(
        outgoing_kernel, [((h, w), BF)], [VM, VM], [VM], [vm((w // LANES, h, LANES), F32)], name="outgoing"
    )(send_rows[0].T, *far(x))
    arrived = exchanged(outgoing.reshape(domains, slots, w)).reshape(h, w)
    eb = 512
    (pre,) = call(
        early_kernel,
        [((e, w), F32)],
        [
            along((1, eb), 1),
            along((1, eb), 1),
            along((eb, w), 0),
            whole((n, w)),
            whole((3 * w, w)),
        ],
        [along((eb, w), 0)],
        [vm((w + 2 * n, w), BF)],
        name="early",
        mib=32,
        grid=(e // eb,),
    )(senders, receivers, *far(ed, x, edge_in))

    ret, keep, give, halo, act, epostg, epg, ntotal = call(
        main_kernel,
        [
            ((domains, 2 * slots, half), BF, NEAR),
            ((domains, 32, half), BF, NEAR),
            ((domains, 32, half), BF, NEAR),
            ((h, w), BF),
            ((e, w), BF),
            ((e, w), BF),
            ((e, w), BF),
            ((n, w), F32),
        ],
        [SM] + [VM] * 5 + [ANY] * 8,
        [VM] * 4 + [ANY] * 4,
        [
            vm((w, w), BF),
            vm((e, w), F32),
            vm((w, w), BF),
            vm((n, w), BF),
            vm((2 * w, w), BF),
            vm((w, w), BF),
            vm((n, w), BF),
            vm((e, w), BF),
            vm((e, w), BF),
            vm((e, w), BF),
            vm((e, w), BF),
            vm((n, w), F32),
            vm((e, w), F32),
            vm((e, LANES), F32),
            vm((n, w), BF),
            vm((n, w), BF),
            vm((n, w), BF),
            vm((n, w), BF),
            vm((n, w), BF),
            vm((8, w), F32),
            vm((8, w), F32),
            dma((7,)),
            dma((e // eb,)),
            dma((4, e // eb)),
        ],
        name="main",
        mib=48,
    )(
        me, senders, receivers, egain, ngain, arrived,
        *far(edge_in, pre, edge_out, x, node_in, node_out, ncot, ecot),
    )
    share = ((domains, 32, half), BF)
    part = along((domains // 4, 32, half), 0)

    def grad_edges_half(k, *before):
        steps = e // eb // 2
        (value,) = call(
            grad_edges_kernel,
            [((e, w), BF)],
            [along((eb, w), 0, k * steps)] * 2 + [whole((w, w))] + [ANY] * len(before),
            [along((eb, w), 0, k * steps)],
            name="grad_edges",
            grid=(steps,),
            alias={3: 0} if before else None,
        )(*far(epg, ecot, edge_in), *before)
        return value

    got, grad_edges = lax.optimization_barrier((swapped(give), grad_edges_half(0)))
    (joined,) = call(
        join_kernel,
        [((domains, 48, half), BF)],
        [along((domains // 4, 16, half), 0), part, part],
        [along((domains // 4, 48, half), 0)],
        name="join",
        grid=(4,),
    )(ret, keep, got)
    joined, epg = lax.optimization_barrier((joined, epg))
    first = exchanged(joined)
    keep2, give2, sums = call(
        edge_weights_kernel,
        [share + (NEAR,), share + (NEAR,), ((2 * n, w), BF)],
        [SM] + [VM] * 2 + [ANY] * 7,
        [VM, VM, ANY],
        [
            vm((e, w), BF),
            vm((e, w), BF),
            vm((n, w), BF),
            vm((h, w), BF),
            vm((h, w), BF),
            vm((e, w), BF),
            vm((e, w), BF),
            vm((2 * n, w), BF),
            vm((domains, 32, w), F32),
            dma((7,)),
            dma,
        ],
        name="edge_weights",
        mib=44,
    )(me, senders, receivers, *far(epg, ed, x, arrived, halo, act, epostg))
    got2, grad_edges = lax.optimization_barrier((swapped(give2), grad_edges_half(1, grad_edges)))
    (joined2,) = call(add_kernel, [share], [part, part], [part], name="add", grid=(4,))(
        keep2, got2
    )
    joined2, first, sums = lax.optimization_barrier((joined2, first, sums))
    second = exchanged(joined2)
    nb = 512
    (total,) = call(
        local_sums_kernel,
        [((n, w), F32)],
        [
            along((nb, w), 0),
            along((nb, w), 0, n // nb),
            along((nb, w), 0),
            pl.BlockSpec((w, w), lambda i: (1, 0)),
            pl.BlockSpec((w, w), lambda i: (2, 0)),
        ],
        [along((nb, w), 0)],
        name="local_sums",
        grid=(n // nb,),
    )(*far(sums, sums, ntotal, edge_in, edge_in))
    (grad_nodes,) = call(
        grad_nodes_kernel,
        [((n, w), BF)],
        [whole((1, h)), whole((domains, 2 * slots, half)), along((nb, w), 0)],
        [along((nb, w), 0)],
        [vm((h, w), BF)],
        name="grad_nodes",
        grid=(n // nb,),
    )(send_rows.reshape(1, h), first, *far(total))
    (node_sum,) = call(
        sum_kernel,
        [((32, half), BF, NEAR)],
        [along((domains, 16, half), 1, 1)],
        [along((16, half), 0)],
        name="node_sum",
        grid=(2,),
    )(first)
    g_nin, g_nout, gains = call(
        node_outputs_kernel,
        [((16, w), F32), ((8, w), F32), ((8, LANES), F32)],
        [SM, VM, VM],
        [VM] * 3,
        name="node_outputs",
    )(me, node_sum, swapped(node_sum))
    (edge_sum,) = call(
        sum_kernel,
        [((32, half), BF, NEAR)],
        [along((domains, 16, half), 1)],
        [along((16, half), 0)],
        name="edge_sum",
        grid=(2,),
    )(second)
    g_ein, g_eout = call(
        edge_outputs_kernel,
        [((24, w), F32), ((8, w), F32)],
        [SM, VM, VM],
        [VM] * 2,
        name="edge_outputs",
    )(me, edge_sum, swapped(edge_sum))
    return (
        grad_edges[None],
        grad_nodes[None],
        g_ein,
        g_eout,
        g_nin,
        g_nout,
        gains[0, 0:8],
        gains[0, 8:16],
    )


def solution(mesh):
    split = P("group", "dom", None)
    placed = (split,) * 4 + (P("group", "dom"),) * 2 + (split,) + (P(),) * 6
    return jax.shard_map(
        local,
        mesh=mesh,
        in_specs=placed,
        out_specs=(split,) * 2 + (P("dom", None),) * 4 + (P("dom"),) * 2,
        check_vma=False,
    )
```

```python
import functools

import jax
import jax.numpy as jnp
from jax import lax
from jax.experimental import pallas as pl
from jax.experimental.pallas import tpu as pltpu
from jax.sharding import PartitionSpec as P

BF = jnp.bfloat16
F32 = jnp.float32
LANES = 128
MIB = 1024 * 1024
NEAR = True


def dot(a, b):
    return jnp.dot(a, b, preferred_element_type=F32)


def dot_nt(a, b):
    return lax.dot_general(a, b, (((1,), (1,)), ((), ())), preferred_element_type=F32)


def dot_tn(a, b):
    return lax.dot_general(a, b, (((0,), (0,)), ((), ())), preferred_element_type=F32)


def spread(ids):
    return jnp.broadcast_to(ids, (LANES, ids.shape[1])).T


def pick(spread_ids, count):
    lane = lax.broadcasted_iota(jnp.int32, spread_ids.shape, 1)
    from_lane = (spread_ids - lane).astype(jnp.int16)
    one = jnp.ones(spread_ids.shape, BF)
    tiles = [
        jnp.where(from_lane == jnp.int16(LANES * k), one, jnp.zeros_like(one))
        for k in range(count // LANES)
    ]
    return jnp.concatenate(tiles, axis=1)


def pick_t(ids, first, count):
    row = lax.broadcasted_iota(jnp.int32, (count, ids.shape[1]), 0) + first
    return jnp.where(row == ids, 1.0, 0.0).astype(BF)


def swish_both(pre):
    gate = jax.nn.sigmoid(pre)
    return pre * gate, gate * (1.0 + pre * (1.0 - gate))


def normalize(hidden):
    centre = hidden - jnp.mean(hidden, axis=-1, keepdims=True)
    inverse = lax.rsqrt(jnp.mean(centre * centre, axis=-1, keepdims=True) + 1e-05)
    return centre * inverse, inverse


def norm_back(upstream, gain, normed, inverse):
    scaled = upstream * gain
    return inverse * (
        scaled
        - jnp.mean(scaled, axis=-1, keepdims=True)
        - normed * jnp.mean(scaled * normed, axis=-1, keepdims=True)
    )


def fold(value):
    return jnp.sum(value.reshape(value.shape[0] // 8, 8, value.shape[1]), axis=0)


def outgoing_kernel(list_ref, nodes_ref, out_ref, rows_ref):
    slots, domains = list_ref.shape
    ids = jnp.concatenate([spread(list_ref[s : s + 1, :]) for s in range(slots)], axis=0)
    rows = dot(pick(ids, nodes_ref.shape[0]), nodes_ref[...])
    for s in range(slots):
        for k in range(rows_ref.shape[0]):
            rows_ref[k, pl.ds(s, domains, stride=slots), :] = rows[
                s * domains : (s + 1) * domains, k * LANES : (k + 1) * LANES
            ]
    for k in range(rows_ref.shape[0]):
        out_ref[:, k * LANES : (k + 1) * LANES] = rows_ref[k].astype(BF)


def early_kernel(send_ref, recv_ref, edges_ref, nodes_ref, ein_ref, out_ref, table):
    n, w = nodes_ref.shape

    @pl.when(pl.program_id(0) == 0)
    def _():
        table[0:w, :] = ein_ref[0:w, :]
        table[w : w + n, :] = dot(nodes_ref[...], ein_ref[w : 2 * w, :]).astype(BF)
        table[w + n : w + 2 * n, :] = dot(nodes_ref[...], ein_ref[2 * w : 3 * w, :]).astype(BF)

    left = jnp.concatenate(
        [edges_ref[...], pick(spread(send_ref[...]), n), pick(spread(recv_ref[...]), n)], axis=1
    )
    out_ref[...] = dot(left, table[...])


def gain_rows(edge_gain, node_gain, domains, width):
    per = edge_gain.shape[1] // domains
    shape = (domains, edge_gain.shape[1])
    own = lax.broadcasted_iota(jnp.int32, shape, 1) // per == lax.broadcasted_iota(
        jnp.int32, shape, 0
    )
    col = lax.broadcasted_iota(jnp.int32, (edge_gain.shape[1], width), 0) % per
    lane = lax.broadcasted_iota(jnp.int32, (edge_gain.shape[1], width), 1)
    total = 0.0
    for k, gain in enumerate((edge_gain, node_gain)):
        mine = jnp.where(own, jnp.broadcast_to(gain, shape), 0.0).astype(BF)
        place = jnp.where(lane == col + per * k, 1.0, 0.0).astype(BF)
        total = total + dot(mine, place)
    return total


def forward_kernel(
    g_ref, send_ref, recv_ref, egain_ref, ngain_ref, arrived_ref,
    ein_hbm, pre_hbm, eout_hbm, nodes_hbm, nin_hbm, nout_hbm, ncot_hbm,
    keep_ref, give_ref, hat, slope, inv, gg, nacc_ref,
    act_hbm, nprg_hbm,
    weight, eout, nodes, nin, nout, ncot,
    act_ref, upd, gath, nact, npostg, nprg, nacc,
    in_sem, pre_sem, out_sem,
):
    n, w = nodes.shape
    e = hat.shape[0]
    h = arrived_ref.shape[0]
    half = w // 2
    domains = keep_ref.shape[0]
    eb = 512
    blocks = e // eb
    loads = [
        pltpu.make_async_copy(source, target, in_sem.at[k])
        for k, (source, target) in enumerate(
            (
                (ein_hbm.at[pl.ds(w, w), :], weight),
                (eout_hbm, eout),
                (nodes_hbm, nodes),
                (nin_hbm, nin),
                (nout_hbm, nout),
                (ncot_hbm, ncot),
            )
        )
    ]

    def rows(b):
        return slice(b * eb, (b + 1) * eb)

    pre_loads = [
        pltpu.make_async_copy(pre_hbm.at[rows(b), :], hat.at[rows(b), :], pre_sem.at[b])
        for b in range(blocks)
    ]
    stores = []

    def store(source, target, k, b):
        copy = pltpu.make_async_copy(
            source.at[rows(b), :], target.at[rows(b), :], out_sem.at[k, b]
        )
        copy.start()
        stores.append(copy)

    loads[0].start()
    pre_loads[0].start()
    loads[1].start()
    for load in pre_loads[1:] + loads[2:]:
        load.start()
    egain = egain_ref[...]
    ngain = ngain_ref[...]
    nacc[...] = jnp.zeros_like(nacc)
    loads[0].wait()
    far_table = dot(arrived_ref[...], weight[...]).astype(BF)
    gg[0:h, :] = far_table
    loads[1].wait()

    def far_part(b):
        return dot(pick(spread(send_ref[:, rows(b)]) - n, h), gg[0:h, :])

    def edge_act(b, far_pre):
        pre_loads[b].wait()
        act, slp = swish_both(hat[rows(b), :] + far_pre)
        act = act.astype(BF)
        act_ref[rows(b), :] = act
        store(act_ref, act_hbm, 0, b)
        slope[rows(b), :] = slp
        return act

    def edge_norm(b, post):
        normed, inverse = normalize(post)
        hat[rows(b), :] = normed
        inv[rows(b), :] = jnp.broadcast_to(inverse, (eb, LANES))
        upd[rows(b), :] = (normed * egain).astype(BF)

    pre, act, post = {}, {}, {}
    for t in range(blocks + 3):
        if t < blocks:
            pre[t] = far_part(t)
        if 0 <= t - 2 < blocks:
            post[t - 2] = dot(act.pop(t - 2), eout[...])
        if 0 <= t - 1 < blocks:
            act[t - 1] = edge_act(t - 1, pre.pop(t - 1))
        if 0 <= t - 3 < blocks:
            edge_norm(t - 3, post.pop(t - 3))
    for load in loads[2:6]:
        load.wait()

    def node_gather(b):
        gathered = dot(pick_t(recv_ref[...], b * eb, eb), upd[...]).astype(BF)
        gath[rows(b), :] = gathered
        return dot(jnp.concatenate([nodes[rows(b), :], gathered], axis=1), nin[...])

    def node_act(b, value):
        act, slp = swish_both(value)
        act = act.astype(BF)
        nact[rows(b), :] = act
        return act, slp

    def node_back(b, value):
        normed, inverse = normalize(value)
        upstream = ncot[rows(b), :].astype(F32)
        nacc[...] += fold(upstream * normed)
        postg = norm_back(upstream, ngain, normed, inverse).astype(BF)
        npostg[rows(b), :] = postg
        return postg

    def node_turn(b, value, slp):
        preg = (value * slp).astype(BF)
        nprg[rows(b), :] = preg
        store(nprg, nprg_hbm, 1, b)
        return preg

    def node_end(b, preg):
        gg[rows(b), :] = dot_nt(preg, nin[w:, :]).astype(BF)

    pre0 = node_gather(0)
    pre1 = node_gather(1)
    act0, slope0 = node_act(0, pre0)
    post0 = dot(act0, nout[...])
    act1, slope1 = node_act(1, pre1)
    post1 = dot(act1, nout[...])
    postg0 = node_back(0, post0)
    turn0 = dot_nt(postg0, nout[...])
    postg1 = node_back(1, post1)
    turn1 = dot_nt(postg1, nout[...])
    preg0 = node_turn(0, turn0, slope0)
    preg1 = node_turn(1, turn1, slope1)
    node_end(0, preg0)
    node_end(1, preg1)
    nacc_ref[...] = jnp.broadcast_to(jnp.sum(nacc[...], axis=0, keepdims=True), nacc.shape)
    mine = g_ref[0]
    for out_ref, which in ((keep_ref, mine), (give_ref, 1 - mine)):
        cols = pl.ds(pl.multiple_of(which * half, half), half)
        pg = nprg[:, cols]
        for k, source in enumerate((nodes, gath)):
            grad = dot_tn(source[...], pg).reshape(domains // 2, 16, half)
            out_ref[k * (domains // 2) : (k + 1) * (domains // 2), 0:16, :] = grad.astype(BF)
        last = dot_tn(nact[...], npostg[:, cols]).reshape(domains, 8, half)
        out_ref[:, 16:24, :] = last.astype(BF)
    for copy in stores:
        copy.wait()


def backward_kernel(
    send_ref, recv_ref, egain_ref, hat, slope, inv, gg, nacc_ref,
    ecot_hbm, eout_hbm, ein_hbm,
    ret_ref, gains_ref, halo_ref,
    epostg_hbm, epg_hbm,
    ecot, eout, weight, epostg_ref, epg_ref, eacc,
    in_sem, ecot_sem, out_sem,
):
    n, w = gg.shape
    e = hat.shape[0]
    h = halo_ref.shape[0]
    half = w // 2
    domains = ret_ref.shape[0]
    eb = 512
    blocks = e // eb

    def rows(b):
        return slice(b * eb, (b + 1) * eb)

    stores = []

    def store(source, target, k, b):
        copy = pltpu.make_async_copy(
            source.at[rows(b), :], target.at[rows(b), :], out_sem.at[k, b]
        )
        copy.start()
        stores.append(copy)

    loads = [
        pltpu.make_async_copy(ecot_hbm.at[rows(b), :], ecot.at[rows(b), :], ecot_sem.at[b])
        for b in range(blocks)
    ]
    weights = [
        pltpu.make_async_copy(eout_hbm, eout, in_sem.at[0]),
        pltpu.make_async_copy(ein_hbm.at[pl.ds(w, w), :], weight, in_sem.at[1]),
    ]
    for load in (loads[0], weights[0], *loads[1:], weights[1]):
        load.start()
    egain = egain_ref[...]
    eacc[...] = jnp.zeros_like(eacc)

    def edge_gather(b):
        return dot(pick(spread(recv_ref[:, rows(b)]), n), gg[...])

    def edge_back(b, value):
        loads[b].wait()
        upstream = ecot[rows(b), :].astype(F32) + value
        normed = hat[rows(b), :]
        eacc[...] += fold(upstream * normed)
        postg = norm_back(upstream, egain, normed, inv[rows(b), 0:1]).astype(BF)
        epostg_ref[rows(b), :] = postg
        store(epostg_ref, epostg_hbm, 0, b)
        return postg

    def edge_end(b, value):
        epg_ref[rows(b), :] = (value * slope[rows(b), :]).astype(BF)
        store(epg_ref, epg_hbm, 1, b)

    pre, act, post = {}, {}, {}
    for t in range(blocks + 3):
        if t < blocks:
            pre[t] = edge_gather(t)
        if t == 2:
            weights[0].wait()
        if 0 <= t - 2 < blocks:
            post[t - 2] = dot_nt(act.pop(t - 2), eout[...])
        if 0 <= t - 1 < blocks:
            act[t - 1] = edge_back(t - 1, pre.pop(t - 1))
        if 0 <= t - 3 < blocks:
            edge_end(t - 3, post.pop(t - 3))
    halo = dot(pick_t(send_ref[...], n, h), epg_ref[...]).astype(BF)
    halo_ref[...] = halo
    weights[1].wait()
    ret = dot_nt(halo, weight[...])
    per = h // domains
    ret_ref[:, 0:per, :] = ret[:, :half].reshape(domains, per, half).astype(BF)
    ret_ref[:, per : 2 * per, :] = ret[:, half:].reshape(domains, per, half).astype(BF)

    gains = gain_rows(
        jnp.sum(eacc[...], axis=0, keepdims=True),
        nacc_ref[0:1, :],
        domains,
        half,
    )
    gains_ref[...] = jnp.broadcast_to(gains[:, None, :], (domains, 8, half)).astype(BF)
    for copy in stores:
        copy.wait()


def grad_edges_kernel(epg_ref, ecot_ref, ein_ref, out_ref):
    out_ref[...] = (ecot_ref[...].astype(F32) + dot_nt(epg_ref[...], ein_ref[...])).astype(BF)


def edge_weights_kernel(
    g_ref, send_ref, recv_ref,
    epg_hbm, edges_hbm, nodes_hbm, arrived_hbm, halo_hbm, act_hbm, epostg_hbm,
    keep_ref, give_ref, sums_hbm,
    epg, edges, nodes, arrived, halo, act, epostg, sums, share, in_sem, out_sem,
):
    n, w = nodes.shape
    half = w // 2
    domains = share.shape[0]
    nb = 512
    loads = [
        pltpu.make_async_copy(source, target, in_sem.at[k])
        for k, (source, target) in enumerate(
            (
                (epg_hbm, epg),
                (edges_hbm, edges),
                (nodes_hbm, nodes),
                (arrived_hbm, arrived),
                (halo_hbm, halo),
                (act_hbm, act),
                (epostg_hbm, epostg),
            )
        )
    ]
    for load in loads:
        load.start()
    loads[0].wait()

    def node_sums(b, carry):
        first = pl.multiple_of(b * nb, nb)
        later = pl.multiple_of(n + b * nb, nb)
        sums[pl.ds(first, nb), :] = dot(pick_t(send_ref[...], first, nb), epg[...]).astype(BF)
        sums[pl.ds(later, nb), :] = dot(pick_t(recv_ref[...], first, nb), epg[...]).astype(BF)
        return carry

    lax.fori_loop(0, n // nb, node_sums, 0)
    out = pltpu.make_async_copy(sums, sums_hbm, out_sem)
    out.start()
    for load in loads[1:]:
        load.wait()
    per = 3 * w // domains // 8

    def put(k, part):
        for j in range(w // 8):
            t = k * (w // 8) + j
            share[t // per, (t % per) * 8 : (t % per) * 8 + 8, :] = part[j * 8 : j * 8 + 8, :]

    put(0, dot_tn(edges[...], epg[...]))
    both = dot_tn(nodes[...], jnp.concatenate([sums[0:n, :], sums[n:, :]], axis=1))
    put(1, both[:, :w] + dot_tn(arrived[...], halo[...]))
    put(2, both[:, w:])
    share[:, 24:32, :] = dot_tn(act[...], epostg[...]).reshape(domains, 8, w)
    mine = g_ref[0]
    keep_ref[...] = share[:, :, pl.ds(pl.multiple_of(mine * half, half), half)].astype(BF)
    give_ref[...] = share[:, :, pl.ds(pl.multiple_of((1 - mine) * half, half), half)].astype(BF)
    out.wait()


def local_sums_kernel(send_ref, recv_ref, nprg_ref, ncot_ref, ws_ref, wr_ref, nin_ref, out_ref):
    out_ref[...] = (
        ncot_ref[...].astype(F32)
        + dot_nt(send_ref[...], ws_ref[...])
        + dot_nt(recv_ref[...], wr_ref[...])
        + dot_nt(nprg_ref[...], nin_ref[...])
    )


def grad_nodes_kernel(list_ref, first_ref, total_ref, out_ref, back):
    domains, rows, half = first_ref.shape
    slots = rows // 2
    block = total_ref.shape[0]

    @pl.when(pl.program_id(0) == 0)
    def _():
        for k in range(2):
            part = first_ref[:, k * slots : (k + 1) * slots, :].astype(F32)
            back[:, k * half : (k + 1) * half] = part.reshape(domains * slots, half).astype(BF)

    sel = pick_t(list_ref[...], pl.program_id(0) * block, block)
    out_ref[...] = (total_ref[...] + dot(sel, back[...])).astype(BF)


def sum_kernel(all_ref, out_ref):
    out_ref[...] = jnp.sum(all_ref[...].astype(F32), axis=0).astype(BF)


def edge_outputs_kernel(g_ref, mine_ref, got_ref, ein_ref, eout_ref):
    half = mine_ref.shape[1]
    low = g_ref[0] == 0
    mine = mine_ref[...].astype(F32)
    got = got_ref[...].astype(F32)
    for k, value in enumerate((jnp.where(low, mine, got), jnp.where(low, got, mine))):
        cols = slice(k * half, (k + 1) * half)
        ein_ref[:, cols] = value[0:24, :]
        eout_ref[:, cols] = value[24:32, :]


def node_outputs_kernel(g_ref, mine_ref, got_ref, nin_ref, nout_ref, gains_ref):
    half = mine_ref.shape[1]
    low = g_ref[0] == 0
    mine = mine_ref[...].astype(F32)
    got = got_ref[...].astype(F32)
    for k, value in enumerate((jnp.where(low, mine, got), jnp.where(low, got, mine))):
        cols = slice(k * half, (k + 1) * half)
        nin_ref[:, cols] = value[0:16, :]
        nout_ref[:, cols] = value[16:24, :]
    gains_ref[...] = mine[24:32, 0:LANES] + got[24:32, 0:LANES]


def join_kernel(ret_ref, keep_ref, got_ref, gains_ref, out_ref):
    out_ref[:, 0:16, :] = ret_ref[...]
    out_ref[:, 16:40, :] = (keep_ref[...].astype(F32) + got_ref[...].astype(F32)).astype(BF)
    out_ref[:, 40:48, :] = gains_ref[...]


def add_kernel(keep_ref, got_ref, out_ref):
    out_ref[...] = (keep_ref[...].astype(F32) + got_ref[...].astype(F32)).astype(BF)


VM = pl.BlockSpec(memory_space=pltpu.VMEM)
SM = pl.BlockSpec(memory_space=pltpu.SMEM)
ANY = pl.BlockSpec(memory_space=pltpu.HBM)


def whole(shape):
    return pl.BlockSpec(shape, lambda i: (0,) * len(shape))


def along(shape, dim, first=0):
    return pl.BlockSpec(
        shape, lambda i: tuple(first + i if d == dim else 0 for d in range(len(shape)))
    )


def call(kernel, outs, in_specs, out_specs, scratch=(), name=None, mib=16, grid=(), alias=None):
    return pl.pallas_call(
        kernel,
        out_shape=[
            jax.ShapeDtypeStruct(*o[:2]) if o[2:] == (NEAR,) else pltpu.HBM(*o) for o in outs
        ],
        grid=grid,
        in_specs=in_specs,
        out_specs=out_specs,
        scratch_shapes=list(scratch),
        compiler_params=pltpu.CompilerParams(vmem_limit_bytes=mib * MIB),
        input_output_aliases=alias or {},
        name=name,
    )


def far(*values):
    return tuple(pltpu.with_memory_space_constraint(v, pltpu.HBM) for v in values)


def swapped(value):
    return lax.ppermute(value, "group", [(0, 1), (1, 0)])


def exchanged(value):
    return lax.all_to_all(value, "dom", split_axis=0, concat_axis=0, tiled=True)


def local(
    nodes,
    edges,
    node_cotangent,
    edge_cotangent,
    senders,
    receivers,
    send_rows,
    edge_in,
    edge_out,
    edge_gain,
    node_in,
    node_out,
    node_gain,
):
    x = nodes[0]
    ed = edges[0]
    ncot = node_cotangent[0]
    ecot = edge_cotangent[0]
    n, w = x.shape
    e = ed.shape[0]
    domains, slots = send_rows.shape[1:]
    h = domains * slots
    half = w // 2
    me = lax.axis_index("group").astype(jnp.int32).reshape(1)
    egain = edge_gain.reshape(1, w)
    ngain = node_gain.reshape(1, w)
    vm = pltpu.VMEM
    dma = pltpu.SemaphoreType.DMA

    (outgoing,) = call(
        outgoing_kernel, [((h, w), BF)], [VM, VM], [VM], [vm((w // LANES, h, LANES), F32)], name="outgoing"
    )(*far(send_rows[0].T, x))
    arrived = exchanged(outgoing.reshape(domains, slots, w)).reshape(h, w)
    eb = 512
    (pre,) = call(
        early_kernel,
        [((e, w), F32)],
        [
            along((1, eb), 1),
            along((1, eb), 1),
            along((eb, w), 0),
            whole((n, w)),
            whole((3 * w, w)),
        ],
        [along((eb, w), 0)],
        [vm((w + 2 * n, w), BF)],
        name="early",
        mib=32,
        grid=(e // eb,),
    )(senders, receivers, *far(ed, x, edge_in))

    keep, give, hat, slope, inv, gg, nacc, act, nprg = call(
        forward_kernel,
        [
            ((domains, 24, half), BF, NEAR),
            ((domains, 24, half), BF, NEAR),
            ((e, w), F32, NEAR),
            ((e, w), F32, NEAR),
            ((e, LANES), F32, NEAR),
            ((n, w), BF, NEAR),
            ((8, w), F32, NEAR),
            ((e, w), BF),
            ((n, w), BF),
        ],
        [SM] + [VM] * 5 + [ANY] * 7,
        [VM] * 7 + [ANY] * 2,
        [
            vm((w, w), BF),
            vm((w, w), BF),
            vm((n, w), BF),
            vm((2 * w, w), BF),
            vm((w, w), BF),
            vm((n, w), BF),
            vm((e, w), BF),
            vm((e, w), BF),
            vm((n, w), BF),
            vm((n, w), BF),
            vm((n, w), BF),
            vm((n, w), BF),
            vm((8, w), F32),
            dma((6,)),
            dma((e // eb,)),
            dma((2, e // eb)),
        ],
        name="forward",
        mib=32,
    )(
        me, senders, receivers, egain, ngain, arrived,
        *far(edge_in, pre, edge_out, x, node_in, node_out, ncot),
    )
    ret, gain_parts, halo, epostg, epg = call(
        backward_kernel,
        [
            ((domains, 2 * slots, half), BF, NEAR),
            ((domains, 8, half), BF, NEAR),
            ((h, w), BF),
            ((e, w), BF),
            ((e, w), BF),
        ],
        [VM] * 8 + [ANY] * 3,
        [VM] * 3 + [ANY] * 2,
        [
            vm((e, w), BF),
            vm((w, w), BF),
            vm((w, w), BF),
            vm((e, w), BF),
            vm((e, w), BF),
            vm((8, w), F32),
            dma((2,)),
            dma((e // eb,)),
            dma((2, e // eb)),
        ],
        name="backward",
        mib=28,
    )(
        senders, receivers, egain, hat, slope, inv, gg, nacc,
        *far(ecot, edge_out, edge_in),
    )
    share = ((domains, 32, half), BF)
    part = along((domains // 4, 32, half), 0)

    def all_grad_edges():
        (value,) = call(
            grad_edges_kernel,
            [((e, w), BF)],
            [along((e // 2, w), 0)] * 2 + [whole((w, w))],
            [along((e // 2, w), 0)],
            name="grad_edges",
            grid=(2,),
        )(*far(epg, ecot, edge_in))
        return value

    got, ret = lax.optimization_barrier((swapped(give), ret))
    (joined,) = call(
        join_kernel,
        [((domains, 48, half), BF)],
        [
            along((domains // 4, 16, half), 0),
            along((domains // 4, 24, half), 0),
            along((domains // 4, 24, half), 0),
            along((domains // 4, 8, half), 0),
        ],
        [along((domains // 4, 48, half), 0)],
        name="join",
        grid=(4,),
    )(ret, keep, got, gain_parts)
    joined, epg = lax.optimization_barrier((joined, epg))
    first = exchanged(joined)
    keep2, give2, sums = call(
        edge_weights_kernel,
        [share + (NEAR,), share + (NEAR,), ((2 * n, w), BF)],
        [SM] + [VM] * 2 + [ANY] * 7,
        [VM, VM, ANY],
        [
            vm((e, w), BF),
            vm((e, w), BF),
            vm((n, w), BF),
            vm((h, w), BF),
            vm((h, w), BF),
            vm((e, w), BF),
            vm((e, w), BF),
            vm((2 * n, w), BF),
            vm((domains, 32, w), F32),
            dma((7,)),
            dma,
        ],
        name="edge_weights",
        mib=44,
    )(me, senders, receivers, *far(epg, ed, x, arrived, halo, act, epostg))
    got2, grad_edges = lax.optimization_barrier((swapped(give2), all_grad_edges()))
    (joined2,) = call(add_kernel, [share], [part, part], [part], name="add", grid=(4,))(
        keep2, got2
    )
    joined2, first, sums = lax.optimization_barrier((joined2, first, sums))
    second = exchanged(joined2)
    nb = 512
    (total,) = call(
        local_sums_kernel,
        [((n, w), F32, NEAR)],
        [
            along((nb, w), 0),
            along((nb, w), 0, n // nb),
            along((nb, w), 0),
            along((nb, w), 0),
            pl.BlockSpec((w, w), lambda i: (1, 0)),
            pl.BlockSpec((w, w), lambda i: (2, 0)),
            whole((w, w)),
        ],
        [along((nb, w), 0)],
        name="local_sums",
        grid=(n // nb,),
    )(*far(sums, sums, nprg, ncot, edge_in, edge_in, node_in))
    (grad_nodes,) = call(
        grad_nodes_kernel,
        [((n, w), BF)],
        [whole((1, h)), whole((domains, 2 * slots, half)), along((nb, w), 0)],
        [along((nb, w), 0)],
        [vm((h, w), BF)],
        name="grad_nodes",
        grid=(n // nb,),
    )(send_rows.reshape(1, h), first, total)
    (node_sum,) = call(
        sum_kernel,
        [((32, half), BF, NEAR)],
        [along((domains, 16, half), 1, 1)],
        [along((16, half), 0)],
        name="node_sum",
        grid=(2,),
    )(first)
    g_nin, g_nout, gains = call(
        node_outputs_kernel,
        [((16, w), F32), ((8, w), F32), ((8, LANES), F32)],
        [SM, VM, VM],
        [VM] * 3,
        name="node_outputs",
    )(me, node_sum, swapped(node_sum))
    (edge_sum,) = call(
        sum_kernel,
        [((32, half), BF, NEAR)],
        [along((domains, 16, half), 1)],
        [along((16, half), 0)],
        name="edge_sum",
        grid=(2,),
    )(second)
    g_ein, g_eout = call(
        edge_outputs_kernel,
        [((24, w), F32), ((8, w), F32)],
        [SM, VM, VM],
        [VM] * 2,
        name="edge_outputs",
    )(me, edge_sum, swapped(edge_sum))
    return (
        grad_edges[None],
        grad_nodes[None],
        g_ein,
        g_eout,
        g_nin,
        g_nout,
        gains[0, 0:8],
        gains[0, 8:16],
    )


def solution(mesh):
    split = P("group", "dom", None)
    placed = (split,) * 4 + (P("group", "dom"),) * 2 + (split,) + (P(),) * 6
    return jax.shard_map(
        local,
        mesh=mesh,
        in_specs=placed,
        out_specs=(split,) * 2 + (P("dom", None),) * 4 + (P("dom"),) * 2,
        check_vma=False,
    )
```

```python
import functools

import jax
import jax.numpy as jnp
from jax import lax
from jax.experimental import pallas as pl
from jax.experimental.pallas import tpu as pltpu
from jax.sharding import PartitionSpec as P

BF = jnp.bfloat16
F32 = jnp.float32
LANES = 128
MIB = 1024 * 1024
NEAR = True


def dot(a, b):
    return jnp.dot(a, b, preferred_element_type=F32)


def dot_nt(a, b):
    return lax.dot_general(a, b, (((1,), (1,)), ((), ())), preferred_element_type=F32)


def dot_tn(a, b):
    return lax.dot_general(a, b, (((0,), (0,)), ((), ())), preferred_element_type=F32)


def spread(ids):
    return jnp.broadcast_to(ids, (LANES, ids.shape[1])).T


def pick(spread_ids, count):
    lane = lax.broadcasted_iota(jnp.int32, spread_ids.shape, 1)
    from_lane = (spread_ids - lane).astype(jnp.int16)
    one = jnp.ones(spread_ids.shape, BF)
    tiles = [
        jnp.where(from_lane == jnp.int16(LANES * k), one, jnp.zeros_like(one))
        for k in range(count // LANES)
    ]
    return jnp.concatenate(tiles, axis=1)


def pick_t(ids, first, count):
    row = lax.broadcasted_iota(jnp.int32, (count, ids.shape[1]), 0) + first
    return jnp.where(row == ids, 1.0, 0.0).astype(BF)


def swish_both(pre):
    gate = jax.nn.sigmoid(pre)
    return pre * gate, gate * (1.0 + pre * (1.0 - gate))


def normalize(hidden):
    centre = hidden - jnp.mean(hidden, axis=-1, keepdims=True)
    inverse = lax.rsqrt(jnp.mean(centre * centre, axis=-1, keepdims=True) + 1e-05)
    return centre * inverse, inverse


def norm_back(upstream, gain, normed, inverse):
    scaled = upstream * gain
    return inverse * (
        scaled
        - jnp.mean(scaled, axis=-1, keepdims=True)
        - normed * jnp.mean(scaled * normed, axis=-1, keepdims=True)
    )


def fold(value):
    return jnp.sum(value.reshape(value.shape[0] // 8, 8, value.shape[1]), axis=0)


def outgoing_kernel(list_ref, nodes_ref, out_ref, rows_ref):
    slots, domains = list_ref.shape
    ids = jnp.concatenate([spread(list_ref[s : s + 1, :]) for s in range(slots)], axis=0)
    rows = dot(pick(ids, nodes_ref.shape[0]), nodes_ref[...])
    for s in range(slots):
        for k in range(rows_ref.shape[0]):
            rows_ref[k, pl.ds(s, domains, stride=slots), :] = rows[
                s * domains : (s + 1) * domains, k * LANES : (k + 1) * LANES
            ]
    for k in range(rows_ref.shape[0]):
        out_ref[:, k * LANES : (k + 1) * LANES] = rows_ref[k].astype(BF)


def early_kernel(
    send_ref, recv_ref, edges_ref, nodes_ref, ein_ref, nin_ref, out_ref, node_ref, table
):
    n, w = nodes_ref.shape
    nb = node_ref.shape[0]

    @pl.when(pl.program_id(0) == 0)
    def _():
        table[0:w, :] = ein_ref[0:w, :]
        table[w : w + n, :] = dot(nodes_ref[...], ein_ref[w : 2 * w, :]).astype(BF)
        table[w + n : w + 2 * n, :] = dot(nodes_ref[...], ein_ref[2 * w : 3 * w, :]).astype(BF)

    left = jnp.concatenate(
        [edges_ref[...], pick(spread(send_ref[...]), n), pick(spread(recv_ref[...]), n)], axis=1
    )
    out_ref[...] = dot(left, table[...])
    first = pl.multiple_of(pl.program_id(0) * nb, nb)
    node_ref[...] = dot(nodes_ref[pl.ds(first, nb), :], nin_ref[...])


def gain_rows(edge_gain, node_gain, domains, width):
    per = edge_gain.shape[1] // domains
    shape = (domains, edge_gain.shape[1])
    own = lax.broadcasted_iota(jnp.int32, shape, 1) // per == lax.broadcasted_iota(
        jnp.int32, shape, 0
    )
    col = lax.broadcasted_iota(jnp.int32, (edge_gain.shape[1], width), 0) % per
    lane = lax.broadcasted_iota(jnp.int32, (edge_gain.shape[1], width), 1)
    total = 0.0
    for k, gain in enumerate((edge_gain, node_gain)):
        mine = jnp.where(own, jnp.broadcast_to(gain, shape), 0.0).astype(BF)
        place = jnp.where(lane == col + per * k, 1.0, 0.0).astype(BF)
        total = total + dot(mine, place)
    return total


def forward_kernel(
    g_ref, send_ref, recv_ref, egain_ref, ngain_ref, arrived_ref,
    ein_hbm, pre_hbm, eout_hbm, nodes_hbm, nin_hbm, nout_hbm, ncot_hbm, npre_hbm,
    keep_ref, give_ref, hat, slope, inv, gg, nacc_ref,
    act_hbm, nprg_hbm,
    weight, eout, nodes, nin, nout, ncot, npre,
    act_ref, upd, gath, nact, npostg, nprg, nacc,
    in_sem, pre_sem, out_sem,
):
    n, w = nodes.shape
    e = hat.shape[0]
    h = arrived_ref.shape[0]
    half = w // 2
    domains = keep_ref.shape[0]
    eb = 512
    blocks = e // eb
    loads = [
        pltpu.make_async_copy(source, target, in_sem.at[k])
        for k, (source, target) in enumerate(
            (
                (ein_hbm.at[pl.ds(w, w), :], weight),
                (eout_hbm, eout),
                (nodes_hbm, nodes),
                (npre_hbm, npre),
                (nin_hbm.at[pl.ds(w, w), :], nin),
                (nout_hbm, nout),
                (ncot_hbm, ncot),
            )
        )
    ]

    def rows(b):
        return slice(b * eb, (b + 1) * eb)

    pre_loads = [
        pltpu.make_async_copy(pre_hbm.at[rows(b), :], hat.at[rows(b), :], pre_sem.at[b])
        for b in range(blocks)
    ]
    stores = []

    def store(source, target, k, b):
        copy = pltpu.make_async_copy(
            source.at[rows(b), :], target.at[rows(b), :], out_sem.at[k, b]
        )
        copy.start()
        stores.append(copy)

    loads[0].start()
    pre_loads[0].start()
    loads[1].start()
    for load in pre_loads[1:] + loads[2:]:
        load.start()
    egain = egain_ref[...]
    ngain = ngain_ref[...]
    nacc[...] = jnp.zeros_like(nacc)
    loads[0].wait()
    far_table = dot(arrived_ref[...], weight[...]).astype(BF)
    gg[0:h, :] = far_table
    loads[1].wait()

    def far_part(b):
        return dot(pick(spread(send_ref[:, rows(b)]) - n, h), gg[0:h, :])

    def edge_act(b, far_pre):
        pre_loads[b].wait()
        act, slp = swish_both(hat[rows(b), :] + far_pre)
        act = act.astype(BF)
        act_ref[rows(b), :] = act
        store(act_ref, act_hbm, 0, b)
        slope[rows(b), :] = slp
        return act

    def edge_norm(b, post):
        normed, inverse = normalize(post)
        hat[rows(b), :] = normed
        inv[rows(b), :] = jnp.broadcast_to(inverse, (eb, LANES))
        upd[rows(b), :] = (normed * egain).astype(BF)

    pre, act, post = {}, {}, {}
    for t in range(blocks + 3):
        if t < blocks:
            pre[t] = far_part(t)
        if 0 <= t - 2 < blocks:
            post[t - 2] = dot(act.pop(t - 2), eout[...])
        if 0 <= t - 1 < blocks:
            act[t - 1] = edge_act(t - 1, pre.pop(t - 1))
        if 0 <= t - 3 < blocks:
            edge_norm(t - 3, post.pop(t - 3))
    for load in loads[2:]:
        load.wait()

    def node_gather(b):
        gathered = dot(pick_t(recv_ref[...], b * eb, eb), upd[...]).astype(BF)
        gath[rows(b), :] = gathered
        return npre[rows(b), :] + dot(gathered, nin[...])

    def node_act(b, value):
        act, slp = swish_both(value)
        act = act.astype(BF)
        nact[rows(b), :] = act
        return act, slp

    def node_back(b, value):
        normed, inverse = normalize(value)
        upstream = ncot[rows(b), :].astype(F32)
        nacc[...] += fold(upstream * normed)
        postg = norm_back(upstream, ngain, normed, inverse).astype(BF)
        npostg[rows(b), :] = postg
        return postg

    def node_turn(b, value, slp):
        preg = (value * slp).astype(BF)
        nprg[rows(b), :] = preg
        store(nprg, nprg_hbm, 1, b)
        return preg

    def node_end(b, preg):
        gg[rows(b), :] = dot_nt(preg, nin[...]).astype(BF)

    pre0 = node_gather(0)
    pre1 = node_gather(1)
    act0, slope0 = node_act(0, pre0)
    post0 = dot(act0, nout[...])
    act1, slope1 = node_act(1, pre1)
    post1 = dot(act1, nout[...])
    postg0 = node_back(0, post0)
    turn0 = dot_nt(postg0, nout[...])
    postg1 = node_back(1, post1)
    turn1 = dot_nt(postg1, nout[...])
    preg0 = node_turn(0, turn0, slope0)
    preg1 = node_turn(1, turn1, slope1)
    node_end(0, preg0)
    node_end(1, preg1)
    nacc_ref[...] = jnp.broadcast_to(jnp.sum(nacc[...], axis=0, keepdims=True), nacc.shape)
    mine = g_ref[0]
    for out_ref, which in ((keep_ref, mine), (give_ref, 1 - mine)):
        cols = pl.ds(pl.multiple_of(which * half, half), half)
        pg = nprg[:, cols]
        for k, source in enumerate((nodes, gath)):
            grad = dot_tn(source[...], pg).reshape(domains // 2, 16, half)
            out_ref[k * (domains // 2) : (k + 1) * (domains // 2), 0:16, :] = grad.astype(BF)
        last = dot_tn(nact[...], npostg[:, cols]).reshape(domains, 8, half)
        out_ref[:, 16:24, :] = last.astype(BF)
    for copy in stores:
        copy.wait()


def backward_kernel(
    send_ref, recv_ref, egain_ref, hat, slope, inv, gg, nacc_ref,
    ecot_hbm, eout_hbm, ein_hbm,
    ret_ref, gains_ref, halo_ref,
    epostg_hbm, epg_hbm,
    ecot, eout, weight, epostg_ref, epg_ref, eacc,
    in_sem, ecot_sem, out_sem,
):
    n, w = gg.shape
    e = hat.shape[0]
    h = halo_ref.shape[0]
    domains = ret_ref.shape[0]
    eb = 512
    blocks = e // eb

    def rows(b):
        return slice(b * eb, (b + 1) * eb)

    stores = []

    def store(source, target, k, b):
        copy = pltpu.make_async_copy(
            source.at[rows(b), :], target.at[rows(b), :], out_sem.at[k, b]
        )
        copy.start()
        stores.append(copy)

    loads = [
        pltpu.make_async_copy(ecot_hbm.at[rows(b), :], ecot.at[rows(b), :], ecot_sem.at[b])
        for b in range(blocks)
    ]
    weights = [
        pltpu.make_async_copy(eout_hbm, eout, in_sem.at[0]),
        pltpu.make_async_copy(ein_hbm.at[pl.ds(w, w), :], weight, in_sem.at[1]),
    ]
    for load in (loads[0], weights[0], *loads[1:], weights[1]):
        load.start()
    egain = egain_ref[...]
    eacc[...] = jnp.zeros_like(eacc)

    def edge_gather(b):
        return dot(pick(spread(recv_ref[:, rows(b)]), n), gg[...])

    def edge_back(b, value):
        loads[b].wait()
        upstream = ecot[rows(b), :].astype(F32) + value
        normed = hat[rows(b), :]
        eacc[...] += fold(upstream * normed)
        postg = norm_back(upstream, egain, normed, inv[rows(b), 0:1]).astype(BF)
        epostg_ref[rows(b), :] = postg
        store(epostg_ref, epostg_hbm, 0, b)
        return postg

    def edge_end(b, value):
        epg_ref[rows(b), :] = (value * slope[rows(b), :]).astype(BF)
        store(epg_ref, epg_hbm, 1, b)

    def halo_part(first, last):
        ids = send_ref[:, first * eb : last * eb]
        return dot(pick_t(ids, n, h), epg_ref[first * eb : last * eb, :])

    pre, act, post = {}, {}, {}
    halo = 0.0
    for t in range(blocks + 3):
        if t < blocks:
            pre[t] = edge_gather(t)
        if t == 2:
            weights[0].wait()
        if 0 <= t - 2 < blocks:
            post[t - 2] = dot_nt(act.pop(t - 2), eout[...])
        if t == blocks + 1:
            halo = halo_part(0, blocks // 2)
        if 0 <= t - 1 < blocks:
            act[t - 1] = edge_back(t - 1, pre.pop(t - 1))
        if 0 <= t - 3 < blocks:
            edge_end(t - 3, post.pop(t - 3))
    gains = gain_rows(jnp.sum(eacc[...], axis=0, keepdims=True), nacc_ref[0:1, :], domains, LANES)
    gains_ref[...] = jnp.broadcast_to(gains[:, None, :], (domains, 8, LANES)).astype(BF)
    halo = (halo + halo_part(blocks // 2, blocks)).astype(BF)
    halo_ref[...] = halo
    weights[1].wait()
    ret = dot_nt(halo, weight[...])
    per = h // domains
    for k in range(w // LANES):
        part = ret[:, k * LANES : (k + 1) * LANES].reshape(domains, per, LANES)
        ret_ref[:, k * per : (k + 1) * per, :] = part.astype(BF)
    for copy in stores:
        copy.wait()


def grad_edges_kernel(epg_ref, ecot_ref, ein_ref, out_ref):
    out_ref[...] = (ecot_ref[...].astype(F32) + dot_nt(epg_ref[...], ein_ref[...])).astype(BF)


def edge_weights_kernel(
    g_ref, send_ref, recv_ref,
    epg_hbm, edges_hbm, nodes_hbm, arrived_hbm, halo_hbm, act_hbm, epostg_hbm,
    keep_ref, give_ref, sums_hbm,
    epg, edges, nodes, arrived, halo, act, epostg, sums, share, in_sem, out_sem,
):
    n, w = nodes.shape
    half = w // 2
    domains = share.shape[0]
    nb = 512
    loads = [
        pltpu.make_async_copy(source, target, in_sem.at[k])
        for k, (source, target) in enumerate(
            (
                (epg_hbm, epg),
                (edges_hbm, edges),
                (nodes_hbm, nodes),
                (arrived_hbm, arrived),
                (halo_hbm, halo),
                (act_hbm, act),
                (epostg_hbm, epostg),
            )
        )
    ]
    for load in loads:
        load.start()
    loads[0].wait()

    def node_sums(b, carry):
        first = pl.multiple_of(b * nb, nb)
        later = pl.multiple_of(n + b * nb, nb)
        sums[pl.ds(first, nb), :] = dot(pick_t(send_ref[...], first, nb), epg[...]).astype(BF)
        sums[pl.ds(later, nb), :] = dot(pick_t(recv_ref[...], first, nb), epg[...]).astype(BF)
        return carry

    lax.fori_loop(0, n // nb, node_sums, 0)
    out = pltpu.make_async_copy(sums, sums_hbm, out_sem)
    out.start()
    for load in loads[1:]:
        load.wait()
    per = 3 * w // domains // 8

    def put(k, part):
        for j in range(w // 8):
            t = k * (w // 8) + j
            share[t // per, (t % per) * 8 : (t % per) * 8 + 8, :] = part[j * 8 : j * 8 + 8, :]

    put(0, dot_tn(edges[...], epg[...]))
    both = dot_tn(nodes[...], jnp.concatenate([sums[0:n, :], sums[n:, :]], axis=1))
    put(1, both[:, :w] + dot_tn(arrived[...], halo[...]))
    put(2, both[:, w:])
    share[:, 24:32, :] = dot_tn(act[...], epostg[...]).reshape(domains, 8, w)
    mine = g_ref[0]
    keep_ref[...] = share[:, :, pl.ds(pl.multiple_of(mine * half, half), half)].astype(BF)
    give_ref[...] = share[:, :, pl.ds(pl.multiple_of((1 - mine) * half, half), half)].astype(BF)
    out.wait()


def local_sums_kernel(send_ref, recv_ref, nprg_ref, ncot_ref, ws_ref, wr_ref, nin_ref, out_ref):
    out_ref[...] = (
        ncot_ref[...].astype(F32)
        + dot_nt(send_ref[...], ws_ref[...])
        + dot_nt(recv_ref[...], wr_ref[...])
        + dot_nt(nprg_ref[...], nin_ref[...])
    )


def grad_nodes_kernel(list_ref, first_ref, total_ref, out_ref, back):
    domains, rows, lanes = first_ref.shape
    quarters = total_ref.shape[1] // lanes
    slots = rows // quarters
    block = total_ref.shape[0]

    @pl.when(pl.program_id(0) == 0)
    def _():
        for k in range(quarters):
            part = first_ref[:, k * slots : (k + 1) * slots, :].astype(F32)
            back[:, k * lanes : (k + 1) * lanes] = part.reshape(domains * slots, lanes).astype(BF)

    sel = pick_t(list_ref[...], pl.program_id(0) * block, block)
    out_ref[...] = (total_ref[...] + dot(sel, back[...])).astype(BF)


def sum_kernel(all_ref, out_ref):
    out_ref[...] = jnp.sum(all_ref[...].astype(F32), axis=0).astype(BF)


def node_sum_kernel(all_ref, out_ref):
    for k in range(2):
        part = all_ref[:, 32 + 24 * k : 56 + 24 * k, :].astype(F32)
        out_ref[0:24, k * LANES : (k + 1) * LANES] = jnp.sum(part, axis=0).astype(BF)
    gains = jnp.sum(all_ref[:, 80:88, :].astype(F32), axis=0).astype(BF)
    out_ref[24:32, :] = jnp.concatenate([gains, gains], axis=1)


def edge_outputs_kernel(g_ref, mine_ref, got_ref, ein_ref, eout_ref):
    half = mine_ref.shape[1]
    low = g_ref[0] == 0
    mine = mine_ref[...].astype(F32)
    got = got_ref[...].astype(F32)
    for k, value in enumerate((jnp.where(low, mine, got), jnp.where(low, got, mine))):
        cols = slice(k * half, (k + 1) * half)
        ein_ref[:, cols] = value[0:24, :]
        eout_ref[:, cols] = value[24:32, :]


def node_outputs_kernel(g_ref, mine_ref, got_ref, nin_ref, nout_ref, gains_ref):
    half = mine_ref.shape[1]
    low = g_ref[0] == 0
    mine = mine_ref[...].astype(F32)
    got = got_ref[...].astype(F32)
    for k, value in enumerate((jnp.where(low, mine, got), jnp.where(low, got, mine))):
        cols = slice(k * half, (k + 1) * half)
        nin_ref[:, cols] = value[0:16, :]
        nout_ref[:, cols] = value[16:24, :]
    gains_ref[...] = mine[24:32, 0:LANES] + got[24:32, 0:LANES]


def in_pieces(make, out_hbm, buffer, sem):
    count = sem.shape[0]
    size = buffer.shape[0] // count
    copies = []
    for k in range(count):
        part = slice(k * size, (k + 1) * size)
        make(part)
        copies.append(pltpu.make_async_copy(buffer.at[part], out_hbm.at[part], sem.at[k]))
        copies[-1].start()
    for copy in copies:
        copy.wait()


def join_kernel(ret_ref, keep_ref, got_ref, gains_ref, out_hbm, buffer, sem):
    def make(part):
        buffer[part, 0:32, :] = ret_ref[part]
        both = (keep_ref[part].astype(F32) + got_ref[part].astype(F32)).astype(BF)
        buffer[part, 32:56, :] = both[:, :, :LANES]
        buffer[part, 56:80, :] = both[:, :, LANES:]
        buffer[part, 80:88, :] = gains_ref[part]

    in_pieces(make, out_hbm, buffer, sem)


def add_kernel(keep_ref, got_ref, out_hbm, buffer, sem):
    def make(part):
        buffer[part] = (keep_ref[part].astype(F32) + got_ref[part].astype(F32)).astype(BF)

    in_pieces(make, out_hbm, buffer, sem)


VM = pl.BlockSpec(memory_space=pltpu.VMEM)
SM = pl.BlockSpec(memory_space=pltpu.SMEM)
ANY = pl.BlockSpec(memory_space=pltpu.HBM)


def whole(shape):
    return pl.BlockSpec(shape, lambda i: (0,) * len(shape))


def along(shape, dim, first=0):
    return pl.BlockSpec(
        shape, lambda i: tuple(first + i if d == dim else 0 for d in range(len(shape)))
    )


def call(kernel, outs, in_specs, out_specs, scratch=(), name=None, mib=16, grid=(), alias=None):
    return pl.pallas_call(
        kernel,
        out_shape=[
            jax.ShapeDtypeStruct(*o[:2]) if o[2:] == (NEAR,) else pltpu.HBM(*o) for o in outs
        ],
        grid=grid,
        in_specs=in_specs,
        out_specs=out_specs,
        scratch_shapes=list(scratch),
        compiler_params=pltpu.CompilerParams(vmem_limit_bytes=mib * MIB),
        input_output_aliases=alias or {},
        name=name,
    )


def far(*values):
    return tuple(pltpu.with_memory_space_constraint(v, pltpu.HBM) for v in values)


def swapped(value):
    return lax.ppermute(value, "group", [(0, 1), (1, 0)])


def exchanged(value):
    return lax.all_to_all(value, "dom", split_axis=0, concat_axis=0, tiled=True)


def local(
    nodes,
    edges,
    node_cotangent,
    edge_cotangent,
    senders,
    receivers,
    send_rows,
    edge_in,
    edge_out,
    edge_gain,
    node_in,
    node_out,
    node_gain,
):
    x = nodes[0]
    ed = edges[0]
    ncot = node_cotangent[0]
    ecot = edge_cotangent[0]
    n, w = x.shape
    e = ed.shape[0]
    domains, slots = send_rows.shape[1:]
    h = domains * slots
    half = w // 2
    me = lax.axis_index("group").astype(jnp.int32).reshape(1)
    egain = edge_gain.reshape(1, w)
    ngain = node_gain.reshape(1, w)
    vm = pltpu.VMEM
    dma = pltpu.SemaphoreType.DMA

    (outgoing,) = call(
        outgoing_kernel, [((h, w), BF)], [VM, VM], [VM], [vm((w // LANES, h, LANES), F32)], name="outgoing"
    )(*far(send_rows[0].T, x))
    arrived = exchanged(outgoing.reshape(domains, slots, w)).reshape(h, w)
    eb = 512
    pre, node_pre = call(
        early_kernel,
        [((e, w), F32), ((n, w), F32)],
        [
            along((1, eb), 1),
            along((1, eb), 1),
            along((eb, w), 0),
            whole((n, w)),
            whole((3 * w, w)),
            whole((w, w)),
        ],
        [along((eb, w), 0), along((n * eb // e, w), 0)],
        [vm((w + 2 * n, w), BF)],
        name="early",
        mib=32,
        grid=(e // eb,),
    )(senders, receivers, *far(ed, x, edge_in, node_in))

    keep, give, hat, slope, inv, gg, nacc, act, nprg = call(
        forward_kernel,
        [
            ((domains, 24, half), BF, NEAR),
            ((domains, 24, half), BF, NEAR),
            ((e, w), F32, NEAR),
            ((e, w), F32, NEAR),
            ((e, LANES), F32, NEAR),
            ((n, w), BF, NEAR),
            ((8, w), F32, NEAR),
            ((e, w), BF),
            ((n, w), BF),
        ],
        [SM] + [VM] * 5 + [ANY] * 8,
        [VM] * 7 + [ANY] * 2,
        [
            vm((w, w), BF),
            vm((w, w), BF),
            vm((n, w), BF),
            vm((w, w), BF),
            vm((w, w), BF),
            vm((n, w), BF),
            vm((n, w), F32),
            vm((e, w), BF),
            vm((e, w), BF),
            vm((n, w), BF),
            vm((n, w), BF),
            vm((n, w), BF),
            vm((n, w), BF),
            vm((8, w), F32),
            dma((7,)),
            dma((e // eb,)),
            dma((2, e // eb)),
        ],
        name="forward",
        mib=32,
    )(
        me, senders, receivers, egain, ngain, arrived,
        *far(edge_in, pre, edge_out, x, node_in, node_out, ncot, node_pre),
    )
    ret, gain_parts, halo, epostg, epg = call(
        backward_kernel,
        [
            ((domains, 4 * slots, LANES), BF, NEAR),
            ((domains, 8, LANES), BF, NEAR),
            ((h, w), BF),
            ((e, w), BF),
            ((e, w), BF),
        ],
        [VM] * 8 + [ANY] * 3,
        [VM] * 3 + [ANY] * 2,
        [
            vm((e, w), BF),
            vm((w, w), BF),
            vm((w, w), BF),
            vm((e, w), BF),
            vm((e, w), BF),
            vm((8, w), F32),
            dma((2,)),
            dma((e // eb,)),
            dma((2, e // eb)),
        ],
        name="backward",
        mib=28,
    )(
        senders, receivers, egain, hat, slope, inv, gg, nacc,
        *far(ecot, edge_out, edge_in),
    )
    share = ((domains, 32, half), BF)
    got, ret = lax.optimization_barrier((swapped(give), ret))
    (joined,) = call(
        join_kernel,
        [((domains, 88, LANES), BF)],
        [VM] * 4,
        [ANY],
        [vm((domains, 88, LANES), BF), dma((4,))],
        name="join",
    )(ret, keep, got, gain_parts)
    joined, epg = lax.optimization_barrier((joined, epg))
    first = exchanged(joined)

    def all_grad_edges():
        (value,) = call(
            grad_edges_kernel,
            [((e, w), BF)],
            [along((e // 2, w), 0)] * 2 + [whole((w, w))],
            [along((e // 2, w), 0)],
            name="grad_edges",
            grid=(2,),
        )(*far(epg, ecot, edge_in))
        return value

    keep2, give2, sums = call(
        edge_weights_kernel,
        [share + (NEAR,), share + (NEAR,), ((2 * n, w), BF)],
        [SM] + [VM] * 2 + [ANY] * 7,
        [VM, VM, ANY],
        [
            vm((e, w), BF),
            vm((e, w), BF),
            vm((n, w), BF),
            vm((h, w), BF),
            vm((h, w), BF),
            vm((e, w), BF),
            vm((e, w), BF),
            vm((2 * n, w), BF),
            vm((domains, 32, w), F32),
            dma((7,)),
            dma,
        ],
        name="edge_weights",
        mib=44,
    )(me, senders, receivers, *far(epg, ed, x, arrived, halo, act, epostg))
    got2, grad_edges = lax.optimization_barrier((swapped(give2), all_grad_edges()))
    (joined2,) = call(
        add_kernel,
        [share],
        [VM] * 2,
        [ANY],
        [vm((domains, 32, half), BF), dma((4,))],
        name="add",
    )(keep2, got2)
    joined2, first, sums = lax.optimization_barrier((joined2, first, sums))
    second = exchanged(joined2)
    nb = 512
    (total,) = call(
        local_sums_kernel,
        [((n, w), F32, NEAR)],
        [
            along((nb, w), 0),
            along((nb, w), 0, n // nb),
            along((nb, w), 0),
            along((nb, w), 0),
            pl.BlockSpec((w, w), lambda i: (1, 0)),
            pl.BlockSpec((w, w), lambda i: (2, 0)),
            whole((w, w)),
        ],
        [along((nb, w), 0)],
        name="local_sums",
        grid=(n // nb,),
    )(*far(sums, sums, nprg, ncot, edge_in, edge_in, node_in))
    (grad_nodes,) = call(
        grad_nodes_kernel,
        [((n, w), BF)],
        [whole((1, h)), whole((domains, 4 * slots, LANES)), along((nb, w), 0)],
        [along((nb, w), 0)],
        [vm((h, w), BF)],
        name="grad_nodes",
        grid=(n // nb,),
    )(send_rows.reshape(1, h), first, total)
    (node_sum,) = call(
        node_sum_kernel, [((32, half), BF, NEAR)], [VM], [VM], name="node_sum"
    )(first)
    g_nin, g_nout, gains = call(
        node_outputs_kernel,
        [((16, w), F32), ((8, w), F32), ((8, LANES), F32)],
        [SM, VM, VM],
        [VM] * 3,
        name="node_outputs",
    )(me, node_sum, swapped(node_sum))
    (edge_sum,) = call(
        sum_kernel, [((32, half), BF, NEAR)], [VM], [VM], name="edge_sum"
    )(second)
    g_ein, g_eout = call(
        edge_outputs_kernel,
        [((24, w), F32), ((8, w), F32)],
        [SM, VM, VM],
        [VM] * 2,
        name="edge_outputs",
    )(me, edge_sum, swapped(edge_sum))
    return (
        grad_edges[None],
        grad_nodes[None],
        g_ein,
        g_eout,
        g_nin,
        g_nout,
        gains[0, 0:8],
        gains[0, 8:16],
    )


def solution(mesh):
    split = P("group", "dom", None)
    placed = (split,) * 4 + (P("group", "dom"),) * 2 + (split,) + (P(),) * 6
    return jax.shard_map(
        local,
        mesh=mesh,
        in_specs=placed,
        out_specs=(split,) * 2 + (P("dom", None),) * 4 + (P("dom"),) * 2,
        check_vma=False,
    )
```

```python
import functools

import jax
import jax.numpy as jnp
from jax import lax
from jax.experimental import pallas as pl
from jax.experimental.pallas import tpu as pltpu
from jax.sharding import PartitionSpec as P

BF = jnp.bfloat16
F32 = jnp.float32
LANES = 128
MIB = 1024 * 1024
NEAR = True


def dot(a, b):
    return jnp.dot(a, b, preferred_element_type=F32)


def dot_nt(a, b):
    return lax.dot_general(a, b, (((1,), (1,)), ((), ())), preferred_element_type=F32)


def dot_tn(a, b):
    return lax.dot_general(a, b, (((0,), (0,)), ((), ())), preferred_element_type=F32)


def spread(ids):
    return jnp.broadcast_to(ids, (LANES, ids.shape[1])).T


def pick(spread_ids, count):
    lane = lax.broadcasted_iota(jnp.int32, spread_ids.shape, 1)
    from_lane = (spread_ids - lane).astype(jnp.int16)
    one = jnp.ones(spread_ids.shape, BF)
    tiles = [
        jnp.where(from_lane == jnp.int16(LANES * k), one, jnp.zeros_like(one))
        for k in range(count // LANES)
    ]
    return jnp.concatenate(tiles, axis=1)


def pick_t(ids, first, count):
    row = lax.broadcasted_iota(jnp.int32, (count, ids.shape[1]), 0) + first
    return jnp.where(row == ids, 1.0, 0.0).astype(BF)


def swish_both(pre):
    gate = jax.nn.sigmoid(pre)
    return pre * gate, gate * (1.0 + pre * (1.0 - gate))


def normalize(hidden):
    centre = hidden - jnp.mean(hidden, axis=-1, keepdims=True)
    inverse = lax.rsqrt(jnp.mean(centre * centre, axis=-1, keepdims=True) + 1e-05)
    return centre * inverse, inverse


def norm_back(upstream, gain, normed, inverse):
    scaled = upstream * gain
    return inverse * (
        scaled
        - jnp.mean(scaled, axis=-1, keepdims=True)
        - normed * jnp.mean(scaled * normed, axis=-1, keepdims=True)
    )


def fold(value):
    return jnp.sum(value.reshape(value.shape[0] // 8, 8, value.shape[1]), axis=0)


def outgoing_kernel(list_ref, nodes_ref, out_ref, rows_ref):
    slots, domains = list_ref.shape
    ids = jnp.concatenate([spread(list_ref[s : s + 1, :]) for s in range(slots)], axis=0)
    rows = dot(pick(ids, nodes_ref.shape[0]), nodes_ref[...])
    for s in range(slots):
        for k in range(rows_ref.shape[0]):
            rows_ref[k, pl.ds(s, domains, stride=slots), :] = rows[
                s * domains : (s + 1) * domains, k * LANES : (k + 1) * LANES
            ]
    for k in range(rows_ref.shape[0]):
        out_ref[:, k * LANES : (k + 1) * LANES] = rows_ref[k].astype(BF)


def early_kernel(
    send_ref, recv_ref, edges_ref, nodes_ref, ein_ref, nin_ref, out_ref, node_ref, table
):
    n, w = nodes_ref.shape
    nb = node_ref.shape[0]

    @pl.when(pl.program_id(0) == 0)
    def _():
        table[0:w, :] = ein_ref[0:w, :]
        table[w : w + n, :] = dot(nodes_ref[...], ein_ref[w : 2 * w, :]).astype(BF)
        table[w + n : w + 2 * n, :] = dot(nodes_ref[...], ein_ref[2 * w : 3 * w, :]).astype(BF)

    left = jnp.concatenate(
        [edges_ref[...], pick(spread(send_ref[...]), n), pick(spread(recv_ref[...]), n)], axis=1
    )
    out_ref[...] = dot(left, table[...])
    first = pl.multiple_of(pl.program_id(0) * nb, nb)
    node_ref[...] = dot(nodes_ref[pl.ds(first, nb), :], nin_ref[...])


def gain_rows(edge_gain, node_gain, domains, width):
    per = edge_gain.shape[1] // domains
    shape = (domains, edge_gain.shape[1])
    own = lax.broadcasted_iota(jnp.int32, shape, 1) // per == lax.broadcasted_iota(
        jnp.int32, shape, 0
    )
    col = lax.broadcasted_iota(jnp.int32, (edge_gain.shape[1], width), 0) % per
    lane = lax.broadcasted_iota(jnp.int32, (edge_gain.shape[1], width), 1)
    total = 0.0
    for k, gain in enumerate((edge_gain, node_gain)):
        mine = jnp.where(own, jnp.broadcast_to(gain, shape), 0.0).astype(BF)
        place = jnp.where(lane == col + per * k, 1.0, 0.0).astype(BF)
        total = total + dot(mine, place)
    return total


def forward_kernel(
    g_ref, send_ref, recv_ref, egain_ref, ngain_ref, arrived_ref, ein_ref, eout,
    pre_hbm, nodes_hbm, nin_hbm, nout_hbm, ncot_hbm, npre_hbm,
    keep_ref, give_ref, hat, slope, inv, gg, nacc_ref,
    act_hbm, nprg_hbm,
    nodes, nin, nout, ncot, npre,
    act_ref, upd, gath, nact, npostg, nprg, nacc,
    in_sem, pre_sem, out_sem,
):
    n, w = nodes.shape
    e = hat.shape[0]
    h = arrived_ref.shape[0]
    half = w // 2
    domains = keep_ref.shape[0]
    eb = 512
    blocks = e // eb
    loads = [
        pltpu.make_async_copy(source, target, in_sem.at[k])
        for k, (source, target) in enumerate(
            (
                (nodes_hbm, nodes),
                (npre_hbm, npre),
                (nin_hbm.at[pl.ds(w, w), :], nin),
                (nout_hbm, nout),
                (ncot_hbm, ncot),
            )
        )
    ]

    def rows(b):
        return slice(b * eb, (b + 1) * eb)

    pre_loads = [
        pltpu.make_async_copy(pre_hbm.at[rows(b), :], hat.at[rows(b), :], pre_sem.at[b])
        for b in range(blocks)
    ]
    stores = []

    def store(source, target, k, b):
        copy = pltpu.make_async_copy(
            source.at[rows(b), :], target.at[rows(b), :], out_sem.at[k, b]
        )
        copy.start()
        stores.append(copy)

    for load in pre_loads + loads:
        load.start()
    egain = egain_ref[...]
    ngain = ngain_ref[...]
    nacc[...] = jnp.zeros_like(nacc)
    gg[0:h, :] = dot(arrived_ref[...], ein_ref[w : 2 * w, :]).astype(BF)

    def far_part(b):
        return dot(pick(spread(send_ref[:, rows(b)]) - n, h), gg[0:h, :])

    def edge_act(b, far_pre):
        pre_loads[b].wait()
        act, slp = swish_both(hat[rows(b), :] + far_pre)
        act = act.astype(BF)
        act_ref[rows(b), :] = act
        store(act_ref, act_hbm, 0, b)
        slope[rows(b), :] = slp
        return act

    def edge_norm(b, post):
        normed, inverse = normalize(post)
        hat[rows(b), :] = normed
        inv[rows(b), :] = jnp.broadcast_to(inverse, (eb, LANES))
        upd[rows(b), :] = (normed * egain).astype(BF)

    pre, act, post = {}, {}, {}
    for t in range(blocks + 3):
        if t < blocks:
            pre[t] = far_part(t)
        if 0 <= t - 2 < blocks:
            post[t - 2] = dot(act.pop(t - 2), eout[...])
        if 0 <= t - 1 < blocks:
            act[t - 1] = edge_act(t - 1, pre.pop(t - 1))
        if 0 <= t - 3 < blocks:
            edge_norm(t - 3, post.pop(t - 3))
    for load in loads:
        load.wait()

    def node_gather(b):
        gathered = dot(pick_t(recv_ref[...], b * eb, eb), upd[...]).astype(BF)
        gath[rows(b), :] = gathered
        return npre[rows(b), :] + dot(gathered, nin[...])

    def node_act(b, value):
        act, slp = swish_both(value)
        act = act.astype(BF)
        nact[rows(b), :] = act
        return act, slp

    def node_back(b, value):
        normed, inverse = normalize(value)
        upstream = ncot[rows(b), :].astype(F32)
        nacc[...] += fold(upstream * normed)
        postg = norm_back(upstream, ngain, normed, inverse).astype(BF)
        npostg[rows(b), :] = postg
        return postg

    def node_turn(b, value, slp):
        preg = (value * slp).astype(BF)
        nprg[rows(b), :] = preg
        store(nprg, nprg_hbm, 1, b)
        return preg

    def node_end(b, preg):
        gg[rows(b), :] = dot_nt(preg, nin[...]).astype(BF)

    pre0 = node_gather(0)
    pre1 = node_gather(1)
    act0, slope0 = node_act(0, pre0)
    post0 = dot(act0, nout[...])
    act1, slope1 = node_act(1, pre1)
    post1 = dot(act1, nout[...])
    postg0 = node_back(0, post0)
    turn0 = dot_nt(postg0, nout[...])
    postg1 = node_back(1, post1)
    turn1 = dot_nt(postg1, nout[...])
    preg0 = node_turn(0, turn0, slope0)
    preg1 = node_turn(1, turn1, slope1)
    node_end(0, preg0)
    node_end(1, preg1)
    nacc_ref[...] = jnp.broadcast_to(jnp.sum(nacc[...], axis=0, keepdims=True), nacc.shape)
    mine = g_ref[0]
    for out_ref, which in ((keep_ref, mine), (give_ref, 1 - mine)):
        cols = pl.ds(pl.multiple_of(which * half, half), half)
        pg = nprg[:, cols]
        for k, source in enumerate((nodes, gath)):
            grad = dot_tn(source[...], pg).reshape(domains // 2, 16, half)
            out_ref[k * (domains // 2) : (k + 1) * (domains // 2), 0:16, :] = grad.astype(BF)
        last = dot_tn(nact[...], npostg[:, cols]).reshape(domains, 8, half)
        out_ref[:, 16:24, :] = last.astype(BF)
    for copy in stores:
        copy.wait()


def backward_kernel(
    send_ref, recv_ref, egain_ref, hat, slope, inv, gg, nacc_ref,
    ecot_hbm, eout_hbm, ein_hbm,
    ret_ref, gains_ref, halo_ref,
    epostg_hbm, epg_hbm,
    ecot, eout, weight, epostg_ref, epg_ref, eacc,
    in_sem, ecot_sem, out_sem,
):
    n, w = gg.shape
    e = hat.shape[0]
    h = halo_ref.shape[0]
    domains = ret_ref.shape[0]
    eb = 512
    blocks = e // eb

    def rows(b):
        return slice(b * eb, (b + 1) * eb)

    stores = []

    def store(source, target, k, b):
        copy = pltpu.make_async_copy(
            source.at[rows(b), :], target.at[rows(b), :], out_sem.at[k, b]
        )
        copy.start()
        stores.append(copy)

    loads = [
        pltpu.make_async_copy(ecot_hbm.at[rows(b), :], ecot.at[rows(b), :], ecot_sem.at[b])
        for b in range(blocks)
    ]
    weights = [
        pltpu.make_async_copy(eout_hbm, eout, in_sem.at[0]),
        pltpu.make_async_copy(ein_hbm.at[pl.ds(w, w), :], weight, in_sem.at[1]),
    ]
    for load in (loads[0], weights[0], *loads[1:], weights[1]):
        load.start()
    egain = egain_ref[...]
    eacc[...] = jnp.zeros_like(eacc)

    def edge_gather(b):
        return dot(pick(spread(recv_ref[:, rows(b)]), n), gg[...])

    def edge_back(b, value):
        loads[b].wait()
        upstream = ecot[rows(b), :].astype(F32) + value
        normed = hat[rows(b), :]
        eacc[...] += fold(upstream * normed)
        postg = norm_back(upstream, egain, normed, inv[rows(b), 0:1]).astype(BF)
        epostg_ref[rows(b), :] = postg
        store(epostg_ref, epostg_hbm, 0, b)
        return postg

    def edge_end(b, value):
        epg_ref[rows(b), :] = (value * slope[rows(b), :]).astype(BF)
        store(epg_ref, epg_hbm, 1, b)

    def halo_part(first, last):
        ids = send_ref[:, first * eb : last * eb]
        return dot(pick_t(ids, n, h), epg_ref[first * eb : last * eb, :])

    pre, act, post = {}, {}, {}
    halo = 0.0
    for t in range(blocks + 3):
        if t < blocks:
            pre[t] = edge_gather(t)
        if t == 2:
            weights[0].wait()
        if 0 <= t - 1 < blocks:
            act[t - 1] = edge_back(t - 1, pre.pop(t - 1))
        if t == blocks + 1:
            halo = halo_part(0, blocks // 2)
        if 0 <= t - 2 < blocks:
            edge_end(t - 2, dot_nt(act.pop(t - 2), eout[...]))
    gains = gain_rows(jnp.sum(eacc[...], axis=0, keepdims=True), nacc_ref[0:1, :], domains, LANES)
    gains_ref[...] = jnp.broadcast_to(gains[:, None, :], (domains, 8, LANES)).astype(BF)
    halo = (halo + halo_part(blocks // 2, blocks)).astype(BF)
    halo_ref[...] = halo
    weights[1].wait()
    ret = dot_nt(halo, weight[...])
    per = h // domains
    for k in range(w // LANES):
        part = ret[:, k * LANES : (k + 1) * LANES].reshape(domains, per, LANES)
        ret_ref[:, k * per : (k + 1) * per, :] = part.astype(BF)
    for copy in stores:
        copy.wait()


def grad_edges_kernel(epg_ref, ecot_ref, ein_ref, out_ref):
    out_ref[...] = (ecot_ref[...].astype(F32) + dot_nt(epg_ref[...], ein_ref[...])).astype(BF)


def edge_weights_kernel(
    g_ref, send_ref, recv_ref,
    epg_hbm, edges_hbm, nodes_hbm, arrived_hbm, halo_hbm, act_hbm, epostg_hbm,
    keep_ref, give_ref, sums_hbm,
    epg, edges, nodes, arrived, halo, act, epostg, sums, share, in_sem, out_sem,
):
    n, w = nodes.shape
    half = w // 2
    domains = share.shape[0]
    nb = 512
    loads = [
        pltpu.make_async_copy(source, target, in_sem.at[k])
        for k, (source, target) in enumerate(
            (
                (epg_hbm, epg),
                (edges_hbm, edges),
                (nodes_hbm, nodes),
                (arrived_hbm, arrived),
                (halo_hbm, halo),
                (act_hbm, act),
                (epostg_hbm, epostg),
            )
        )
    ]
    for load in loads:
        load.start()
    loads[0].wait()

    def node_sums(b, carry):
        first = pl.multiple_of(b * nb, nb)
        later = pl.multiple_of(n + b * nb, nb)
        sums[pl.ds(first, nb), :] = dot(pick_t(send_ref[...], first, nb), epg[...]).astype(BF)
        sums[pl.ds(later, nb), :] = dot(pick_t(recv_ref[...], first, nb), epg[...]).astype(BF)
        return carry

    lax.fori_loop(0, n // nb, node_sums, 0)
    out = pltpu.make_async_copy(sums, sums_hbm, out_sem)
    out.start()
    for load in loads[1:]:
        load.wait()
    per = 3 * w // domains // 8

    def put(k, part):
        for j in range(w // 8):
            t = k * (w // 8) + j
            share[t // per, (t % per) * 8 : (t % per) * 8 + 8, :] = part[j * 8 : j * 8 + 8, :]

    put(0, dot_tn(edges[...], epg[...]))
    both = dot_tn(nodes[...], jnp.concatenate([sums[0:n, :], sums[n:, :]], axis=1))
    put(1, both[:, :w] + dot_tn(arrived[...], halo[...]))
    put(2, both[:, w:])
    share[:, 24:32, :] = dot_tn(act[...], epostg[...]).reshape(domains, 8, w)
    mine = g_ref[0]
    keep_ref[...] = share[:, :, pl.ds(pl.multiple_of(mine * half, half), half)].astype(BF)
    give_ref[...] = share[:, :, pl.ds(pl.multiple_of((1 - mine) * half, half), half)].astype(BF)
    out.wait()


def local_sums_kernel(send_ref, recv_ref, nprg_ref, ncot_ref, ws_ref, wr_ref, nin_ref, out_ref):
    out_ref[...] = (
        ncot_ref[...].astype(F32)
        + dot_nt(send_ref[...], ws_ref[...])
        + dot_nt(recv_ref[...], wr_ref[...])
        + dot_nt(nprg_ref[...], nin_ref[...])
    )


def grad_nodes_kernel(list_ref, first_ref, total_ref, out_ref, back):
    domains, rows, lanes = first_ref.shape
    quarters = total_ref.shape[1] // lanes
    slots = rows // quarters
    block = total_ref.shape[0]

    @pl.when(pl.program_id(0) == 0)
    def _():
        for k in range(quarters):
            part = first_ref[:, k * slots : (k + 1) * slots, :].astype(F32)
            back[:, k * lanes : (k + 1) * lanes] = part.reshape(domains * slots, lanes).astype(BF)

    sel = pick_t(list_ref[...], pl.program_id(0) * block, block)
    out_ref[...] = (total_ref[...] + dot(sel, back[...])).astype(BF)


def sum_kernel(all_ref, out_ref):
    out_ref[...] = jnp.sum(all_ref[...].astype(F32), axis=0).astype(BF)


def node_sum_kernel(all_ref, out_ref):
    for k in range(2):
        part = all_ref[:, 32 + 24 * k : 56 + 24 * k, :].astype(F32)
        out_ref[0:24, k * LANES : (k + 1) * LANES] = jnp.sum(part, axis=0).astype(BF)
    gains = jnp.sum(all_ref[:, 80:88, :].astype(F32), axis=0).astype(BF)
    out_ref[24:32, :] = jnp.concatenate([gains, gains], axis=1)


def edge_outputs_kernel(g_ref, mine_ref, got_ref, ein_ref, eout_ref):
    half = mine_ref.shape[1]
    low = g_ref[0] == 0
    mine = mine_ref[...].astype(F32)
    got = got_ref[...].astype(F32)
    for k, value in enumerate((jnp.where(low, mine, got), jnp.where(low, got, mine))):
        cols = slice(k * half, (k + 1) * half)
        ein_ref[:, cols] = value[0:24, :]
        eout_ref[:, cols] = value[24:32, :]


def node_outputs_kernel(g_ref, mine_ref, got_ref, nin_ref, nout_ref, gains_ref):
    half = mine_ref.shape[1]
    low = g_ref[0] == 0
    mine = mine_ref[...].astype(F32)
    got = got_ref[...].astype(F32)
    for k, value in enumerate((jnp.where(low, mine, got), jnp.where(low, got, mine))):
        cols = slice(k * half, (k + 1) * half)
        nin_ref[:, cols] = value[0:16, :]
        nout_ref[:, cols] = value[16:24, :]
    gains_ref[...] = mine[24:32, 0:LANES] + got[24:32, 0:LANES]


def in_pieces(make, out_hbm, buffer, sem):
    count = sem.shape[0]
    size = buffer.shape[0] // count
    copies = []
    for k in range(count):
        part = slice(k * size, (k + 1) * size)
        make(part)
        copies.append(pltpu.make_async_copy(buffer.at[part], out_hbm.at[part], sem.at[k]))
        copies[-1].start()
    for copy in copies:
        copy.wait()


def join_kernel(ret_ref, keep_ref, got_ref, gains_ref, out_hbm, buffer, sem):
    def make(part):
        buffer[part, 0:32, :] = ret_ref[part]
        both = (keep_ref[part].astype(F32) + got_ref[part].astype(F32)).astype(BF)
        buffer[part, 32:56, :] = both[:, :, :LANES]
        buffer[part, 56:80, :] = both[:, :, LANES:]
        buffer[part, 80:88, :] = gains_ref[part]

    in_pieces(make, out_hbm, buffer, sem)


def add_kernel(keep_ref, got_ref, out_hbm, buffer, sem):
    def make(part):
        buffer[part] = (keep_ref[part].astype(F32) + got_ref[part].astype(F32)).astype(BF)

    in_pieces(make, out_hbm, buffer, sem)


VM = pl.BlockSpec(memory_space=pltpu.VMEM)
SM = pl.BlockSpec(memory_space=pltpu.SMEM)
ANY = pl.BlockSpec(memory_space=pltpu.HBM)


def whole(shape):
    return pl.BlockSpec(shape, lambda i: (0,) * len(shape))


def along(shape, dim, first=0):
    return pl.BlockSpec(
        shape, lambda i: tuple(first + i if d == dim else 0 for d in range(len(shape)))
    )


def call(kernel, outs, in_specs, out_specs, scratch=(), name=None, mib=16, grid=(), alias=None):
    return pl.pallas_call(
        kernel,
        out_shape=[
            jax.ShapeDtypeStruct(*o[:2]) if o[2:] == (NEAR,) else pltpu.HBM(*o) for o in outs
        ],
        grid=grid,
        in_specs=in_specs,
        out_specs=out_specs,
        scratch_shapes=list(scratch),
        compiler_params=pltpu.CompilerParams(vmem_limit_bytes=mib * MIB),
        input_output_aliases=alias or {},
        name=name,
    )


def far(*values):
    return tuple(pltpu.with_memory_space_constraint(v, pltpu.HBM) for v in values)


def swapped(value):
    return lax.ppermute(value, "group", [(0, 1), (1, 0)])


def exchanged(value):
    return lax.all_to_all(value, "dom", split_axis=0, concat_axis=0, tiled=True)


def local(
    nodes,
    edges,
    node_cotangent,
    edge_cotangent,
    senders,
    receivers,
    send_rows,
    edge_in,
    edge_out,
    edge_gain,
    node_in,
    node_out,
    node_gain,
):
    x = nodes[0]
    ed = edges[0]
    ncot = node_cotangent[0]
    ecot = edge_cotangent[0]
    n, w = x.shape
    e = ed.shape[0]
    domains, slots = send_rows.shape[1:]
    h = domains * slots
    half = w // 2
    me = lax.axis_index("group").astype(jnp.int32).reshape(1)
    egain = edge_gain.reshape(1, w)
    ngain = node_gain.reshape(1, w)
    vm = pltpu.VMEM
    dma = pltpu.SemaphoreType.DMA

    (outgoing,) = call(
        outgoing_kernel, [((h, w), BF)], [VM, VM], [VM], [vm((w // LANES, h, LANES), F32)], name="outgoing"
    )(*far(send_rows[0].T, x))
    arrived = exchanged(outgoing.reshape(domains, slots, w)).reshape(h, w)
    eb = 512
    pre, node_pre = call(
        early_kernel,
        [((e, w), F32), ((n, w), F32)],
        [
            along((1, eb), 1),
            along((1, eb), 1),
            along((eb, w), 0),
            whole((n, w)),
            whole((3 * w, w)),
            whole((w, w)),
        ],
        [along((eb, w), 0), along((n * eb // e, w), 0)],
        [vm((w + 2 * n, w), BF)],
        name="early",
        mib=32,
        grid=(e // eb,),
    )(senders, receivers, *far(ed, x, edge_in, node_in))

    keep, give, hat, slope, inv, gg, nacc, act, nprg = call(
        forward_kernel,
        [
            ((domains, 24, half), BF, NEAR),
            ((domains, 24, half), BF, NEAR),
            ((e, w), F32, NEAR),
            ((e, w), F32, NEAR),
            ((e, LANES), F32, NEAR),
            ((n, w), BF, NEAR),
            ((8, w), F32, NEAR),
            ((e, w), BF),
            ((n, w), BF),
        ],
        [SM] + [VM] * 7 + [ANY] * 6,
        [VM] * 7 + [ANY] * 2,
        [
            vm((n, w), BF),
            vm((w, w), BF),
            vm((w, w), BF),
            vm((n, w), BF),
            vm((n, w), F32),
            vm((e, w), BF),
            vm((e, w), BF),
            vm((n, w), BF),
            vm((n, w), BF),
            vm((n, w), BF),
            vm((n, w), BF),
            vm((8, w), F32),
            dma((5,)),
            dma((e // eb,)),
            dma((2, e // eb)),
        ],
        name="forward",
        mib=31,
    )(
        me, senders, receivers, egain, ngain, arrived, edge_in, edge_out,
        *far(pre, x, node_in, node_out, ncot, node_pre),
    )
    ret, gain_parts, halo, epostg, epg = call(
        backward_kernel,
        [
            ((domains, 4 * slots, LANES), BF, NEAR),
            ((domains, 8, LANES), BF, NEAR),
            ((h, w), BF),
            ((e, w), BF),
            ((e, w), BF),
        ],
        [VM] * 8 + [ANY] * 3,
        [VM] * 3 + [ANY] * 2,
        [
            vm((e, w), BF),
            vm((w, w), BF),
            vm((w, w), BF),
            vm((e, w), BF),
            vm((e, w), BF),
            vm((8, w), F32),
            dma((2,)),
            dma((e // eb,)),
            dma((2, e // eb)),
        ],
        name="backward",
        mib=28,
    )(
        senders, receivers, egain, hat, slope, inv, gg, nacc,
        *far(ecot, edge_out, edge_in),
    )
    share = ((domains, 32, half), BF)
    got, ret = lax.optimization_barrier((swapped(give), ret))
    (joined,) = call(
        join_kernel,
        [((domains, 88, LANES), BF)],
        [VM] * 4,
        [ANY],
        [vm((domains, 88, LANES), BF), dma((4,))],
        name="join",
    )(ret, keep, got, gain_parts)
    joined, epg = lax.optimization_barrier((joined, epg))
    first = exchanged(joined)

    def all_grad_edges():
        (value,) = call(
            grad_edges_kernel,
            [((e, w), BF)],
            [along((e // 2, w), 0)] * 2 + [whole((w, w))],
            [along((e // 2, w), 0)],
            name="grad_edges",
            grid=(2,),
        )(*far(epg, ecot, edge_in))
        return value

    keep2, give2, sums = call(
        edge_weights_kernel,
        [share + (NEAR,), share + (NEAR,), ((2 * n, w), BF)],
        [SM] + [VM] * 2 + [ANY] * 7,
        [VM, VM, ANY],
        [
            vm((e, w), BF),
            vm((e, w), BF),
            vm((n, w), BF),
            vm((h, w), BF),
            vm((h, w), BF),
            vm((e, w), BF),
            vm((e, w), BF),
            vm((2 * n, w), BF),
            vm((domains, 32, w), F32),
            dma((7,)),
            dma,
        ],
        name="edge_weights",
        mib=44,
    )(me, senders, receivers, *far(epg, ed, x, arrived, halo, act, epostg))
    got2, grad_edges = lax.optimization_barrier((swapped(give2), all_grad_edges()))
    (joined2,) = call(
        add_kernel,
        [share],
        [VM] * 2,
        [ANY],
        [vm((domains, 32, half), BF), dma((4,))],
        name="add",
    )(keep2, got2)
    joined2, first, sums = lax.optimization_barrier((joined2, first, sums))
    second = exchanged(joined2)
    nb = 512
    (total,) = call(
        local_sums_kernel,
        [((n, w), F32, NEAR)],
        [
            along((nb, w), 0),
            along((nb, w), 0, n // nb),
            along((nb, w), 0),
            along((nb, w), 0),
            pl.BlockSpec((w, w), lambda i: (1, 0)),
            pl.BlockSpec((w, w), lambda i: (2, 0)),
            whole((w, w)),
        ],
        [along((nb, w), 0)],
        name="local_sums",
        grid=(n // nb,),
    )(*far(sums, sums, nprg, ncot, edge_in, edge_in, node_in))
    (grad_nodes,) = call(
        grad_nodes_kernel,
        [((n, w), BF)],
        [whole((1, h)), whole((domains, 4 * slots, LANES)), along((nb, w), 0)],
        [along((nb, w), 0)],
        [vm((h, w), BF)],
        name="grad_nodes",
        grid=(n // nb,),
    )(send_rows.reshape(1, h), first, total)
    (node_sum,) = call(
        node_sum_kernel, [((32, half), BF, NEAR)], [VM], [VM], name="node_sum"
    )(first)
    g_nin, g_nout, gains = call(
        node_outputs_kernel,
        [((16, w), F32), ((8, w), F32), ((8, LANES), F32)],
        [SM, VM, VM],
        [VM] * 3,
        name="node_outputs",
    )(me, node_sum, swapped(node_sum))
    (edge_sum,) = call(
        sum_kernel, [((32, half), BF, NEAR)], [VM], [VM], name="edge_sum"
    )(second)
    g_ein, g_eout = call(
        edge_outputs_kernel,
        [((24, w), F32), ((8, w), F32)],
        [SM, VM, VM],
        [VM] * 2,
        name="edge_outputs",
    )(me, edge_sum, swapped(edge_sum))
    return (
        grad_edges[None],
        grad_nodes[None],
        g_ein,
        g_eout,
        g_nin,
        g_nout,
        gains[0, 0:8],
        gains[0, 8:16],
    )


def solution(mesh):
    split = P("group", "dom", None)
    placed = (split,) * 4 + (P("group", "dom"),) * 2 + (split,) + (P(),) * 6
    return jax.shard_map(
        local,
        mesh=mesh,
        in_specs=placed,
        out_specs=(split,) * 2 + (P("dom", None),) * 4 + (P("dom"),) * 2,
        check_vma=False,
    )
```

```python
import functools

import jax
import jax.numpy as jnp
from jax import lax
from jax.experimental import pallas as pl
from jax.experimental.pallas import tpu as pltpu
from jax.sharding import PartitionSpec as P

BF = jnp.bfloat16
F32 = jnp.float32
LANES = 128
MIB = 1024 * 1024
NEAR = True


def dot(a, b):
    return jnp.dot(a, b, preferred_element_type=F32)


def dot_nt(a, b):
    return lax.dot_general(a, b, (((1,), (1,)), ((), ())), preferred_element_type=F32)


def dot_tn(a, b):
    return lax.dot_general(a, b, (((0,), (0,)), ((), ())), preferred_element_type=F32)


def spread(ids):
    return jnp.broadcast_to(ids, (LANES, ids.shape[1])).T


def pick(spread_ids, count):
    lane = lax.broadcasted_iota(jnp.int32, spread_ids.shape, 1)
    from_lane = (spread_ids - lane).astype(jnp.int16)
    one = jnp.ones(spread_ids.shape, BF)
    tiles = [
        jnp.where(from_lane == jnp.int16(LANES * k), one, jnp.zeros_like(one))
        for k in range(count // LANES)
    ]
    return jnp.concatenate(tiles, axis=1)


def pick_t(ids, first, count):
    row = lax.broadcasted_iota(jnp.int32, (count, ids.shape[1]), 0) + first
    return jnp.where(row == ids, 1.0, 0.0).astype(BF)


def swish_both(pre):
    gate = jax.nn.sigmoid(pre)
    return pre * gate, gate * (1.0 + pre * (1.0 - gate))


def normalize(hidden):
    centre = hidden - jnp.mean(hidden, axis=-1, keepdims=True)
    inverse = lax.rsqrt(jnp.mean(centre * centre, axis=-1, keepdims=True) + 1e-05)
    return centre * inverse, inverse


def norm_back(upstream, gain, normed, inverse):
    scaled = upstream * gain
    return inverse * (
        scaled
        - jnp.mean(scaled, axis=-1, keepdims=True)
        - normed * jnp.mean(scaled * normed, axis=-1, keepdims=True)
    )


def fold(value):
    return jnp.sum(value.reshape(value.shape[0] // 8, 8, value.shape[1]), axis=0)


def outgoing_kernel(list_ref, nodes_ref, out_ref, rows_ref):
    slots, domains = list_ref.shape
    ids = jnp.concatenate([spread(list_ref[s : s + 1, :]) for s in range(slots)], axis=0)
    rows = dot(pick(ids, nodes_ref.shape[0]), nodes_ref[...])
    for s in range(slots):
        for k in range(rows_ref.shape[0]):
            rows_ref[k, pl.ds(s, domains, stride=slots), :] = rows[
                s * domains : (s + 1) * domains, k * LANES : (k + 1) * LANES
            ]
    for k in range(rows_ref.shape[0]):
        out_ref[:, k * LANES : (k + 1) * LANES] = rows_ref[k].astype(BF)


def early_kernel(
    send_ref, recv_ref, edges_ref, nodes_ref, ein_ref, nin_ref, out_ref, node_ref, table
):
    n, w = nodes_ref.shape
    nb = node_ref.shape[0]

    @pl.when(pl.program_id(0) == 0)
    def _():
        table[0:w, :] = ein_ref[0:w, :]
        table[w : w + n, :] = dot(nodes_ref[...], ein_ref[w : 2 * w, :]).astype(BF)
        table[w + n : w + 2 * n, :] = dot(nodes_ref[...], ein_ref[2 * w : 3 * w, :]).astype(BF)

    left = jnp.concatenate(
        [edges_ref[...], pick(spread(send_ref[...]), n), pick(spread(recv_ref[...]), n)], axis=1
    )
    out_ref[...] = dot(left, table[...])
    first = pl.multiple_of(pl.program_id(0) * nb, nb)
    node_ref[...] = dot(nodes_ref[pl.ds(first, nb), :], nin_ref[...])


def gain_rows(edge_gain, node_gain, domains, width):
    per = edge_gain.shape[1] // domains
    shape = (domains, edge_gain.shape[1])
    own = lax.broadcasted_iota(jnp.int32, shape, 1) // per == lax.broadcasted_iota(
        jnp.int32, shape, 0
    )
    col = lax.broadcasted_iota(jnp.int32, (edge_gain.shape[1], width), 0) % per
    lane = lax.broadcasted_iota(jnp.int32, (edge_gain.shape[1], width), 1)
    total = 0.0
    for k, gain in enumerate((edge_gain, node_gain)):
        mine = jnp.where(own, jnp.broadcast_to(gain, shape), 0.0).astype(BF)
        place = jnp.where(lane == col + per * k, 1.0, 0.0).astype(BF)
        total = total + dot(mine, place)
    return total


def forward_kernel(
    g_ref, send_ref, recv_ref, egain_ref, ngain_ref, arrived_ref, ein_ref, eout,
    pre_hbm, nodes_hbm, nin_hbm, nout_hbm, ncot_hbm, npre_hbm,
    keep_ref, give_ref, hat, slope, inv, gg, nacc_ref,
    act_hbm, nprg_hbm, gath_hbm,
    nodes, nin, nout, ncot, npre,
    act_ref, upd, gath, nact, npostg, nprg, nacc,
    in_sem, pre_sem, out_sem,
):
    n, w = nodes.shape
    e = hat.shape[0]
    h = arrived_ref.shape[0]
    half = w // 2
    domains = keep_ref.shape[0]
    eb = 512
    blocks = e // eb
    loads = [
        pltpu.make_async_copy(source, target, in_sem.at[k])
        for k, (source, target) in enumerate(
            (
                (nodes_hbm, nodes),
                (npre_hbm, npre),
                (nin_hbm.at[pl.ds(w, w), :], nin),
                (nout_hbm, nout),
                (ncot_hbm, ncot),
            )
        )
    ]

    def rows(b):
        return slice(b * eb, (b + 1) * eb)

    pre_loads = [
        pltpu.make_async_copy(pre_hbm.at[rows(b), :], hat.at[rows(b), :], pre_sem.at[b])
        for b in range(blocks)
    ]
    stores = []

    def store(source, target, k, b):
        copy = pltpu.make_async_copy(
            source.at[rows(b), :], target.at[rows(b), :], out_sem.at[k, b]
        )
        copy.start()
        stores.append(copy)

    for load in pre_loads + loads:
        load.start()
    egain = egain_ref[...]
    ngain = ngain_ref[...]
    nacc[...] = jnp.zeros_like(nacc)
    gg[0:h, :] = dot(arrived_ref[...], ein_ref[w : 2 * w, :]).astype(BF)

    def far_part(b):
        return dot(pick(spread(send_ref[:, rows(b)]) - n, h), gg[0:h, :])

    def edge_act(b, far_pre):
        pre_loads[b].wait()
        act, slp = swish_both(hat[rows(b), :] + far_pre)
        act = act.astype(BF)
        act_ref[rows(b), :] = act
        store(act_ref, act_hbm, 0, b)
        slope[rows(b), :] = slp
        return act

    def edge_norm(b, post):
        normed, inverse = normalize(post)
        hat[rows(b), :] = normed
        inv[rows(b), :] = jnp.broadcast_to(inverse, (eb, LANES))
        upd[rows(b), :] = (normed * egain).astype(BF)

    pre, act, post = {}, {}, {}
    for t in range(blocks + 3):
        if t < blocks:
            pre[t] = far_part(t)
        if 0 <= t - 2 < blocks:
            post[t - 2] = dot(act.pop(t - 2), eout[...])
        if 0 <= t - 1 < blocks:
            act[t - 1] = edge_act(t - 1, pre.pop(t - 1))
        if 0 <= t - 3 < blocks:
            edge_norm(t - 3, post.pop(t - 3))
    for load in loads:
        load.wait()

    def node_gather(b):
        gathered = dot(pick_t(recv_ref[...], b * eb, eb), upd[...]).astype(BF)
        gath[rows(b), :] = gathered
        store(gath, gath_hbm, 2, b)
        return npre[rows(b), :] + dot(gathered, nin[...])

    def node_act(b, value):
        act, slp = swish_both(value)
        act = act.astype(BF)
        nact[rows(b), :] = act
        return act, slp

    def node_back(b, value):
        normed, inverse = normalize(value)
        upstream = ncot[rows(b), :].astype(F32)
        nacc[...] += fold(upstream * normed)
        postg = norm_back(upstream, ngain, normed, inverse).astype(BF)
        npostg[rows(b), :] = postg
        return postg

    def node_turn(b, value, slp):
        preg = (value * slp).astype(BF)
        nprg[rows(b), :] = preg
        store(nprg, nprg_hbm, 1, b)
        return preg

    def node_end(b, preg):
        gg[rows(b), :] = dot_nt(preg, nin[...]).astype(BF)

    pre0 = node_gather(0)
    pre1 = node_gather(1)
    act0, slope0 = node_act(0, pre0)
    post0 = dot(act0, nout[...])
    act1, slope1 = node_act(1, pre1)
    post1 = dot(act1, nout[...])
    postg0 = node_back(0, post0)
    turn0 = dot_nt(postg0, nout[...])
    postg1 = node_back(1, post1)
    turn1 = dot_nt(postg1, nout[...])
    preg0 = node_turn(0, turn0, slope0)
    preg1 = node_turn(1, turn1, slope1)
    node_end(0, preg0)
    node_end(1, preg1)
    nacc_ref[...] = jnp.broadcast_to(jnp.sum(nacc[...], axis=0, keepdims=True), nacc.shape)
    mine = g_ref[0]
    for out_ref, which in ((keep_ref, mine), (give_ref, 1 - mine)):
        cols = pl.ds(pl.multiple_of(which * half, half), half)
        out_ref[...] = dot_tn(nact[...], npostg[:, cols]).reshape(domains, 8, half).astype(BF)
    for copy in stores:
        copy.wait()


def backward_kernel(
    send_ref, recv_ref, egain_ref, hat, slope, inv, gg, nacc_ref,
    ecot_hbm, eout_hbm, ein_hbm,
    ret_ref, gains_ref, halo_ref,
    epostg_hbm, epg_hbm,
    ecot, eout, weight, epostg_ref, epg_ref, eacc,
    in_sem, ecot_sem, out_sem,
):
    n, w = gg.shape
    e = hat.shape[0]
    h = halo_ref.shape[0]
    domains = ret_ref.shape[0]
    eb = 512
    blocks = e // eb

    def rows(b):
        return slice(b * eb, (b + 1) * eb)

    stores = []

    def store(source, target, k, b):
        copy = pltpu.make_async_copy(
            source.at[rows(b), :], target.at[rows(b), :], out_sem.at[k, b]
        )
        copy.start()
        stores.append(copy)

    loads = [
        pltpu.make_async_copy(ecot_hbm.at[rows(b), :], ecot.at[rows(b), :], ecot_sem.at[b])
        for b in range(blocks)
    ]
    weights = [
        pltpu.make_async_copy(eout_hbm, eout, in_sem.at[0]),
        pltpu.make_async_copy(ein_hbm.at[pl.ds(w, w), :], weight, in_sem.at[1]),
    ]
    for load in (loads[0], weights[0], *loads[1:], weights[1]):
        load.start()
    egain = egain_ref[...]
    eacc[...] = jnp.zeros_like(eacc)

    def edge_gather(b):
        return dot(pick(spread(recv_ref[:, rows(b)]), n), gg[...])

    def edge_back(b, value):
        loads[b].wait()
        upstream = ecot[rows(b), :].astype(F32) + value
        normed = hat[rows(b), :]
        eacc[...] += fold(upstream * normed)
        postg = norm_back(upstream, egain, normed, inv[rows(b), 0:1]).astype(BF)
        epostg_ref[rows(b), :] = postg
        store(epostg_ref, epostg_hbm, 0, b)
        return postg

    def edge_end(b, value):
        epg_ref[rows(b), :] = (value * slope[rows(b), :]).astype(BF)
        store(epg_ref, epg_hbm, 1, b)

    def halo_part(first, last):
        ids = send_ref[:, first * eb : last * eb]
        return dot(pick_t(ids, n, h), epg_ref[first * eb : last * eb, :])

    pre, act, post = {}, {}, {}
    halo = 0.0
    for t in range(blocks + 3):
        if t < blocks:
            pre[t] = edge_gather(t)
        if t == 2:
            weights[0].wait()
        if 0 <= t - 1 < blocks:
            act[t - 1] = edge_back(t - 1, pre.pop(t - 1))
        if t == blocks + 1:
            halo = halo_part(0, blocks // 2)
        if 0 <= t - 2 < blocks:
            edge_end(t - 2, dot_nt(act.pop(t - 2), eout[...]))
    gains = gain_rows(jnp.sum(eacc[...], axis=0, keepdims=True), nacc_ref[0:1, :], domains, LANES)
    gains_ref[...] = jnp.broadcast_to(gains[:, None, :], (domains, 8, LANES)).astype(BF)
    halo = (halo + halo_part(blocks // 2, blocks)).astype(BF)
    halo_ref[...] = halo
    weights[1].wait()
    ret = dot_nt(halo, weight[...])
    per = h // domains
    for k in range(w // LANES):
        part = ret[:, k * LANES : (k + 1) * LANES].reshape(domains, per, LANES)
        ret_ref[:, k * per : (k + 1) * per, :] = part.astype(BF)
    for copy in stores:
        copy.wait()


def grad_edges_kernel(epg_ref, ecot_ref, ein_ref, out_ref):
    out_ref[...] = (ecot_ref[...].astype(F32) + dot_nt(epg_ref[...], ein_ref[...])).astype(BF)


def edge_weights_kernel(
    g_ref, send_ref, recv_ref,
    epg_hbm, edges_hbm, nodes_hbm, arrived_hbm, halo_hbm, act_hbm, epostg_hbm, gath_hbm, nprg_hbm,
    keep_ref, give_ref, sums_hbm,
    epg, edges, nodes, arrived, halo, act, epostg, gath, nprg, sums, share, in_sem, out_sem,
):
    n, w = nodes.shape
    half = w // 2
    domains = share.shape[0]
    nb = 512
    loads = [
        pltpu.make_async_copy(source, target, in_sem.at[k])
        for k, (source, target) in enumerate(
            (
                (epg_hbm, epg),
                (edges_hbm, edges),
                (nodes_hbm, nodes),
                (arrived_hbm, arrived),
                (halo_hbm, halo),
                (act_hbm, act),
                (epostg_hbm, epostg),
                (gath_hbm, gath),
                (nprg_hbm, nprg),
            )
        )
    ]
    for load in loads:
        load.start()
    loads[0].wait()

    def node_sums(b, carry):
        first = pl.multiple_of(b * nb, nb)
        later = pl.multiple_of(n + b * nb, nb)
        sums[pl.ds(first, nb), :] = dot(pick_t(send_ref[...], first, nb), epg[...]).astype(BF)
        sums[pl.ds(later, nb), :] = dot(pick_t(recv_ref[...], first, nb), epg[...]).astype(BF)
        return carry

    lax.fori_loop(0, n // nb, node_sums, 0)
    out = pltpu.make_async_copy(sums, sums_hbm, out_sem)
    out.start()
    for load in loads[1:]:
        load.wait()
    per = 3 * w // domains // 8

    def put(k, part):
        for j in range(w // 8):
            t = k * (w // 8) + j
            share[t // per, (t % per) * 8 : (t % per) * 8 + 8, :] = part[j * 8 : j * 8 + 8, :]

    put(0, dot_tn(edges[...], epg[...]))
    both = dot_tn(nodes[...], jnp.concatenate([sums[0:n, :], sums[n:, :]], axis=1))
    put(1, both[:, :w] + dot_tn(arrived[...], halo[...]))
    put(2, both[:, w:])
    share[:, 24:32, :] = dot_tn(act[...], epostg[...]).reshape(domains, 8, w)
    for k, source in enumerate((nodes, gath)):
        grad = dot_tn(source[...], nprg[...]).reshape(domains // 2, 16, w)
        share[k * (domains // 2) : (k + 1) * (domains // 2), 32:48, :] = grad
    mine = g_ref[0]
    keep_ref[...] = share[:, :, pl.ds(pl.multiple_of(mine * half, half), half)].astype(BF)
    give_ref[...] = share[:, :, pl.ds(pl.multiple_of((1 - mine) * half, half), half)].astype(BF)
    out.wait()


def local_sums_kernel(send_ref, recv_ref, nprg_ref, ncot_ref, ws_ref, wr_ref, nin_ref, out_ref):
    out_ref[...] = (
        ncot_ref[...].astype(F32)
        + dot_nt(send_ref[...], ws_ref[...])
        + dot_nt(recv_ref[...], wr_ref[...])
        + dot_nt(nprg_ref[...], nin_ref[...])
    )


def grad_nodes_kernel(list_ref, first_ref, total_ref, out_ref, back):
    domains, rows, lanes = first_ref.shape
    quarters = total_ref.shape[1] // lanes
    slots = rows // quarters
    block = total_ref.shape[0]

    @pl.when(pl.program_id(0) == 0)
    def _():
        for k in range(quarters):
            part = first_ref[:, k * slots : (k + 1) * slots, :].astype(F32)
            back[:, k * lanes : (k + 1) * lanes] = part.reshape(domains * slots, lanes).astype(BF)

    sel = pick_t(list_ref[...], pl.program_id(0) * block, block)
    out_ref[...] = (total_ref[...] + dot(sel, back[...])).astype(BF)


def sum_kernel(all_ref, out_ref):
    out_ref[...] = jnp.sum(all_ref[...].astype(F32), axis=0).astype(BF)


def node_sum_kernel(all_ref, out_ref):
    for k in range(2):
        part = all_ref[:, 32 + 8 * k : 40 + 8 * k, :].astype(F32)
        out_ref[0:8, k * LANES : (k + 1) * LANES] = jnp.sum(part, axis=0).astype(BF)
    gains = jnp.sum(all_ref[:, 48:56, :].astype(F32), axis=0).astype(BF)
    out_ref[8:16, :] = jnp.concatenate([gains, gains], axis=1)


def edge_outputs_kernel(g_ref, mine_ref, got_ref, ein_ref, eout_ref, nin_ref):
    half = mine_ref.shape[1]
    low = g_ref[0] == 0
    mine = mine_ref[...].astype(F32)
    got = got_ref[...].astype(F32)
    for k, value in enumerate((jnp.where(low, mine, got), jnp.where(low, got, mine))):
        cols = slice(k * half, (k + 1) * half)
        ein_ref[:, cols] = value[0:24, :]
        eout_ref[:, cols] = value[24:32, :]
        nin_ref[:, cols] = value[32:48, :]


def node_outputs_kernel(g_ref, mine_ref, got_ref, nout_ref, gains_ref):
    half = mine_ref.shape[1]
    low = g_ref[0] == 0
    mine = mine_ref[...].astype(F32)
    got = got_ref[...].astype(F32)
    for k, value in enumerate((jnp.where(low, mine, got), jnp.where(low, got, mine))):
        cols = slice(k * half, (k + 1) * half)
        nout_ref[:, cols] = value[0:8, :]
    gains_ref[...] = mine[8:16, 0:LANES] + got[8:16, 0:LANES]


def in_pieces(make, out_hbm, buffer, sem):
    count = sem.shape[0]
    size = buffer.shape[0] // count
    copies = []
    for k in range(count):
        part = slice(k * size, (k + 1) * size)
        make(part)
        copies.append(pltpu.make_async_copy(buffer.at[part], out_hbm.at[part], sem.at[k]))
        copies[-1].start()
    for copy in copies:
        copy.wait()


def join_kernel(ret_ref, keep_ref, got_ref, gains_ref, out_hbm, buffer, sem):
    def make(part):
        buffer[part, 0:32, :] = ret_ref[part]
        both = (keep_ref[part].astype(F32) + got_ref[part].astype(F32)).astype(BF)
        buffer[part, 32:40, :] = both[:, :, :LANES]
        buffer[part, 40:48, :] = both[:, :, LANES:]
        buffer[part, 48:56, :] = gains_ref[part]

    in_pieces(make, out_hbm, buffer, sem)


def add_kernel(keep_ref, got_ref, out_hbm, buffer, sem):
    def make(part):
        buffer[part] = (keep_ref[part].astype(F32) + got_ref[part].astype(F32)).astype(BF)

    in_pieces(make, out_hbm, buffer, sem)


VM = pl.BlockSpec(memory_space=pltpu.VMEM)
SM = pl.BlockSpec(memory_space=pltpu.SMEM)
ANY = pl.BlockSpec(memory_space=pltpu.HBM)


def whole(shape):
    return pl.BlockSpec(shape, lambda i: (0,) * len(shape))


def along(shape, dim, first=0):
    return pl.BlockSpec(
        shape, lambda i: tuple(first + i if d == dim else 0 for d in range(len(shape)))
    )


def call(kernel, outs, in_specs, out_specs, scratch=(), name=None, mib=16, grid=(), alias=None):
    return pl.pallas_call(
        kernel,
        out_shape=[
            jax.ShapeDtypeStruct(*o[:2]) if o[2:] == (NEAR,) else pltpu.HBM(*o) for o in outs
        ],
        grid=grid,
        in_specs=in_specs,
        out_specs=out_specs,
        scratch_shapes=list(scratch),
        compiler_params=pltpu.CompilerParams(vmem_limit_bytes=mib * MIB),
        input_output_aliases=alias or {},
        name=name,
    )


def far(*values):
    return tuple(pltpu.with_memory_space_constraint(v, pltpu.HBM) for v in values)


def swapped(value):
    return lax.ppermute(value, "group", [(0, 1), (1, 0)])


def exchanged(value):
    return lax.all_to_all(value, "dom", split_axis=0, concat_axis=0, tiled=True)


def local(
    nodes,
    edges,
    node_cotangent,
    edge_cotangent,
    senders,
    receivers,
    send_rows,
    edge_in,
    edge_out,
    edge_gain,
    node_in,
    node_out,
    node_gain,
):
    x = nodes[0]
    ed = edges[0]
    ncot = node_cotangent[0]
    ecot = edge_cotangent[0]
    n, w = x.shape
    e = ed.shape[0]
    domains, slots = send_rows.shape[1:]
    h = domains * slots
    half = w // 2
    me = lax.axis_index("group").astype(jnp.int32).reshape(1)
    egain = edge_gain.reshape(1, w)
    ngain = node_gain.reshape(1, w)
    vm = pltpu.VMEM
    dma = pltpu.SemaphoreType.DMA

    (outgoing,) = call(
        outgoing_kernel, [((h, w), BF)], [VM, VM], [VM], [vm((w // LANES, h, LANES), F32)], name="outgoing"
    )(*far(send_rows[0].T, x))
    arrived = exchanged(outgoing.reshape(domains, slots, w)).reshape(h, w)
    eb = 512
    pre, node_pre = call(
        early_kernel,
        [((e, w), F32), ((n, w), F32)],
        [
            along((1, eb), 1),
            along((1, eb), 1),
            along((eb, w), 0),
            whole((n, w)),
            whole((3 * w, w)),
            whole((w, w)),
        ],
        [along((eb, w), 0), along((n * eb // e, w), 0)],
        [vm((w + 2 * n, w), BF)],
        name="early",
        mib=32,
        grid=(e // eb,),
    )(senders, receivers, *far(ed, x, edge_in, node_in))

    keep, give, hat, slope, inv, gg, nacc, act, nprg, gath = call(
        forward_kernel,
        [
            ((domains, 8, half), BF, NEAR),
            ((domains, 8, half), BF, NEAR),
            ((e, w), F32, NEAR),
            ((e, w), F32, NEAR),
            ((e, LANES), F32, NEAR),
            ((n, w), BF, NEAR),
            ((8, w), F32, NEAR),
            ((e, w), BF),
            ((n, w), BF),
            ((n, w), BF),
        ],
        [SM] + [VM] * 7 + [ANY] * 6,
        [VM] * 7 + [ANY] * 3,
        [
            vm((n, w), BF),
            vm((w, w), BF),
            vm((w, w), BF),
            vm((n, w), BF),
            vm((n, w), F32),
            vm((e, w), BF),
            vm((e, w), BF),
            vm((n, w), BF),
            vm((n, w), BF),
            vm((n, w), BF),
            vm((n, w), BF),
            vm((8, w), F32),
            dma((5,)),
            dma((e // eb,)),
            dma((3, e // eb)),
        ],
        name="forward",
        mib=31,
    )(
        me, senders, receivers, egain, ngain, arrived, edge_in, edge_out,
        *far(pre, x, node_in, node_out, ncot, node_pre),
    )
    ret, gain_parts, halo, epostg, epg = call(
        backward_kernel,
        [
            ((domains, 4 * slots, LANES), BF, NEAR),
            ((domains, 8, LANES), BF, NEAR),
            ((h, w), BF),
            ((e, w), BF),
            ((e, w), BF),
        ],
        [VM] * 8 + [ANY] * 3,
        [VM] * 3 + [ANY] * 2,
        [
            vm((e, w), BF),
            vm((w, w), BF),
            vm((w, w), BF),
            vm((e, w), BF),
            vm((e, w), BF),
            vm((8, w), F32),
            dma((2,)),
            dma((e // eb,)),
            dma((2, e // eb)),
        ],
        name="backward",
        mib=28,
    )(
        senders, receivers, egain, hat, slope, inv, gg, nacc,
        *far(ecot, edge_out, edge_in),
    )
    share = ((domains, 48, half), BF)
    got, ret = lax.optimization_barrier((swapped(give), ret))
    (joined,) = call(
        join_kernel,
        [((domains, 56, LANES), BF)],
        [VM] * 4,
        [ANY],
        [vm((domains, 56, LANES), BF), dma((4,))],
        name="join",
    )(ret, keep, got, gain_parts)
    joined, epg = lax.optimization_barrier((joined, epg))
    first = exchanged(joined)

    def all_grad_edges():
        (value,) = call(
            grad_edges_kernel,
            [((e, w), BF)],
            [along((e // 2, w), 0)] * 2 + [whole((w, w))],
            [along((e // 2, w), 0)],
            name="grad_edges",
            grid=(2,),
        )(*far(epg, ecot, edge_in))
        return value

    keep2, give2, sums = call(
        edge_weights_kernel,
        [share + (NEAR,), share + (NEAR,), ((2 * n, w), BF)],
        [SM] + [VM] * 2 + [ANY] * 9,
        [VM, VM, ANY],
        [
            vm((e, w), BF),
            vm((e, w), BF),
            vm((n, w), BF),
            vm((h, w), BF),
            vm((h, w), BF),
            vm((e, w), BF),
            vm((e, w), BF),
            vm((n, w), BF),
            vm((n, w), BF),
            vm((2 * n, w), BF),
            vm((domains, 48, w), F32),
            dma((9,)),
            dma,
        ],
        name="edge_weights",
        mib=50,
    )(me, senders, receivers, *far(epg, ed, x, arrived, halo, act, epostg, gath, nprg))
    got2, grad_edges = lax.optimization_barrier((swapped(give2), all_grad_edges()))
    (joined2,) = call(
        add_kernel,
        [share],
        [VM] * 2,
        [ANY],
        [vm((domains, 48, half), BF), dma((4,))],
        name="add",
    )(keep2, got2)
    joined2, first, sums = lax.optimization_barrier((joined2, first, sums))
    second = exchanged(joined2)
    nb = 512
    (total,) = call(
        local_sums_kernel,
        [((n, w), F32, NEAR)],
        [
            along((nb, w), 0),
            along((nb, w), 0, n // nb),
            along((nb, w), 0),
            along((nb, w), 0),
            pl.BlockSpec((w, w), lambda i: (1, 0)),
            pl.BlockSpec((w, w), lambda i: (2, 0)),
            whole((w, w)),
        ],
        [along((nb, w), 0)],
        name="local_sums",
        grid=(n // nb,),
    )(*far(sums, sums, nprg, ncot, edge_in, edge_in, node_in))
    (grad_nodes,) = call(
        grad_nodes_kernel,
        [((n, w), BF)],
        [whole((1, h)), whole((domains, 4 * slots, LANES)), along((nb, w), 0)],
        [along((nb, w), 0)],
        [vm((h, w), BF)],
        name="grad_nodes",
        grid=(n // nb,),
    )(send_rows.reshape(1, h), first, total)
    (node_sum,) = call(
        node_sum_kernel, [((16, half), BF, NEAR)], [VM], [VM], name="node_sum"
    )(first)
    g_nout, gains = call(
        node_outputs_kernel,
        [((8, w), F32), ((8, LANES), F32)],
        [SM, VM, VM],
        [VM] * 2,
        name="node_outputs",
    )(me, node_sum, swapped(node_sum))
    (edge_sum,) = call(
        sum_kernel, [((48, half), BF, NEAR)], [VM], [VM], name="edge_sum"
    )(second)
    g_ein, g_eout, g_nin = call(
        edge_outputs_kernel,
        [((24, w), F32), ((8, w), F32), ((16, w), F32)],
        [SM, VM, VM],
        [VM] * 3,
        name="edge_outputs",
    )(me, edge_sum, swapped(edge_sum))
    return (
        grad_edges[None],
        grad_nodes[None],
        g_ein,
        g_eout,
        g_nin,
        g_nout,
        gains[0, 0:8],
        gains[0, 8:16],
    )


def solution(mesh):
    split = P("group", "dom", None)
    placed = (split,) * 4 + (P("group", "dom"),) * 2 + (split,) + (P(),) * 6
    return jax.shard_map(
        local,
        mesh=mesh,
        in_specs=placed,
        out_specs=(split,) * 2 + (P("dom", None),) * 4 + (P("dom"),) * 2,
        check_vma=False,
    )
```
